32 devices in a mesh: group: 4 (over x, core), replica: 8 (over z, y).
Axes of the slice: x: 2, y: 2, z: 4, core: 2. Of those that a mesh axis runs over, the one named last changes fastest.
Arguments:
- hidden_in: bfloat16 [8, 1024, 896], P('replica', 'group'), may hold values from -6 to 6
- out_grad: bfloat16 [8, 1024, 896], P('replica', 'group'), may hold values from -6 to 6
- positions: int32 [8, 1024], P('replica', 'group'), may hold values from 0 to 3069, as said below
- block_ids: int32 [8, 1024], P('replica'), may hold values from 0 to 7, never falling along the last dimension, each value on 1 to 256 neighbouring positions
- gain_one: bfloat16 [896], P('group'), may hold values from 0.5 to 1.5
- w_query: bfloat16 [896, 896], P('group'), may hold values from -0.1875 to 0.1875
- b_query: bfloat16 [896], P('group'), may hold values from -3 to 3
- w_key: bfloat16 [896, 128], P('group'), may hold values from -0.1875 to 0.1875
- b_key: bfloat16 [128], P('group'), may hold values from -3 to 3
- w_value: bfloat16 [896, 128], P('group'), may hold values from -0.1875 to 0.1875
- b_value: bfloat16 [128], P('group'), may hold values from -3 to 3
- w_out: bfloat16 [896, 896], P('group'), may hold values from -1.5 to 1.5
- gain_two: bfloat16 [896], P('group'), may hold values from 0.5 to 1.5
- w_gate: bfloat16 [896, 4864], P('group'), may hold values from -0.1875 to 0.1875
- w_up: bfloat16 [896, 4864], P('group'), may hold values from -0.1875 to 0.1875
- w_down: bfloat16 [4864, 896], P('group'), may hold values from -0.078125 to 0.078125
Outputs:
- layer_out: bfloat16 [8, 1024, 896], P('replica', 'group')
- in_grad: bfloat16 [8, 1024, 896], P('replica', 'group')
- grad_gain_one: float32 [896], P('group')
- grad_w_query: float32 [896, 896], P('group')
- grad_b_query: float32 [896], P('group')
- grad_w_key: float32 [896, 128], P('group')
- grad_b_key: float32 [128], P('group')
- grad_w_value: float32 [896, 128], P('group')
- grad_b_value: float32 [128], P('group')
- grad_w_out: float32 [896, 896], P('group')
- grad_gain_two: float32 [896], P('group')
- grad_w_gate: float32 [896, 4864], P('group')
- grad_w_up: float32 [896, 4864], P('group')
- grad_w_down: float32 [4864, 896], P('group')
The draws below stay inside these ranges and needn't reach their ends.
Inputs may be any that keep to these rules, and one draw needn't show every extreme that they name: `block_ids`: along each sequence block ids never fall, and one block holds at most 256 tokens. Each sequence starts at position 0, and positions rise by 1, 2 or 3 from token to token.
All inputs are finite; a program needn't handle non-finite values.
Results may differ from the reference program's by a relative error of at most 0.018.
Values may be sent and summed in bfloat16 or wider, within the bound.
No kernel may reach another device: no remote copies, remote signals or barrier semaphores. Data moves between devices by JAX's collectives and lax.ppermute only.
A program may use at most 256 MiB of HBM per device.

```python
import math
import jax
import jax.numpy as jnp
import numpy as np
from jax import lax

D = 896
HEADS = 14
KV_HEADS = 2
HEAD_DIM = 64
FF = 4864
LEN = 1024
BLOCK = 256
QD = 896
KVD = 128
SEQUENCES = 8


def draw_positions(key, part):
    steps = jax.random.randint(key, (SEQUENCES, LEN), 1, 4, dtype=jnp.int32)
    rows = jnp.arange(SEQUENCES, dtype=jnp.int32)[:, None]
    steps = jnp.where(rows == 0, jnp.int32(1), steps)
    steps = jnp.where(rows == SEQUENCES - 1, jnp.int32(3), steps)
    columns = jnp.arange(LEN, dtype=jnp.int32)[None, :]
    steps = jnp.where(columns == 0, jnp.int32(0), steps)
    return jnp.cumsum(steps, axis=1).astype(jnp.int32)


def steps_of(stream_key, extent, cuts, smallest, largest):
    loudness = 1.0
    for dim, blocks in cuts:
        draws = jax.random.uniform(jax.random.fold_in(jax.random.fold_in(stream_key, 6), dim), (blocks,), jnp.float32, smallest / len(cuts), largest / len(cuts))
        loudness = loudness * jnp.repeat(jnp.exp(draws), extent[dim] // blocks).reshape((-1,) + (1,) * (len(extent) - 1 - dim))
    return loudness


def profile(amount, total, most, slope):
    loads = [(1 << 20) // math.isqrt(rank ** slope) + 1 for rank in range(2, amount + 1)]
    surplus, counts = total - most - (amount - 1), [1] * (amount - 1)
    while surplus > 0:
        candidates = [i for i in range(amount - 1) if counts[i] < most]
        pool, budget = sum([loads[i] for i in candidates]), surplus
        for i in candidates:
            more = min(most - counts[i], max(1, budget * loads[i] // pool), surplus)
            counts[i] = counts[i] + more
            surplus = surplus - more
    return np.array([most] + counts)


def ragged(key, count, total, limit, skew):
    if count == 2:
        one = jax.random.randint(key, (), max(1, total - limit), min(limit, total - 1) + 1)
        return jnp.stack([one, total - one])
    tallies = jnp.asarray(profile(count, total, limit, skew), jnp.int32)
    pairs = (count - 1) // 2
    source_of, sink = tallies[1:1 + 2 * pairs:2], tallies[2:2 + 2 * pairs:2]
    slack = jnp.minimum(source_of - 1, limit - sink)
    passed = jax.random.randint(jax.random.fold_in(key, 1), (pairs,), 0, 1 << 20) % (slack + 1)
    tallies = tallies.at[1:1 + 2 * pairs:2].set(source_of - passed).at[2:2 + 2 * pairs:2].set(sink + passed)
    return tallies[jax.random.permutation(jax.random.fold_in(key, 2), count)]


def bell_draw(stream_key, extent, deviation, most, cuts=(), held_as=jnp.bfloat16):
    gain = steps_of(stream_key, extent, cuts, -0.22, 0.18) if cuts else 1.0
    values = jax.random.normal(stream_key, extent, jnp.float32) * deviation * gain
    return jnp.minimum(jnp.maximum(values, -most), most).astype(held_as)


def setup_inputs(seed: int = 0) -> dict:
    splits = jax.random.split(jax.random.key(seed), 17)
    hidden_in = bell_draw(splits[0], (SEQUENCES, LEN, D), 1.0, 6.0, ((0, 8), (1, 4)))
    out_grad = bell_draw(splits[1], (SEQUENCES, LEN, D), 1.0, 6.0, ((0, 8), (1, 4)))
    positions = draw_positions(jax.random.fold_in(splits[16], 71), 0)
    block_ids = jax.vmap(lambda own: jnp.searchsorted(jnp.cumsum(ragged(own, 2 * LEN // BLOCK, LEN, BLOCK, 1)), jnp.arange(LEN), side="right"))(jax.random.split(splits[3], SEQUENCES)).reshape((SEQUENCES, LEN)).astype(jnp.int32)
    gain_one = jnp.clip(1.0 + 0.1 * jax.random.normal(splits[4], (D,), jnp.float32), 0.5, 1.5).astype(jnp.bfloat16)
    w_query = bell_draw(splits[5], (D, QD), D ** -0.5, 0.1875, ((0, 4),))
    b_query = bell_draw(splits[6], (QD,), 0.5, 3.0, ((0, 4),))
    w_key = bell_draw(splits[7], (D, KVD), D ** -0.5, 0.1875, ((0, 4),))
    b_key = bell_draw(splits[8], (KVD,), 0.5, 3.0, ((0, 4),))
    w_value = bell_draw(splits[9], (D, KVD), D ** -0.5, 0.1875, ((0, 4),))
    b_value = bell_draw(splits[10], (KVD,), 0.5, 3.0, ((0, 4),))
    w_out = bell_draw(splits[11], (QD, D), (QD // 64) ** -0.5, 1.5, ((0, 4),))
    gain_two = jnp.clip(1.0 + 0.1 * jax.random.normal(splits[12], (D,), jnp.float32), 0.5, 1.5).astype(jnp.bfloat16)
    w_gate = bell_draw(splits[13], (D, FF), D ** -0.5, 0.1875, ((0, 4),))
    w_up = bell_draw(splits[14], (D, FF), D ** -0.5, 0.1875, ((0, 4),))
    w_down = bell_draw(splits[15], (FF, D), FF ** -0.5, 0.078125, ((0, 4),))
    return dict(hidden_in=hidden_in, out_grad=out_grad, positions=positions, block_ids=block_ids, gain_one=gain_one, w_query=w_query, b_query=b_query, w_key=w_key, b_key=b_key, w_value=w_value, b_value=b_value, w_out=w_out, gain_two=gain_two, w_gate=w_gate, w_up=w_up, w_down=w_down)


EPSILON = 1e-06
THETA = 1000000.0

@jax.custom_vjp
def low(v):
    return lax.optimization_barrier(v.astype(jnp.bfloat16)).astype(jnp.float32)

@jax.custom_vjp
def low_back(v):
    return v

def low_keep(v):
    return (low(v), None)

def low_pass(kept, grad):
    return (grad,)

def back_keep(v):
    return (v, None)

def back_low(kept, grad):
    return (low(grad),)
low.defvjp(low_keep, low_pass)
low_back.defvjp(back_keep, back_low)

def rms_scale(values):
    return lax.rsqrt(lax.optimization_barrier(jnp.mean(values * values, axis=-1, keepdims=True)) + EPSILON)

def rotate(values, cosine, sine):
    half = values.shape[-1] // 2
    turned = jnp.concatenate([-values[..., half:], values[..., :half]], axis=-1)
    return values * cosine + turned * sine

def tables(positions):
    half = HEAD_DIM // 2
    freqs = THETA ** (-(2.0 * jnp.arange(half, dtype=jnp.float32)) / HEAD_DIM)
    angles = positions.astype(jnp.float32)[..., None] * freqs
    angles = jnp.concatenate([angles, angles], axis=-1)[:, :, None, :]
    return (jnp.cos(angles), jnp.sin(angles))

def layer(x, gain_one, w_query, b_query, w_key, b_key, w_value, b_value, w_out, gain_two, w_gate, w_up, w_down, cosine, sine, visible):
    highest = lax.Precision.HIGHEST
    batch, length, width = x.shape
    groups = HEADS // KV_HEADS
    normed_one = low(x * rms_scale(x) * gain_one)
    query_pre = low_back(jnp.dot(normed_one, w_query, precision=highest) + b_query)
    key_pre = low_back(jnp.dot(normed_one, w_key, precision=highest) + b_key)
    value = low(low_back(jnp.dot(normed_one, w_value, precision=highest) + b_value))
    query = low(rotate(query_pre.reshape(batch, length, HEADS, HEAD_DIM), cosine, sine))
    key = low(rotate(key_pre.reshape(batch, length, KV_HEADS, HEAD_DIM), cosine, sine))
    query = query.reshape(batch, length, KV_HEADS, groups, HEAD_DIM)
    value = value.reshape(batch, length, KV_HEADS, HEAD_DIM)
    scores = low_back(jnp.einsum('bqgha,bkga->bghqk', query, key, precision=highest) * (1.0 / HEAD_DIM ** 0.5))
    masked = jnp.where(visible[:, None, None, :, :], scores, -jnp.inf)
    probs = low(jax.nn.softmax(masked, axis=-1))
    attended = jnp.einsum('bghqk,bkga->bqgha', probs, value, precision=highest)
    attended = low(low_back(attended.reshape(batch, length, HEADS * HEAD_DIM)))
    residual = x + low_back(jnp.dot(attended, w_out, precision=highest))
    normed_two = low(residual * rms_scale(residual) * gain_two)
    gate = low_back(jnp.dot(normed_two, w_gate, precision=highest))
    up = low_back(jnp.dot(normed_two, w_up, precision=highest))
    hidden = low(jax.nn.silu(gate) * up)
    return residual + low_back(jnp.dot(hidden, w_down, precision=highest))

def reference(hidden_in, out_grad, positions, block_ids, gain_one, w_query, b_query, w_key, b_key, w_value, b_value, w_out, gain_two, w_gate, w_up, w_down):
    weights = tuple((w.astype(jnp.float32) for w in (gain_one, w_query, b_query, w_key, b_key, w_value, b_value, w_out, gain_two, w_gate, w_up, w_down)))
    count = hidden_in.shape[0] // 2
    inputs = hidden_in.reshape(count, 2, LEN, D)
    cotangents = out_grad.reshape(count, 2, LEN, D)
    places = positions.reshape(count, 2, LEN)
    blocks = block_ids.reshape(count, 2, LEN)

    def one_batch(totals, items):
        x_part, dy_part, pos_part, blk_part = items
        cosine, sine = tables(pos_part)
        visible = blk_part[:, None, :] <= blk_part[:, :, None]

        def forward(x_value, *params):
            return layer(x_value, *params, cosine, sine, visible)
        result, pullback = jax.vjp(forward, x_part.astype(jnp.float32), *weights)
        grads = pullback(dy_part.astype(jnp.float32))
        totals = tuple((t + g for t, g in zip(totals, grads[1:])))
        return (totals, (result.astype(jnp.bfloat16), grads[0].astype(jnp.bfloat16)))
    start = tuple((jnp.zeros(w.shape, jnp.float32) for w in weights))
    totals, (outs, dins) = lax.scan(one_batch, start, (inputs, cotangents, places, blocks))
    layer_out = outs.reshape(hidden_in.shape)
    in_grad = dins.reshape(hidden_in.shape)
    return (layer_out, in_grad, totals[0], totals[1], totals[2], totals[3], totals[4], totals[5], totals[6], totals[7], totals[8], totals[9], totals[10], totals[11])
```

```python
import jax
import jax.numpy as jnp
from jax import lax
from jax.sharding import PartitionSpec as P

HEADS = 14
KV_HEADS = 2
HEAD_DIM = 64

EPSILON = 1e-06
THETA = 1000000.0

F32 = jnp.float32
BF16 = jnp.bfloat16


def rms_scale(values):
    return lax.rsqrt(jnp.mean(values * values, axis=-1, keepdims=True) + EPSILON)


def rotate(values, cosine, sine):
    half = values.shape[-1] // 2
    turned = jnp.concatenate([-values[..., half:], values[..., :half]], axis=-1)
    return values * cosine + turned * sine


def norm_back(grad_normed, unit, scale, gain):
    grad_gain = jnp.sum(grad_normed * unit, axis=0)
    inner = grad_normed * gain
    grad_in = scale * (inner - unit * jnp.mean(inner * unit, axis=-1, keepdims=True))
    return (grad_gain, grad_in)


def mm(left, right):
    return jnp.dot(left, right, preferred_element_type=F32)


def mm_nt(left, right):
    return lax.dot_general(left, right, (((1,), (1,)), ((), ())), preferred_element_type=F32)


def mm_tn(left, right):
    return lax.dot_general(left, right, (((0,), (0,)), ((), ())), preferred_element_type=F32)


def pick(stack, index):
    return lax.dynamic_index_in_dim(stack, index, 0, keepdims=False)


class Ring:
    def __init__(self, count):
        self.count = count
        self.order = [0, 2, 4, 6, 7, 5, 3, 1] if count == 8 else list(range(count))
        self.plus = count // 2
        self.minus = count - 1 - self.plus

    def place(self):
        places = [self.order.index(i) for i in range(self.count)]
        return jnp.asarray(places, jnp.int32)[lax.axis_index("replica")]

    def move(self, value, step):
        n = self.count
        pairs = [(self.order[p], self.order[(p + step) % n]) for p in range(n)]
        return lax.ppermute(value, "replica", pairs)

    def scatter_sum(self, parts, place):
        n = self.count
        total = pick(parts, place).astype(F32)
        for hops, step in ((self.plus, 1), (self.minus, -1)):
            moving = None
            for left in range(hops, 0, -1):
                part = pick(parts, (place + step * left) % n)
                if moving is not None:
                    part = (part.astype(F32) + moving.astype(F32)).astype(BF16)
                moving = self.move(part, step)
            total = total + moving.astype(F32)
        return total.astype(BF16)

    def gather(self, own, place):
        n = self.count
        found = [(place, own)]
        ahead = back = own
        for hop in range(1, self.plus + 1):
            ahead = self.move(ahead, 1)
            found.append(((place - hop) % n, ahead))
            if hop <= self.minus:
                back = self.move(back, -1)
                found.append(((place + hop) % n, back))
        return found

    def assemble(self, found, dtype):
        block = found[0][1]
        out = jnp.zeros((self.count,) + block.shape, dtype)
        for index, value in found:
            start = (index,) + (0,) * block.ndim
            out = lax.dynamic_update_slice(out, value.astype(dtype)[None], start)
        return out


def swap(value, mask):
    return lax.ppermute(value, "group", [(j, j ^ mask) for j in range(4)])


def spread(own):
    one = swap(own, 1)
    two = swap(own, 2)
    return [own, one, two, swap(two, 1)]


def collect(blocks):
    blocks = [b.astype(BF16) for b in blocks]
    got = swap(jnp.stack([blocks[1], blocks[3]]), 1).astype(F32)
    mine = blocks[0].astype(F32) + got[0]
    other = (blocks[2].astype(F32) + got[1]).astype(BF16)
    return mine + swap(other, 2).astype(F32)


def in_order(blocks, me):
    stack = jnp.stack(blocks)
    return [pick(stack, me ^ j) for j in range(4)]


def make_body(replicas):
    ring = Ring(replicas)

    def body(
        hidden_in,
        out_grad,
        positions,
        block_ids,
        gain_one,
        w_query,
        b_query,
        w_key,
        b_key,
        w_value,
        b_value,
        w_out,
        gain_two,
        w_gate,
        w_up,
        w_down,
    ):
        _, part, width = hidden_in.shape
        length = block_ids.shape[1]
        rows = w_gate.shape[0]
        ff = w_down.shape[0]
        kvd = KV_HEADS * HEAD_DIM
        groups = HEADS // KV_HEADS
        factor = 1.0 / HEAD_DIM**0.5
        me = lax.axis_index("group")
        place = ring.place()

        qkv_own = jnp.concatenate([w_query, w_key, w_value], axis=1)
        vec_own = jnp.concatenate([gain_one, b_query, b_key, b_value, gain_two])
        qkv = spread(qkv_own)
        vec = jnp.stack(in_order(spread(vec_own), me)).astype(F32)
        g_one = vec[:, :rows].reshape(-1)
        bq = vec[:, rows : 2 * rows].reshape(-1)
        kvp = kvd // 4
        bk = vec[:, 2 * rows : 2 * rows + kvp].reshape(-1)
        bv = vec[:, 2 * rows + kvp : 2 * rows + 2 * kvp].reshape(-1)
        g_two = vec[:, 2 * rows + 2 * kvp :].reshape(-1)
        w_qkv = jnp.concatenate(in_order(qkv, me), axis=0)
        wo = jnp.concatenate(in_order(spread(w_out), me), axis=0)
        chunk = rows // replicas
        both = jnp.stack([w_gate, w_up]).reshape(2, rows, 4, ff).transpose(2, 0, 1, 3)
        near = swap(pick(both, me ^ 1), 1)
        far = []
        for mask in (2, 3):
            mine = pick(both, me ^ mask)
            mine = lax.dynamic_slice_in_dim(mine, place * chunk, chunk, 1)
            far.append(swap(mine, mask))
        far = jnp.stack(far)
        far = ring.assemble(ring.gather(far, place), BF16)
        far = far.transpose(1, 2, 0, 3, 4).reshape(2, 2, rows, ff)
        w_both = jnp.stack(in_order([pick(both, me), near, far[0], far[1]], me), axis=1)
        w_both = w_both.reshape(2, width, ff)
        wg, wu = w_both[0], w_both[1]

        half = HEAD_DIM // 2
        freqs = THETA ** (-(2.0 * jnp.arange(half, dtype=F32)) / HEAD_DIM)
        angles = positions[0].astype(F32)[:, None] * freqs
        angles = jnp.concatenate([angles, angles], axis=-1)[:, None, :]
        cosine = jnp.cos(angles)
        sine = jnp.sin(angles)
        x_value = hidden_in[0].astype(F32)
        scale_one = rms_scale(x_value)
        unit_one = x_value * scale_one
        normed_one = (unit_one * g_one).astype(BF16)
        pre = mm(normed_one, w_qkv)
        query_pre = pre[:, :width] + bq
        key_pre = pre[:, width : width + kvd] + bk
        value_low = (pre[:, width + kvd :] + bv).astype(BF16)
        query = rotate(query_pre.reshape(part, HEADS, HEAD_DIM), cosine, sine).astype(BF16)
        key_low = rotate(key_pre.reshape(part, KV_HEADS, HEAD_DIM), cosine, sine).astype(BF16)
        kv = spread(jnp.concatenate([key_low.reshape(part, kvd), value_low], axis=1))
        kv = jnp.concatenate(kv, axis=0)
        key_heads = kv[:, :kvd].reshape(length, KV_HEADS, HEAD_DIM)
        value_heads = kv[:, kvd:].reshape(length, KV_HEADS, HEAD_DIM)
        ids = block_ids.reshape(4, part)
        own_ids = pick(ids, me)
        key_ids = jnp.stack([pick(ids, me ^ k) for k in range(4)]).reshape(-1)
        visible = (key_ids[None, :] <= own_ids[:, None])[None, None]
        query_heads = query.reshape(part, KV_HEADS, groups, HEAD_DIM)
        scores = (
            jnp.einsum("qgha,kga->ghqk", query_heads, key_heads, preferred_element_type=F32)
            * factor
        )
        masked = jnp.where(visible, scores, -jnp.inf)
        top = jnp.max(masked, axis=-1, keepdims=True)
        raised = jnp.exp(masked - top)
        total = jnp.sum(raised, axis=-1, keepdims=True)
        log_total = top + jnp.log(total)
        probs_low = (raised / total).astype(BF16)
        attended = jnp.einsum(
            "ghqk,kga->qgha", probs_low, value_heads, preferred_element_type=F32
        )
        attended = attended.reshape(part, HEADS * HEAD_DIM).astype(BF16)
        residual = x_value + mm(attended, wo)
        scale_two = rms_scale(residual)
        unit_two = residual * scale_two
        normed_two = (unit_two * g_two).astype(BF16)

        tokens = jnp.concatenate(spread(normed_two), axis=0)
        dy = jnp.concatenate(spread(out_grad[0]), axis=0)
        grad_hidden = mm_nt(dy, w_down)
        gate = mm(tokens, wg)
        up_value = mm(tokens, wu)
        sigma = jax.nn.sigmoid(gate)
        activated = gate * sigma
        hidden = (activated * up_value).astype(BF16)
        grad_down = mm_tn(hidden, dy).astype(BF16)
        grad_gate_pre = (grad_hidden * up_value * sigma * (1.0 + gate * (1.0 - sigma))).astype(BF16)
        grad_up_pre = (grad_hidden * activated).astype(BF16)
        grad_gate = mm_tn(tokens, grad_gate_pre).astype(BF16)
        grad_up = mm_tn(tokens, grad_up_pre).astype(BF16)

        down = ring.scatter_sum(grad_down.reshape(replicas, ff // replicas, width), place)
        out_down = ring.assemble(ring.gather(down, place), F32).reshape(ff, width)

        def finish(grad):
            grad = grad.reshape(4, replicas, chunk, ff).transpose(1, 0, 2, 3)
            mine = ring.scatter_sum(grad, place)
            blocks = [pick(mine, me)] + [swap(pick(mine, me ^ k), k) for k in (1, 2, 3)]
            got = ring.assemble(ring.gather(jnp.stack(blocks), place), BF16)
            got = jnp.stack([lax.dynamic_index_in_dim(got, me ^ j, 1, keepdims=False) for j in range(4)], axis=2)
            return got.reshape(rows, 4 * ff).astype(F32)

        out_gate = finish(grad_gate)
        out_up = finish(grad_up)

        partial = mm(hidden, w_down).reshape(4, part, width)
        layer_out = (residual + collect([partial[k] for k in range(4)])).astype(BF16)
        partial = (mm_nt(grad_gate_pre, wg) + mm_nt(grad_up_pre, wu)).reshape(4, part, width)
        grad_normed_two = collect([partial[k] for k in range(4)])

        grad_gain_two, grad_res_norm = norm_back(grad_normed_two, unit_two, scale_two, g_two)
        grad_residual = out_grad[0].astype(F32) + grad_res_norm
        grad_branch = grad_residual.astype(BF16)
        grad_wo = mm_tn(attended, grad_branch)
        grad_attended = mm_nt(grad_branch, wo).astype(BF16)
        grad_att_heads = grad_attended.reshape(part, KV_HEADS, groups, HEAD_DIM)
        again = (
            jnp.einsum("qgha,kga->ghqk", query_heads, key_heads, preferred_element_type=F32)
            * factor
        )
        probs = jnp.where(visible, jnp.exp(again - log_total), 0.0)
        probs_back = probs.astype(BF16)
        grad_probs = jnp.einsum(
            "qgha,kga->ghqk", grad_att_heads, value_heads, preferred_element_type=F32
        )
        grad_values = jnp.einsum(
            "ghqk,qgha->kga", probs_back, grad_att_heads, preferred_element_type=F32
        )
        row_sum = jnp.sum(probs * grad_probs, axis=-1, keepdims=True)
        grad_scores = (probs * (grad_probs - row_sum)).astype(BF16)
        grad_query = (
            jnp.einsum("ghqk,kga->qgha", grad_scores, key_heads, preferred_element_type=F32)
            * factor
        )
        grad_keys = (
            jnp.einsum("ghqk,qgha->kga", grad_scores, query_heads, preferred_element_type=F32)
            * factor
        )
        grad_kv = jnp.concatenate(
            [grad_keys.reshape(4, part, kvd), grad_values.reshape(4, part, kvd)], axis=2
        )
        grad_kv = collect([grad_kv[k] for k in range(4)])
        grad_query_pre = rotate(grad_query.reshape(part, HEADS, HEAD_DIM), cosine, -sine)
        grad_query_pre = grad_query_pre.astype(BF16).reshape(part, width)
        grad_key_pre = rotate(grad_kv[:, :kvd].reshape(part, KV_HEADS, HEAD_DIM), cosine, -sine)
        grad_key_pre = grad_key_pre.astype(BF16).reshape(part, kvd)
        grad_value_pre = grad_kv[:, kvd:].astype(BF16)
        grad_pre = jnp.concatenate([grad_query_pre, grad_key_pre, grad_value_pre], axis=1)
        grad_bias = jnp.sum(grad_pre.astype(F32), axis=0)
        grad_w_qkv = mm_tn(normed_one, grad_pre)
        grad_normed_one = mm_nt(grad_pre, w_qkv)
        grad_gain_one, grad_in_norm = norm_back(grad_normed_one, unit_one, scale_one, g_one)
        in_grad = (grad_residual + grad_in_norm).astype(BF16)

        columns = 2 * width + 2 * kvd
        per = rows // replicas + 1
        vectors = jnp.concatenate(
            [
                grad_gain_one.reshape(4, rows),
                grad_bias[:width].reshape(4, rows),
                grad_bias[width : width + kvd].reshape(4, kvp),
                grad_bias[width + kvd :].reshape(4, kvp),
                grad_gain_two.reshape(4, rows),
            ],
            axis=1,
        )
        vectors = jnp.pad(vectors, ((0, 0), (0, columns - vectors.shape[1])))[:, None]
        packed = jnp.concatenate([grad_w_qkv, grad_wo], axis=1).reshape(4, rows, columns)
        empty = jnp.zeros((4, per * replicas - rows - 1, columns), F32)
        packed = jnp.concatenate([packed, vectors, empty], axis=1).astype(BF16)
        packed = collect([pick(packed, me ^ k) for k in range(4)]).astype(BF16)
        packed = ring.scatter_sum(packed.reshape(replicas, per, columns), place)
        packed = ring.assemble(ring.gather(packed, place), F32).reshape(replicas * per, columns)
        weights, vectors = packed[:rows], packed[rows]
        cut = width + kvd
        return (
            layer_out[None],
            in_grad[None],
            vectors[:rows],
            weights[:, :width],
            vectors[rows : 2 * rows],
            weights[:, width:cut],
            vectors[2 * rows : 2 * rows + kvp],
            weights[:, cut : cut + kvd],
            vectors[2 * rows + kvp : 2 * rows + 2 * kvp],
            weights[:, cut + kvd :],
            vectors[2 * rows + 2 * kvp : 3 * rows + 2 * kvp],
            out_gate,
            out_up,
            out_down,
        )

    return body


def solution(mesh):
    tokens = P("replica", "group", None)
    matrix = P("group", None)
    vector = P("group")
    weights = (
        vector,
        matrix,
        vector,
        matrix,
        vector,
        matrix,
        vector,
        matrix,
        vector,
        matrix,
        matrix,
        matrix,
    )
    in_specs = (tokens, tokens, P("replica", "group"), P("replica", None)) + weights
    out_specs = (tokens, tokens) + weights
    body = make_body(mesh.shape["replica"])
    return jax.shard_map(body, mesh=mesh, in_specs=in_specs, out_specs=out_specs, check_vma=False)
```

```python
import functools

import jax
import jax.numpy as jnp
from jax import lax
from jax.experimental import pallas as pl
from jax.experimental.pallas import tpu as pltpu
from jax.sharding import PartitionSpec as P

HEADS = 14
KV_HEADS = 2
HEAD_DIM = 64
GROUPS = HEADS // KV_HEADS
KVD = KV_HEADS * HEAD_DIM
FACTOR = 1.0 / HEAD_DIM**0.5
LANES = 128
HIDDEN_KEY = -1e30

EPSILON = 1e-06
THETA = 1000000.0

F32 = jnp.float32
BF16 = jnp.bfloat16

ANY = pl.BlockSpec(memory_space=pl.ANY)
VMEM = pl.BlockSpec(memory_space=pltpu.VMEM)
SMEM = pl.BlockSpec(memory_space=pltpu.SMEM)


def rms_scale(values):
    return lax.rsqrt(jnp.mean(values * values, axis=-1, keepdims=True) + EPSILON)


def mm(left, right):
    return jnp.dot(left, right, preferred_element_type=F32)


def mm_nt(left, right):
    return lax.dot_general(left, right, (((1,), (1,)), ((), ())), preferred_element_type=F32)


def mm_tn(left, right):
    return lax.dot_general(left, right, (((0,), (0,)), ((), ())), preferred_element_type=F32)


def norm_back(grad_normed, unit, scale, gain):
    grad_gain = jnp.sum(grad_normed * unit, axis=0)
    inner = grad_normed * gain
    grad_in = scale * (inner - unit * jnp.mean(inner * unit, axis=-1, keepdims=True))
    return (grad_gain, grad_in)


def pick(stack, index, axis=0):
    return lax.dynamic_index_in_dim(stack, index, axis, keepdims=False)


def cost(flops, moved, special=0):
    return pl.CostEstimate(flops=int(flops), bytes_accessed=int(moved), transcendentals=int(special))


def turn_back(values, sine):
    wide = values.shape[1]
    lane = lax.broadcasted_iota(jnp.int32, values.shape, 1) % HEAD_DIM
    ahead = pltpu.roll(values, wide - HEAD_DIM // 2, 1)
    behind = pltpu.roll(values, HEAD_DIM // 2, 1)
    return jnp.where(lane < HEAD_DIM // 2, ahead, behind) * sine


def split_kernel(where, gate, up, own, near, far, *, chunk, ff, step):
    me, place = where[0], where[1]
    half = gate.shape[0] // chunk
    for j in range(4):
        columns = pl.ds(j * ff, ff)
        for target, out in ((me, own), (me ^ 1, near)):

            @pl.when(target == j)
            def _(out=out, columns=columns):
                @pl.loop(0, gate.shape[0] // step)
                def _(i):
                    rows = pl.ds(pl.multiple_of(i * step, step), step)
                    out[0, rows, :] = gate[rows, columns]
                    out[1, rows, :] = up[rows, columns]

        for slot in (0, 1):

            @pl.when((me ^ (2 + slot)) == j)
            def _(slot=slot, columns=columns):
                rows = pl.ds(pl.multiple_of(lax.rem(place, half) * chunk, 8), chunk)

                @pl.when(place < half)
                def _():
                    far[slot] = gate[rows, columns]

                @pl.when(place >= half)
                def _():
                    far[slot] = up[rows, columns]


def split(gate, up, me, place, replicas):
    rows = gate.shape[0]
    ff = gate.shape[1] // 4
    chunk = 2 * rows // replicas
    if chunk % 8:
        both = jnp.stack([gate, up]).reshape(2, rows, 4, ff).transpose(2, 0, 1, 3)
        far = [pick(both, me ^ k).reshape(replicas, chunk, ff) for k in (2, 3)]
        far = jnp.stack([pick(f, place) for f in far])
        return pick(both, me), pick(both, me ^ 1), far
    shape = jax.ShapeDtypeStruct((2, rows, ff), BF16)
    return pl.pallas_call(
        functools.partial(split_kernel, chunk=chunk, ff=ff, step=32),
        out_shape=(shape, shape, jax.ShapeDtypeStruct((2, chunk, ff), BF16)),
        in_specs=[SMEM, VMEM, VMEM],
        out_specs=(VMEM, VMEM, VMEM),
        cost_estimate=cost(0, 16 * rows * ff),
        name="split",
    )(jnp.stack([me, place]), gate, up)


def arrange_kernel(where, *refs, moves):
    out, sems = refs[-2], refs[-1]
    copies = []
    for i, (source, take, put) in enumerate(moves):
        copy = pltpu.make_async_copy(refs[source].at[take(where)], out.at[put(where)], sems.at[i])
        copy.start()
        copies.append(copy)
    for copy in copies:
        copy.wait()


def arrange(where, sources, shape, moves):
    size = 1
    for extent in shape:
        size *= extent
    return pl.pallas_call(
        functools.partial(arrange_kernel, moves=moves),
        out_shape=jax.ShapeDtypeStruct(shape, BF16),
        in_specs=[SMEM] + [ANY] * len(sources),
        out_specs=VMEM,
        scratch_shapes=[pltpu.SemaphoreType.DMA((len(moves),))],
        cost_estimate=cost(0, 4 * size),
        name="arrange",
    )(where, *sources)


def join_kernel(where, *refs, count, ff):
    pieces, gate, up, slab, sems = refs[:count], *refs[count:]
    me = where[0]
    chunk = pieces[0].shape[1]
    half = count // 2

    def copy(i, out):
        row = pl.multiple_of(lax.rem(where[1 + i], half) * chunk, 8)
        return pltpu.make_async_copy(slab.at[i % 2], out.at[pl.ds(row, chunk), :], sems.at[i])

    for i in range(count):
        if i >= 2:
            copy(i - 2, gate).wait()
        for j in range(4):
            slab[i % 2, :, pl.ds(j * ff, ff)] = pieces[i][me ^ j].astype(F32)

        @pl.when(where[1 + i] < half)
        def _(i=i):
            copy(i, gate).start()

        @pl.when(where[1 + i] >= half)
        def _(i=i):
            copy(i, up).start()

    for i in range(count - 2, count):
        copy(i, gate).wait()


def join(found, me, rows):
    count = len(found)
    _, chunk, ff = found[0][1].shape
    if chunk % 8:
        got = jnp.zeros((count, 4, chunk, ff), F32)
        for index, value in found:
            got = lax.dynamic_update_slice(got, value.astype(F32)[None], (index, 0, 0, 0))
        got = jnp.stack([pick(got, me ^ j, 1) for j in range(4)], axis=2)
        got = got.reshape(2, rows, 4 * ff)
        return got[0], got[1]
    shape = jax.ShapeDtypeStruct((rows, 4 * ff), F32)
    where = jnp.stack([me] + [index for index, _ in found])
    return pl.pallas_call(
        functools.partial(join_kernel, count=count, ff=ff),
        out_shape=(shape, shape),
        in_specs=[SMEM] + [VMEM] * count,
        out_specs=(ANY, ANY),
        scratch_shapes=[pltpu.VMEM((2, chunk, 4 * ff), F32), pltpu.SemaphoreType.DMA((count,))],
        cost_estimate=cost(0, 48 * rows * ff),
        name="join",
    )(where, *[value for _, value in found])


def load_rows(where, blocks, out, sems, first):
    rows = blocks[0].shape[0]
    copies = []
    for k, block in enumerate(blocks):
        row = pl.multiple_of((where[0] ^ k) * rows, 8)
        copies.append(pltpu.make_async_copy(block, out.at[pl.ds(row, rows), :], sems.at[first + k]))
        copies[-1].start()
    return copies


def qkv_kernel(where, hidden, gain, bias, cosine, sine, *refs):
    wq, wk, wv = refs[0:4], refs[4:8], refs[8:12]
    query, kv, normed_out, weights, sems = refs[12:]
    width = hidden.shape[1]
    copies = load_rows(where, wq, weights.at[:, pl.ds(0, width)], sems, 0)
    copies += load_rows(where, wk, weights.at[:, pl.ds(width, KVD)], sems, 4)
    copies += load_rows(where, wv, weights.at[:, pl.ds(width + KVD, KVD)], sems, 8)
    x = hidden[...].astype(F32)
    normed = (x * rms_scale(x) * gain[...]).astype(BF16)
    normed_out[...] = normed
    for copy in copies:
        copy.wait()
    cos, sin = cosine[...], sine[...]
    for first in range(0, width + 2 * KVD, LANES):
        lanes = pl.ds(first, LANES)
        value = mm(normed, weights[:, lanes]) + bias[:, lanes]
        if first < width + KVD:
            value = value * cos + turn_back(value, sin)
        if first < width:
            query[:, lanes] = (value.astype(BF16).astype(F32) * FACTOR).astype(BF16)
        else:
            kv[:, pl.ds(first - width, LANES)] = value.astype(BF16)


def project_qkv(me, hidden, gain, bias, cosine, sine, wq, wk, wv):
    part, width = hidden.shape
    total = width + 2 * KVD
    return pl.pallas_call(
        qkv_kernel,
        out_shape=(
            jax.ShapeDtypeStruct((part, width), BF16),
            jax.ShapeDtypeStruct((part, 2 * KVD), BF16),
            jax.ShapeDtypeStruct((part, width), BF16),
            jax.ShapeDtypeStruct((width, total), BF16),
        ),
        in_specs=[SMEM] + [VMEM] * 5 + [ANY] * 12,
        out_specs=(VMEM,) * 4,
        scratch_shapes=[pltpu.SemaphoreType.DMA((12,))],
        cost_estimate=cost(2 * part * width * total, 4 * width * total),
        name="qkv",
    )(me, hidden, gain, bias, cosine, sine, *wq, *wk, *wv)


def attend_kernel(where, hidden, gain, own_ids, key_ids, query, kv0, kv1, kv2, kv3, w0, w1, w2, w3, *refs):
    attended, lse, residual, normed, weights, kv, mask, sems = refs
    part, width = hidden.shape
    copies = load_rows(where, (w0, w1, w2, w3), weights, sems, 0)
    for k, block in enumerate((kv0, kv1, kv2, kv3)):
        kv[pl.ds(k * part, part), :] = block[...]
    mask[...] = jnp.where(key_ids[...] <= own_ids[...], 0.0, HIDDEN_KEY)
    lane = lax.broadcasted_iota(jnp.int32, (part, LANES), 1)
    logs = jnp.zeros((part, LANES), F32)
    for h in range(HEADS):
        g = h // GROUPS
        keys = kv[:, pl.ds(g * HEAD_DIM, HEAD_DIM)]
        values = kv[:, pl.ds(KVD + g * HEAD_DIM, HEAD_DIM)]
        lanes = pl.ds(h * HEAD_DIM, HEAD_DIM)
        scores = mm_nt(query[:, lanes], keys) + mask[...]
        top = jnp.max(scores, axis=-1, keepdims=True)
        raised = jnp.exp(scores - top)
        total = jnp.sum(raised, axis=-1, keepdims=True)
        logs = jnp.where(lane == h, top + jnp.log(total), logs)
        probs = (raised * (1.0 / total)).astype(BF16)
        attended[:, lanes] = mm(probs, values).astype(BF16)
    lse[...] = logs
    for copy in copies:
        copy.wait()
    value = hidden[...].astype(F32) + mm(attended[...], weights[...])
    residual[...] = value
    normed[...] = (value * rms_scale(value) * gain[...]).astype(BF16)


def attend(me, hidden, gain, own_ids, key_ids, query, kv, wo):
    part, width = hidden.shape
    length = key_ids.shape[1]
    work = part * length * HEADS
    return pl.pallas_call(
        attend_kernel,
        out_shape=(
            jax.ShapeDtypeStruct((part, width), BF16),
            jax.ShapeDtypeStruct((part, LANES), F32),
            jax.ShapeDtypeStruct((part, width), F32),
            jax.ShapeDtypeStruct((part, width), BF16),
            jax.ShapeDtypeStruct((width, width), BF16),
        ),
        in_specs=[SMEM] + [VMEM] * 9 + [ANY] * 4,
        out_specs=(VMEM,) * 5,
        scratch_shapes=[
            pltpu.VMEM((length, 2 * KVD), BF16),
            pltpu.VMEM((part, length), F32),
            pltpu.SemaphoreType.DMA((4,)),
        ],
        cost_estimate=cost(4 * work * HEAD_DIM + 2 * part * width * width, 8 * part * width, work),
        name="attend",
    )(me, hidden, gain, own_ids, key_ids, query, *kv, *wo)


def rotate(values, cosine, sine):
    half = values.shape[-1] // 2
    turned = jnp.concatenate([-values[..., half:], values[..., :half]], axis=-1)
    return values * cosine + turned * sine


class Ring:
    def __init__(self, count, lead):
        self.count = count
        self.lead = lead
        self.order = [0, 2, 4, 6, 7, 5, 3, 1] if count == 8 else list(range(count))
        self.plus = count // 2
        self.minus = count - 1 - self.plus

    def place(self):
        places = [self.order.index(i) for i in range(self.count)]
        return jnp.asarray(places, jnp.int32)[lax.axis_index("replica")]

    def move(self, value, step):
        n = self.count
        pairs = [(self.order[p], self.order[(p + step) % n]) for p in range(n)]
        return lax.ppermute(value, "replica", pairs)

    def scatter_sum(self, part_of, place):
        n = self.count
        ends = []
        for hops, step in ((self.plus, self.lead), (self.minus, -self.lead)):
            moving = None
            for left in range(hops, 0, -1):
                part = part_of((place + step * left) % n)
                if moving is not None:
                    part = (part.astype(F32) + moving.astype(F32)).astype(BF16)
                moving = self.move(part, step)
            ends.append(moving.astype(F32))
        return (part_of(place).astype(F32) + ends[0] + ends[1]).astype(BF16)

    def gather(self, own, place):
        n = self.count
        found = [(place, own)]
        ahead = back = own
        for hop in range(1, self.plus + 1):
            ahead = self.move(ahead, self.lead)
            found.append(((place - self.lead * hop) % n, ahead))
            if hop <= self.minus:
                back = self.move(back, -self.lead)
                found.append(((place + self.lead * hop) % n, back))
        return found

    def assemble(self, found, dtype):
        block = found[0][1]
        out = jnp.zeros((self.count,) + block.shape, dtype)
        for index, value in found:
            start = (index,) + (0,) * block.ndim
            out = lax.dynamic_update_slice(out, value.astype(dtype)[None], start)
        return out


def swap(value, mask):
    return lax.ppermute(value, "group", [(j, j ^ mask) for j in range(4)])


def spread(own):
    one = swap(own, 1)
    two = swap(own, 2)
    return [own, one, two, swap(two, 1)]


def collect(blocks):
    blocks = [b.astype(BF16) for b in blocks]
    got = swap(jnp.stack([blocks[1], blocks[3]]), 1).astype(F32)
    mine = blocks[0].astype(F32) + got[0]
    other = (blocks[2].astype(F32) + got[1]).astype(BF16)
    return mine + swap(other, 2).astype(F32)


def after(value, *others):
    return lax.optimization_barrier((value,) + others)[0]


def make_body(replicas):
    ring_a = Ring(replicas, 1)
    ring_b = Ring(replicas, -1)

    def body(
        hidden_in,
        out_grad,
        positions,
        block_ids,
        gain_one,
        w_query,
        b_query,
        w_key,
        b_key,
        w_value,
        b_value,
        w_out,
        gain_two,
        w_gate,
        w_up,
        w_down,
    ):
        _, part, width = hidden_in.shape
        length = block_ids.shape[1]
        rows = w_gate.shape[0]
        ff = w_down.shape[0]
        kvp = KVD // 4
        half = replicas // 2
        chunk = 2 * rows // replicas
        me = lax.axis_index("group")
        place = ring_a.place()
        where = me.reshape(1)

        vec_own = jnp.concatenate([gain_one, b_query, b_key, b_value, gain_two])
        vec = spread(vec_own)
        wq = spread(w_query)
        wk = spread(w_key)
        wv = spread(w_value)
        vec = jnp.stack(vec)
        vec = jnp.stack([pick(vec, me ^ j) for j in range(4)]).astype(F32)
        cuts = (0, rows, 2 * rows, 2 * rows + kvp, 2 * rows + 2 * kvp, 3 * rows + 2 * kvp)
        g_one, bq, bk, bv, g_two = [
            vec[:, a:b].reshape(1, -1) for a, b in zip(cuts[:-1], cuts[1:])
        ]
        own, near, far = split(w_gate, w_up, me, place, replicas)
        near = swap(near, 1)
        far = after(far, wq[2])
        far = jnp.stack([swap(far[0], 2), swap(far[1], 3)])
        wo = spread(after(w_out, far))
        dy = spread(after(out_grad[0], wo[2]))
        pieces = ring_a.gather(far, place)
        shape = (2, 4, half, chunk, ff)
        moves = []
        for mat in range(2):
            moves.append((0, lambda s, m=mat: m, lambda s, m=mat: (m, s[0])))
            moves.append((1, lambda s, m=mat: m, lambda s, m=mat: (m, s[0] ^ 1)))
        for i in range(replicas):
            for slot in range(2):
                moves.append(
                    (
                        2 + i,
                        lambda s, j=slot: j,
                        lambda s, i=i, j=slot: (
                            lax.div(s[1 + i], half),
                            s[0] ^ (2 + j),
                            lax.rem(s[1 + i], half),
                        ),
                    )
                )
        sources = [own.reshape(shape[0:1] + shape[2:]), near.reshape(shape[0:1] + shape[2:])]
        spots = jnp.stack([me] + [index for index, _ in pieces])
        w_both = arrange(spots, sources + [value for _, value in pieces], shape, moves)
        w_both = w_both.reshape(2, width, ff)
        wg, wu = w_both[0], w_both[1]

        freqs = THETA ** (-(2.0 * jnp.arange(HEAD_DIM // 2, dtype=F32)) / HEAD_DIM)
        angles = positions[0].astype(F32)[:, None] * jnp.tile(freqs, LANES * 2 // HEAD_DIM)
        sign = jnp.where(jnp.arange(LANES) % HEAD_DIM < HEAD_DIM // 2, -1.0, 1.0)
        cosine = jnp.cos(angles)
        sine = jnp.sin(angles) * sign
        bias = jnp.concatenate([bq, bk, bv], axis=1)
        query, kv, normed_one, w_qkv = project_qkv(
            where, hidden_in[0], g_one, bias, cosine, sine, wq, wk, wv
        )
        kv = spread(kv)
        ids = block_ids.reshape(4, part)
        own_ids = pick(ids, me).reshape(part, 1)
        key_ids = jnp.concatenate([pick(ids, me ^ k) for k in range(4)]).reshape(1, length)
        attended, lse, residual, normed_two, w_o = attend(
            where, hidden_in[0], g_two, own_ids, key_ids, query, kv, wo
        )

        tokens = jnp.concatenate(spread(normed_two), axis=0)
        dy = jnp.concatenate(dy, axis=0)
        grad_hidden = mm_nt(dy, w_down)
        gate = mm(tokens, wg)
        up_value = mm(tokens, wu)
        sigma = jax.nn.sigmoid(gate)
        activated = gate * sigma
        hidden = (activated * up_value).astype(BF16)
        grad_down = mm_tn(hidden, dy).astype(BF16)
        grad_gate_pre = (grad_hidden * up_value * sigma * (1.0 + gate * (1.0 - sigma))).astype(BF16)
        grad_up_pre = (grad_hidden * activated).astype(BF16)
        grad_gate = mm_tn(tokens, grad_gate_pre).astype(BF16).reshape(4, half, chunk, ff)
        grad_up = mm_tn(tokens, grad_up_pre).astype(BF16).reshape(4, half, chunk, ff)

        grad_down = grad_down.reshape(replicas, ff // replicas, width)
        down = ring_a.scatter_sum(lambda p: pick(grad_down, p), place)
        out_down = ring_a.assemble(ring_a.gather(down, place), F32).reshape(ff, width)

        def gate_up(p):
            row = p % half
            return jnp.where(p < half, pick(grad_gate, row, 1), pick(grad_up, row, 1))

        mine = ring_b.scatter_sum(gate_up, place)
        blocks = [pick(mine, me)] + [swap(pick(mine, me ^ k), k) for k in (1, 2, 3)]
        out_gate, out_up = join(ring_b.gather(jnp.stack(blocks), place), me, rows)

        partial = mm(hidden, w_down).reshape(4, part, width)
        layer_out = (residual + collect([partial[k] for k in range(4)])).astype(BF16)
        partial = (mm_nt(grad_gate_pre, wg) + mm_nt(grad_up_pre, wu)).reshape(4, part, width)
        grad_normed_two = collect([partial[k] for k in range(4)])

        scale_two = rms_scale(residual)
        unit_two = residual * scale_two
        grad_gain_two, grad_res_norm = norm_back(grad_normed_two, unit_two, scale_two, g_two)
        grad_residual = out_grad[0].astype(F32) + grad_res_norm
        grad_branch = grad_residual.astype(BF16)
        grad_wo = mm_tn(attended, grad_branch)
        grad_attended = mm_nt(grad_branch, w_o).astype(BF16)
        grad_att_heads = grad_attended.reshape(part, KV_HEADS, GROUPS, HEAD_DIM)
        kv_all = jnp.concatenate(kv, axis=0)
        key_heads = kv_all[:, :KVD].reshape(length, KV_HEADS, HEAD_DIM)
        value_heads = kv_all[:, KVD:].reshape(length, KV_HEADS, HEAD_DIM)
        query_heads = query.reshape(part, KV_HEADS, GROUPS, HEAD_DIM)
        visible = (key_ids <= own_ids)[None, None]
        log_total = lse[:, :HEADS].T.reshape(KV_HEADS, GROUPS, part, 1)
        again = jnp.einsum("qgha,kga->ghqk", query_heads, key_heads, preferred_element_type=F32)
        probs = jnp.where(visible, jnp.exp(again - log_total), 0.0)
        probs_back = probs.astype(BF16)
        grad_probs = jnp.einsum(
            "qgha,kga->ghqk", grad_att_heads, value_heads, preferred_element_type=F32
        )
        grad_values = jnp.einsum(
            "ghqk,qgha->kga", probs_back, grad_att_heads, preferred_element_type=F32
        )
        row_sum = jnp.sum(probs * grad_probs, axis=-1, keepdims=True)
        grad_scores = (probs * (grad_probs - row_sum)).astype(BF16)
        grad_query = (
            jnp.einsum("ghqk,kga->qgha", grad_scores, key_heads, preferred_element_type=F32)
            * FACTOR
        )
        grad_keys = jnp.einsum(
            "ghqk,qgha->kga", grad_scores, query_heads, preferred_element_type=F32
        )
        grad_kv = jnp.concatenate(
            [grad_keys.reshape(4, part, KVD), grad_values.reshape(4, part, KVD)], axis=2
        )
        grad_kv = collect([grad_kv[k] for k in range(4)])
        cos = cosine[:, None, :HEAD_DIM]
        sin = (sine * sign)[:, None, :HEAD_DIM]
        grad_query_pre = rotate(grad_query.reshape(part, HEADS, HEAD_DIM), cos, -sin)
        grad_query_pre = grad_query_pre.astype(BF16).reshape(part, width)
        grad_key_pre = rotate(grad_kv[:, :KVD].reshape(part, KV_HEADS, HEAD_DIM), cos, -sin)
        grad_key_pre = grad_key_pre.astype(BF16).reshape(part, KVD)
        grad_value_pre = grad_kv[:, KVD:].astype(BF16)
        grad_pre = jnp.concatenate([grad_query_pre, grad_key_pre, grad_value_pre], axis=1)
        grad_bias = jnp.sum(grad_pre.astype(F32), axis=0)
        grad_w_qkv = mm_tn(normed_one, grad_pre)
        grad_normed_one = mm_nt(grad_pre, w_qkv)
        x_value = hidden_in[0].astype(F32)
        scale_one = rms_scale(x_value)
        unit_one = x_value * scale_one
        grad_gain_one, grad_in_norm = norm_back(grad_normed_one, unit_one, scale_one, g_one)
        in_grad = (grad_residual + grad_in_norm).astype(BF16)

        wide = width + KVD
        cut = width + KVD
        vectors = jnp.concatenate(
            [
                grad_gain_one.reshape(4, rows),
                grad_bias[:width].reshape(4, rows),
                grad_bias[width:cut].reshape(4, kvp),
                grad_bias[cut:].reshape(4, kvp),
                grad_gain_two.reshape(4, rows),
            ],
            axis=1,
        )
        each = -(-cuts[-1] // replicas)
        vectors = jnp.pad(vectors, ((0, 0), (0, each * replicas - cuts[-1])))
        vectors = vectors.reshape(4, replicas, 1, each)
        vectors = jnp.pad(vectors, ((0, 0), (0, 0), (0, 7), (0, wide - each))).astype(BF16)
        lower = jnp.concatenate([grad_wo, grad_w_qkv[:, cut:]], axis=1)
        packed = [grad_w_qkv[:, :cut].astype(BF16), lower.astype(BF16)]
        packed = [p.reshape(4, half, chunk, wide) for p in packed]
        packed = jnp.concatenate([jnp.concatenate(packed, axis=1), vectors], axis=2)
        packed = collect([pick(packed, me ^ k) for k in range(4)]).astype(BF16)
        mine = ring_a.scatter_sum(lambda p: pick(packed, p), place)
        packed = ring_a.assemble(ring_a.gather(mine, place), F32)
        vectors = packed[:, chunk, :each].reshape(-1)
        packed = packed[:, :chunk].reshape(2, rows, wide)
        vectors = [vectors[a:b] for a, b in zip(cuts[:-1], cuts[1:])]
        return (
            layer_out[None],
            in_grad[None],
            vectors[0],
            packed[0, :, :width],
            vectors[1],
            packed[0, :, width:],
            vectors[2],
            packed[1, :, width:],
            vectors[3],
            packed[1, :, :width],
            vectors[4],
            out_gate,
            out_up,
            out_down,
        )

    return body


def solution(mesh):
    tokens = P("replica", "group", None)
    matrix = P("group", None)
    vector = P("group")
    weights = (
        vector,
        matrix,
        vector,
        matrix,
        vector,
        matrix,
        vector,
        matrix,
        vector,
        matrix,
        matrix,
        matrix,
    )
    in_specs = (tokens, tokens, P("replica", "group"), P("replica", None)) + weights
    out_specs = (tokens, tokens) + weights
    body = make_body(mesh.shape["replica"])
    return jax.shard_map(body, mesh=mesh, in_specs=in_specs, out_specs=out_specs, check_vma=False)
```

```python
import functools

import jax
import jax.numpy as jnp
from jax import lax
from jax.experimental import pallas as pl
from jax.experimental.pallas import tpu as pltpu
from jax.sharding import PartitionSpec as P

HEADS = 14
KV_HEADS = 2
HEAD_DIM = 64
GROUPS = HEADS // KV_HEADS
KVD = KV_HEADS * HEAD_DIM
FACTOR = 1.0 / HEAD_DIM**0.5
LANES = 128
HIDDEN_KEY = -1e30
SPOTS = (0, 256, 512, 768, 896)
VECTOR = 1024

EPSILON = 1e-06
THETA = 1000000.0

F32 = jnp.float32
BF16 = jnp.bfloat16

ANY = pl.BlockSpec(memory_space=pl.ANY)
VMEM = pl.BlockSpec(memory_space=pltpu.VMEM)
SMEM = pl.BlockSpec(memory_space=pltpu.SMEM)


def rms_scale(values):
    return lax.rsqrt(jnp.mean(values * values, axis=-1, keepdims=True) + EPSILON)


def mm(left, right):
    return jnp.dot(left, right, preferred_element_type=F32)


def mm_nt(left, right):
    return lax.dot_general(left, right, (((1,), (1,)), ((), ())), preferred_element_type=F32)


def mm_tn(left, right):
    return lax.dot_general(left, right, (((0,), (0,)), ((), ())), preferred_element_type=F32)


def pick(stack, index, axis=0):
    return lax.dynamic_index_in_dim(stack, index, axis, keepdims=False)


def cost(flops, moved, special=0):
    return pl.CostEstimate(flops=int(flops), bytes_accessed=int(moved), transcendentals=int(special))


def turn_back(values, sine):
    wide = values.shape[1]
    lane = lax.broadcasted_iota(jnp.int32, values.shape, 1) % HEAD_DIM
    ahead = pltpu.roll(values, wide - HEAD_DIM // 2, 1)
    behind = pltpu.roll(values, HEAD_DIM // 2, 1)
    return jnp.where(lane < HEAD_DIM // 2, ahead, behind) * sine


def split_kernel(where, gate, up, own, near, far_a, far_b, *, chunk, ff, step):
    me, place = where[0], where[1]
    half = gate.shape[0] // chunk
    for j in range(4):
        columns = pl.ds(j * ff, ff)
        for target, out in ((me, own), (me ^ 1, near)):

            @pl.when(target == j)
            def _(out=out, columns=columns):
                @pl.loop(0, gate.shape[0] // step)
                def _(i):
                    rows = pl.ds(pl.multiple_of(i * step, step), step)
                    out[0, rows, :] = gate[rows, columns]
                    out[1, rows, :] = up[rows, columns]

        for k, far in ((2, far_a), (3, far_b)):

            @pl.when((me ^ k) == j)
            def _(far=far, columns=columns):
                rows = pl.ds(pl.multiple_of(lax.rem(place, half) * chunk, 8), chunk)
                far[0] = gate[rows, columns]
                far[1] = up[rows, columns]


def pack_kernel(key, value, *refs):
    out = refs[-1]
    rows = key.shape[0]
    out[0:rows, 0:KVD] = key[...]
    out[0:rows, KVD:] = value[...]
    out[rows:, :] = jnp.zeros((out.shape[0] - rows, 2 * KVD), BF16)
    for i, ref in enumerate(refs[:-1]):
        size = ref.shape[0]
        out[rows + 8 * i : rows + 8 * i + 1, 0:size] = ref[...].reshape(1, size)


def pack(key, value, *vectors):
    rows = key.shape[0]
    return pl.pallas_call(
        pack_kernel,
        out_shape=jax.ShapeDtypeStruct((rows + 8 * len(vectors), 2 * KVD), BF16),
        in_specs=[VMEM] * (2 + len(vectors)),
        out_specs=VMEM,
        cost_estimate=cost(0, 8 * rows * KVD),
        name="pack",
    )(key, value, *vectors)


def split(where, gate, up, replicas):
    rows = gate.shape[0]
    ff = gate.shape[1] // 4
    chunk = 2 * rows // replicas
    if chunk % 8:
        me, place = where[0], where[1]
        both = jnp.stack([gate, up]).reshape(2, rows, 4, ff).transpose(2, 0, 1, 3)
        far = [pick(both, me ^ k).reshape(2, replicas // 2, chunk, ff) for k in (2, 3)]
        spot = place % (replicas // 2)
        return pick(both, me), pick(both, me ^ 1), pick(far[0], spot, 1), pick(far[1], spot, 1)
    shape = jax.ShapeDtypeStruct((2, rows, ff), BF16)
    piece = jax.ShapeDtypeStruct((2, chunk, ff), BF16)
    return pl.pallas_call(
        functools.partial(split_kernel, chunk=chunk, ff=ff, step=32),
        out_shape=(shape, shape, piece, piece),
        in_specs=[SMEM, VMEM, VMEM],
        out_specs=(VMEM,) * 4,
        cost_estimate=cost(0, 16 * rows * ff),
        name="split",
    )(where, gate, up)


def arrange_kernel(where, *refs, moves):
    out, sems = refs[-2], refs[-1]
    copies = []
    for i, (source, take, put) in enumerate(moves):
        copy = pltpu.make_async_copy(refs[source].at[take(where)], out.at[put(where)], sems.at[i])
        copy.start()
        copies.append(copy)
    for copy in copies:
        copy.wait()


def arrange(where, sources, shape, moves):
    size = 1
    for extent in shape:
        size *= extent
    return pl.pallas_call(
        functools.partial(arrange_kernel, moves=moves),
        out_shape=jax.ShapeDtypeStruct(shape, BF16),
        in_specs=[SMEM] + [ANY] * len(sources),
        out_specs=VMEM,
        scratch_shapes=[pltpu.SemaphoreType.DMA((len(moves),))],
        cost_estimate=cost(0, 4 * size),
        name="arrange",
    )(where, *sources)


def join_kernel(where, *refs, offsets, half, ff):
    count = len(offsets)
    pieces = refs[:count]
    gate, up, slab, sems = refs[-4:]
    me = where[0]
    chunk = pieces[0].shape[1]

    def spot(i):
        return lax.rem(where[1] + offsets[i] + 2 * half, 2 * half)

    def copy(i, out):
        row = pl.multiple_of(lax.rem(spot(i), half) * chunk, 8)
        return pltpu.make_async_copy(slab.at[i % 2], out.at[pl.ds(row, chunk), :], sems.at[i])

    for i in range(count):
        if i >= 2:
            copy(i - 2, gate).wait()
        for j in range(4):
            slab[i % 2, :, pl.ds(j * ff, ff)] = pieces[i][me ^ j].astype(F32)

        @pl.when(spot(i) < half)
        def _(i=i):
            copy(i, gate).start()

        @pl.when(spot(i) >= half)
        def _(i=i):
            copy(i, up).start()

    for i in range(count - 2, count):
        copy(i, gate).wait()


def join(offsets, where, rows, replicas, values, *before):
    count = len(offsets)
    _, chunk, ff = values[0].shape
    half = replicas // 2
    if chunk % 8:
        got = before[0] if before else jnp.zeros((replicas, chunk, 4, ff), F32)
        for offset, value in zip(offsets, values):
            value = jnp.stack([pick(value, where[0] ^ j) for j in range(4)], axis=1)
            spot = (where[1] + offset) % replicas
            got = lax.dynamic_update_slice(got, value.astype(F32)[None], (spot, 0, 0, 0))
        return got, got
    shape = jax.ShapeDtypeStruct((rows, 4 * ff), F32)
    return pl.pallas_call(
        functools.partial(join_kernel, offsets=offsets, half=half, ff=ff),
        out_shape=(shape, shape),
        in_specs=[SMEM] + [VMEM] * count + [ANY] * len(before),
        out_specs=(ANY, ANY),
        scratch_shapes=[pltpu.VMEM((2, chunk, 4 * ff), F32), pltpu.SemaphoreType.DMA((count,))],
        input_output_aliases={1 + count: 0, 2 + count: 1} if before else {},
        cost_estimate=cost(0, 48 * rows * ff * count // replicas),
        name="join",
    )(where, *values, *before)


def joined(gate, up, rows):
    if gate.ndim == 2:
        return gate, up
    gate = gate.reshape(2, rows, -1)
    return gate[0], gate[1]


def load_rows(where, blocks, out, sems, first):
    rows = blocks[0].shape[0]
    copies = []
    for k, block in enumerate(blocks):
        row = pl.multiple_of((where[0] ^ k) * rows, 8)
        copies.append(pltpu.make_async_copy(block, out.at[pl.ds(row, rows), :], sems.at[first + k]))
        copies[-1].start()
    return copies


def order_vec(me, blocks, row, size, out, to):
    parts = [b[row : row + 1, 0:size].astype(F32) for b in blocks]
    odd = jnp.full(parts[0].shape, me % 2, jnp.int32) == 1
    far = jnp.full(parts[0].shape, me // 2, jnp.int32) == 1
    for j in range(4):
        same = jnp.where(odd, parts[j ^ 1], parts[j])
        other = jnp.where(odd, parts[j ^ 3], parts[j ^ 2])
        out[pl.ds(to, 1), pl.ds(j * size, size)] = jnp.where(far, other, same)


def four(own, other, two):
    return (own, other.at[0], two, other.at[1])


def kv_kernel(where, hidden, cosine, sine, own, other, two, kv, normed_out, vectors, weights):
    blocks = four(own, other, two)
    width = hidden.shape[1]
    rows = width // 4
    vectors[...] = jnp.zeros_like(vectors)
    for i, size in enumerate((rows, rows, rows, KVD // 4, KVD // 4)):
        order_vec(where[0], blocks, rows + 8 * i, size, vectors, i)
    for k, block in enumerate(blocks):
        row = pl.multiple_of((where[0] ^ k) * rows, 8)
        weights[pl.ds(row, rows), :] = block[0:rows, :]
    x = hidden[...].astype(F32)
    normed = (x * rms_scale(x) * vectors[0:1, 0:width]).astype(BF16)
    normed_out[...] = normed
    both = mm(normed, weights[...])
    key = both[:, :KVD] + vectors[3:4, 0:KVD]
    key = key * cosine[...] + turn_back(key, sine[...])
    kv[:, 0:KVD] = key.astype(BF16)
    kv[:, KVD : 2 * KVD] = (both[:, KVD:] + vectors[4:5, 0:KVD]).astype(BF16)


def project_kv(where, hidden, cosine, sine, *blocks):
    part, width = hidden.shape
    return pl.pallas_call(
        kv_kernel,
        out_shape=(
            jax.ShapeDtypeStruct((part, 2 * KVD), BF16),
            jax.ShapeDtypeStruct((part, width), BF16),
            jax.ShapeDtypeStruct((8, width), F32),
            jax.ShapeDtypeStruct((width, 2 * KVD), BF16),
        ),
        in_specs=[SMEM] + [VMEM] * 6,
        out_specs=(VMEM,) * 4,
        cost_estimate=cost(4 * part * width * KVD, 4 * part * width),
        name="kv",
    )(where, hidden, cosine, sine, *blocks)


def heads_forward(heads, query, kv, mask, attended, logs, first):
    lane = lax.broadcasted_iota(jnp.int32, logs.shape, 1)
    for h in heads:
        g = h // GROUPS
        keys = kv[:, pl.ds(g * HEAD_DIM, HEAD_DIM)]
        values = kv[:, pl.ds(KVD + g * HEAD_DIM, HEAD_DIM)]
        lanes = pl.ds(h * HEAD_DIM, HEAD_DIM)
        scores = mm_nt(query[:, lanes], keys) + mask[...]
        top = jnp.max(scores, axis=-1, keepdims=True)
        raised = jnp.exp(scores - top)
        total = jnp.sum(raised, axis=-1, keepdims=True)
        logs = jnp.where(lane == h, top + jnp.log(total), logs)
        probs = (raised * (1.0 / total)).astype(BF16)
        attended[:, pl.ds(h * HEAD_DIM - first, HEAD_DIM)] = mm(probs, values).astype(BF16)
    return logs


def attend_kernel(where, normed_one, vectors, cosine, sine, own_ids, key_ids, *refs, heads):
    blocks, wq = four(*refs[0:3]), four(*refs[3:6])
    query, attended, lse, w_q, kv, mask, sems = refs[6:]
    part, width = normed_one.shape
    copies = load_rows(where, wq, w_q, sems, 0)
    for k, block in enumerate(blocks):
        kv[pl.ds(k * part, part), :] = block[...]
    mask[...] = jnp.where(key_ids[...] <= own_ids[...], 0.0, HIDDEN_KEY)
    cos, sin = cosine[...], sine[...]
    for copy in copies:
        copy.wait()
    for first in range(0, width, LANES):
        lanes = pl.ds(first, LANES)
        value = mm(normed_one[...], w_q[:, lanes]) + vectors[1:2, lanes]
        value = value * cos + turn_back(value, sin)
        query[:, lanes] = (value.astype(BF16).astype(F32) * FACTOR).astype(BF16)
    logs = jnp.zeros((part, LANES), F32)
    lse[...] = heads_forward(heads, query, kv, mask, attended, logs, 0)


def attend(heads, where, normed_one, vectors, cosine, sine, own_ids, key_ids, kv, wq):
    part, width = normed_one.shape
    length = key_ids.shape[1]
    work = part * length * len(heads)
    return pl.pallas_call(
        functools.partial(attend_kernel, heads=heads),
        out_shape=(
            jax.ShapeDtypeStruct((part, width), BF16),
            jax.ShapeDtypeStruct((part, len(heads) * HEAD_DIM), BF16),
            jax.ShapeDtypeStruct((part, LANES), F32),
            jax.ShapeDtypeStruct((width, width), BF16),
            jax.ShapeDtypeStruct((length, 2 * KVD), BF16),
            jax.ShapeDtypeStruct((part, length), F32),
        ),
        in_specs=[SMEM] + [VMEM] * 9 + [ANY] * 3,
        out_specs=(VMEM,) * 6,
        scratch_shapes=[pltpu.SemaphoreType.DMA((4,))],
        cost_estimate=cost(4 * work * HEAD_DIM + 2 * part * width * width, 8 * part * width, work),
        name="attend",
    )(where, normed_one, vectors, cosine, sine, own_ids, key_ids, *kv, *wq)


def residual_kernel(where, hidden, vectors, mask, query, kv, before, lse_before, *refs, heads):
    wo = four(*refs[0:3])
    attended, lse, residual, normed, w_o, sems = refs[3:]
    first = before.shape[1]
    late = load_rows(where, wo, w_o, sems, 0)
    attended[:, 0:first] = before[...]
    lse[...] = heads_forward(heads, query, kv, mask, attended, lse_before[...], 0)
    for copy in late:
        copy.wait()
    value = hidden[...].astype(F32) + mm(attended[...], w_o[...])
    residual[...] = value
    normed[...] = (value * rms_scale(value) * vectors[2:3, :]).astype(BF16)


def attend_rest(heads, where, hidden, vectors, mask, query, kv, before, lse, wo):
    part, width = hidden.shape
    work = part * kv.shape[0] * len(heads)
    tokens = jax.ShapeDtypeStruct((part, width), BF16)
    return pl.pallas_call(
        functools.partial(residual_kernel, heads=heads),
        out_shape=(
            tokens,
            jax.ShapeDtypeStruct((part, LANES), F32),
            jax.ShapeDtypeStruct((part, width), F32),
            tokens,
            jax.ShapeDtypeStruct((width, width), BF16),
        ),
        in_specs=[SMEM] + [VMEM] * 7 + [ANY] * 3,
        out_specs=(VMEM,) * 5,
        scratch_shapes=[pltpu.SemaphoreType.DMA((4,))],
        cost_estimate=cost(4 * work * HEAD_DIM + 2 * part * width * width, 8 * part * width, work),
        name="attend_rest",
    )(where, hidden, vectors, mask, query, kv, before, lse, *wo)


def units_kernel(one, two, grad_hidden, weights, tokens, hidden, dgate, dup):
    part = one.shape[0]
    tokens[0:part, :] = one[...]
    tokens[part:, :] = two[...]
    value = tokens[...]
    gate = mm(value, weights[0])
    up = mm(value, weights[1])
    back = grad_hidden[...]
    sigma = jax.nn.sigmoid(gate)
    active = gate * sigma
    hidden[...] = (active * up).astype(BF16)
    dup[...] = (back * active).astype(BF16)
    dgate[...] = (back * up * sigma * (1.0 + gate * (1.0 - sigma))).astype(BF16)


def back_units_kernel(dy_one, dy_two, w_down, out, dy, *, slot):
    part = dy_one.shape[0]
    dy[0:part, :] = dy_one[...]
    dy[part:, :] = dy_two[slot]
    out[...] = mm_nt(dy[...], w_down[...])


def back_units(slot, dy_one, dy_two, w_down):
    part, width = dy_one.shape
    ff = w_down.shape[0]
    return pl.pallas_call(
        functools.partial(back_units_kernel, slot=slot),
        out_shape=(
            jax.ShapeDtypeStruct((2 * part, ff), F32),
            jax.ShapeDtypeStruct((2 * part, width), BF16),
        ),
        in_specs=[VMEM] * 3,
        out_specs=(VMEM, VMEM),
        cost_estimate=cost(4 * part * width * ff, 2 * width * ff + 8 * part * ff),
        name="back_units",
    )(dy_one, dy_two, w_down)


def units(one, two, grad_hidden, weights):
    part, width = one.shape
    ff = weights.shape[2]
    shape = jax.ShapeDtypeStruct((2 * part, ff), BF16)
    return pl.pallas_call(
        units_kernel,
        out_shape=(jax.ShapeDtypeStruct((2 * part, width), BF16), shape, shape, shape),
        in_specs=[VMEM] * 4,
        out_specs=(VMEM,) * 4,
        cost_estimate=cost(8 * part * width * ff, 6 * width * ff, 2 * part * ff),
        name="units",
    )(one, two, grad_hidden, weights)


def weight_kernel(*refs, count):
    left_a, left_b = refs[0:2]
    rights = refs[2 : 2 + 2 * count]
    outs = refs[2 + 2 * count :]
    for i, out in enumerate(outs):
        total = mm_tn(left_a[...], rights[2 * i][...]) + mm_tn(left_b[...], rights[2 * i + 1][...])
        out[...] = total.astype(BF16)


def weight_grads(left, rights):
    tall = left[0].shape[1]
    wide = rights[0][0].shape[1]
    count = len(rights)
    shape = jax.ShapeDtypeStruct((tall, wide), BF16)
    return pl.pallas_call(
        functools.partial(weight_kernel, count=count),
        out_shape=(shape,) * count,
        in_specs=[VMEM] * (2 + 2 * count),
        out_specs=(VMEM,) * count,
        cost_estimate=cost(4 * count * left[0].shape[0] * tall * wide, 6 * count * tall * wide),
        name="weight_grads",
    )(*left, *[r for pair in rights for r in pair])


def partial_kernel(*refs, mats, transposed):
    lefts = refs[: 2 * mats]
    weights, keep, send = refs[2 * mats :]
    part = keep.shape[1]
    for chip in range(2):
        if transposed:
            total = mm_nt(lefts[2 * chip][...], weights[0])
            total += mm_nt(lefts[2 * chip + 1][...], weights[1])
        else:
            total = mm(lefts[chip][...], weights[...])
        keep[chip] = total[:part].astype(BF16)
        send[chip] = total[part:].astype(BF16)


def partial_sums(lefts, weights, width, transposed):
    rows = lefts[0].shape[0]
    mats = len(lefts) // 2
    shape = jax.ShapeDtypeStruct((2, rows // 2, width), BF16)
    return pl.pallas_call(
        functools.partial(partial_kernel, mats=mats, transposed=transposed),
        out_shape=(shape, shape),
        in_specs=[VMEM] * (2 * mats + 1),
        out_specs=(VMEM, VMEM),
        cost_estimate=cost(4 * mats * rows * lefts[0].shape[1] * width, 8 * mats * rows * width),
        name="partial_sums",
    )(*lefts, weights)


def branch_kernel(own, near, far, residual, dy, vectors, w_o, dresidual, dbranch, dattended, gain):
    value = residual[...]
    scale = rms_scale(value)
    unit = value * scale
    grad = own[0].astype(F32) + near[0].astype(F32) + far[...].astype(F32)
    gain[...] = jnp.sum(grad * unit, axis=0, keepdims=True)
    inner = grad * vectors[2:3, :]
    total = scale * (inner - unit * jnp.mean(inner * unit, axis=-1, keepdims=True))
    total = dy[...].astype(F32) + total
    dresidual[...] = total
    low = total.astype(BF16)
    dbranch[...] = low
    dattended[...] = mm_nt(low, w_o[...]).astype(BF16)


def branch_back(own, near, far, residual, dy, vectors, w_o):
    part, width = residual.shape
    tokens = jax.ShapeDtypeStruct((part, width), BF16)
    return pl.pallas_call(
        branch_kernel,
        out_shape=(
            jax.ShapeDtypeStruct((part, width), F32),
            tokens,
            tokens,
            jax.ShapeDtypeStruct((1, width), F32),
        ),
        in_specs=[VMEM] * 7,
        out_specs=(VMEM,) * 4,
        cost_estimate=cost(2 * part * width * width, 20 * part * width),
        name="branch_back",
    )(own, near, far, residual, dy, vectors, w_o)


def back_kernel(mask, query, kv, lse, dattended, *refs, heads, first):
    dquery, dkv = refs[-2:]
    logs = lse[...]
    lane = lax.broadcasted_iota(jnp.int32, logs.shape, 1)
    if len(refs) > 2:
        dkv[...] = refs[0][...]
    else:
        dkv[...] = jnp.zeros_like(dkv)
    for h in heads:
        g = h // GROUPS
        k_lanes = pl.ds(g * HEAD_DIM, HEAD_DIM)
        v_lanes = pl.ds(KVD + g * HEAD_DIM, HEAD_DIM)
        lanes = pl.ds(h * HEAD_DIM, HEAD_DIM)
        q, do = query[:, lanes], dattended[:, lanes]
        keys, values = kv[:, k_lanes], kv[:, v_lanes]
        log = jnp.sum(jnp.where(lane == h, logs, 0.0), axis=-1, keepdims=True)
        probs = jnp.exp(mm_nt(q, keys) + mask[...] - log)
        dprobs = mm_nt(do, values)
        total = jnp.sum(probs * dprobs, axis=-1, keepdims=True)
        dscores = (probs * (dprobs - total)).astype(BF16)
        dquery[:, pl.ds(h * HEAD_DIM - first, HEAD_DIM)] = mm(dscores, keys) * FACTOR
        dkv[:, k_lanes] += mm_tn(dscores, q)
        dkv[:, v_lanes] += mm_tn(probs.astype(BF16), do)


def attend_back(heads, mask, query, kv, lse, dattended, *before):
    part = query.shape[0]
    length = kv.shape[0]
    first = heads[0] * HEAD_DIM
    work = part * length * len(heads)
    return pl.pallas_call(
        functools.partial(back_kernel, heads=heads, first=first),
        out_shape=(
            jax.ShapeDtypeStruct((part, len(heads) * HEAD_DIM), F32),
            jax.ShapeDtypeStruct((length, 2 * KVD), F32),
        ),
        in_specs=[VMEM] * (5 + len(before)),
        out_specs=(VMEM, VMEM),
        cost_estimate=cost(10 * work * HEAD_DIM, 8 * length * KVD, work),
        name="attend_back",
    )(mask, query, kv, lse, dattended, *before)


def grads_kernel(where, hidden, normed, attended, dbranch, dresidual, dq_a, dq_b, own, near, far, cosine, sine, vectors, gain_two, w_q, w_kv, in_grad, keep, send, dpre, weights, values):
    me = where[0]
    part, width = hidden.shape
    rows = width // 4
    cos, sin = cosine[...], sine[...]
    split_at = dq_a.shape[1]
    grad = own[0].astype(F32) + near[0].astype(F32) + far[...].astype(F32)
    for first in range(0, width + KVD, LANES):
        if first < split_at:
            value = dq_a[:, pl.ds(first, LANES)]
        elif first < width:
            value = dq_b[:, pl.ds(first - split_at, LANES)]
        else:
            value = grad[:, :KVD]
        dpre[:, pl.ds(first, LANES)] = (value * cos - turn_back(value, sin)).astype(BF16)
    dpre[:, pl.ds(width + KVD, KVD)] = grad[:, KVD:].astype(BF16)
    bias = jnp.sum(dpre[...].astype(F32), axis=0, keepdims=True)

    x = hidden[...].astype(F32)
    scale = rms_scale(x)
    unit = x * scale
    back = mm_nt(dpre[:, 0:width], w_q[...]) + mm_nt(dpre[:, pl.ds(width, 2 * KVD)], w_kv[...])
    gain_one = jnp.sum(back * unit, axis=0, keepdims=True)
    inner = back * vectors[0:1, :]
    total = scale * (inner - unit * jnp.mean(inner * unit, axis=-1, keepdims=True))
    in_grad[...] = (dresidual[...] + total).astype(BF16)

    cut = width + KVD
    weights[:, 0, :] = mm_tn(normed[...], dpre[:, pl.ds(0, cut)]).reshape(4, rows, cut)
    weights[:, 1, :, 0:width] = mm_tn(attended[...], dbranch[...]).reshape(4, rows, width)
    weights[:, 1, :, width:cut] = mm_tn(normed[...], dpre[:, pl.ds(cut, KVD)]).reshape(4, rows, KVD)
    sizes = (rows, rows, rows, KVD // 4, KVD // 4)
    sources = (gain_one, bias[:, :width], gain_two[...], bias[:, width:cut], bias[:, cut:])
    values[...] = jnp.zeros_like(values)
    for j in range(4):
        for spot, size, source in zip(SPOTS, sizes, sources):
            values[j, 0:1, pl.ds(spot, size)] = source[:, j * size : (j + 1) * size]
    count = keep.shape[1]
    chunk = 2 * rows // count
    half = count // 2
    each = VECTOR // count
    for k in range(4):
        out = (keep, send)[k % 2]
        j = me ^ k
        for r in range(count):
            if count == 1:
                out[k // 2, 0, 0:rows, :] = weights[j, 0].astype(BF16)
                out[k // 2, 0, rows:chunk, :] = weights[j, 1].astype(BF16)
            else:
                part_of = weights[j, r // half, pl.ds((r % half) * chunk, chunk), :]
                out[k // 2, r, 0:chunk, :] = part_of.astype(BF16)
            if each < cut:
                out[k // 2, r, pl.ds(chunk, 8), :] = jnp.zeros((8, cut), BF16)
            out[k // 2, r, pl.ds(chunk, 8), 0:each] = values[j, :, pl.ds(r * each, each)].astype(BF16)


def attention_grads(replicas, where, hidden, *args):
    part, width = hidden.shape
    rows = width // 4
    chunk = 2 * rows // replicas
    wide = width + KVD
    aligned = chunk % 8 == 0
    count = replicas if aligned else 1
    shape = jax.ShapeDtypeStruct((2, count, 2 * rows // count + 8, wide), BF16)
    in_grad, *packed = pl.pallas_call(
        grads_kernel,
        out_shape=(jax.ShapeDtypeStruct((part, width), BF16), shape, shape),
        in_specs=[SMEM] + [VMEM] * 16,
        out_specs=(VMEM,) * 3,
        scratch_shapes=[
            pltpu.VMEM((part, width + 2 * KVD), BF16),
            pltpu.VMEM((4, 2, rows, wide), F32),
            pltpu.VMEM((4, 8, VECTOR), F32),
        ],
        cost_estimate=cost(12 * part * width * width, 20 * width * width),
        name="attention_grads",
    )(where, hidden, *args)
    if not aligned:
        each = VECTOR // replicas
        for i, value in enumerate(packed):
            weights = value[:, 0, : 2 * rows].reshape(2, replicas, chunk, wide)
            values = value[:, 0, 2 * rows :].reshape(2, 8, replicas, each).transpose(0, 2, 1, 3)
            values = jnp.pad(values, ((0, 0), (0, 0), (0, 0), (0, wide - each)))
            packed[i] = jnp.concatenate([weights, values], axis=2)
    return in_grad, *packed


class Order:
    def __init__(self):
        self.last = None

    def __call__(self, run, *values):
        values = self.hold(*values)
        found = run(*values)
        self.last = tuple(found) if isinstance(found, (tuple, list)) else (found,)
        return found

    def wait(self, *values):
        self.last = (*(self.last or ()), *values)

    def hold(self, *values):
        if self.last is None:
            return values
        return lax.optimization_barrier((*values, *self.last))[: len(values)]


class Ring:
    def __init__(self, count, lead):
        self.count = count
        self.lead = lead
        self.order = [0, 2, 4, 6, 7, 5, 3, 1] if count == 8 else list(range(count))
        self.plus = count // 2
        self.minus = count - 1 - self.plus

    def place(self):
        replica = lax.axis_index("replica")
        if self.count == 8:
            line, side = replica // 2, replica % 2
            return jnp.where(side == 0, line, 7 - line)
        return replica

    def replica(self, place):
        if self.count == 8:
            return jnp.where(place < 4, 2 * place, 15 - 2 * place)
        return place

    def move(self, value, step):
        n = self.count
        pairs = [(self.order[p], self.order[(p + step) % n]) for p in range(n)]
        return lax.ppermute(value, "replica", pairs)

    def both(self):
        return ((self.plus, self.lead), (self.minus, -self.lead))


class RingSum:
    def __init__(self, ring, order, place, take, *arrays):
        self.ring, self.order, self.place, self.take, self.arrays = ring, order, place, take, arrays
        self.left = [hops for hops, _ in ring.both()]
        self.arrived = []
        self.moving = self._send(None)

    def _send(self, moving):
        ring = self.ring
        active = [i for i in range(2) if self.left[i] > 0]

        def run(*values):
            parts = []
            for n, i in enumerate(active):
                step = ring.both()[i][1]
                part = self.take((self.place + step * self.left[i]) % ring.count, *values[: len(self.arrays)])
                if moving is not None:
                    got = values[len(self.arrays) + n]
                    part = (part.astype(F32) + got.astype(F32)).astype(BF16)
                parts.append(part)
            return parts

        got = [] if moving is None else [moving[i] for i in active]
        parts = self.order(run, *self.arrays, *got)
        sent = [None, None]
        for part, i in zip(parts, active):
            sent[i] = ring.move(part, ring.both()[i][1])
            self.left[i] -= 1
            if self.left[i] == 0:
                self.arrived.append(sent[i])
        return sent

    def step(self):
        self.moving = self._send(self.moving)

    def total(self):
        while max(self.left) > 0:
            self.step()
        count = len(self.arrays)

        def run(*values):
            own = self.take(self.place, *values[:count]).astype(F32)
            return sum((v.astype(F32) for v in values[count:]), own).astype(BF16)

        return self.order(run, *self.arrays, *self.arrived)


class RingGather:
    def __init__(self, ring, order, place, own):
        self.ring, self.order, self.place = ring, order, place
        self.found = [(0, own)]
        self.hop = 0
        self.moving = [own, own]
        self._send()

    def _send(self):
        self.hop += 1
        for i, (hops, step) in enumerate(self.ring.both()):
            if self.hop <= hops:
                self.moving[i] = self.ring.move(self.moving[i], step)
                self.found.append((-step * self.hop, self.moving[i]))

    def step(self):
        if self.hop < self.ring.plus:
            self.moving = list(self.order(lambda *v: v, *self.moving))
            self._send()

    def finish(self):
        while self.hop < self.ring.plus:
            self.step()
        return self.found


class Share:
    def __init__(self, ring, order, place, own):
        self.ring, self.order, self.place = ring, order, place
        self.found = [(0, (0, 1), own)]
        self.hop = 0
        self.moving = [own, own]
        self._send()

    def _send(self):
        self.hop += 1
        for i, step in enumerate((1, -1)):
            halves = (0, 1)
            if self.hop == self.ring.count // 4:
                halves = (i,)
                self.moving[i] = self.moving[i][:, i : i + 1]
            self.moving[i] = self.ring.move(self.moving[i], step)
            self.found.append((-step * self.hop, halves, self.moving[i]))

    def step(self):
        self.moving = list(self.order(lambda *v: v, *self.moving))
        self._send()


def assemble(found, place, dtype):
    block = found[0][1]
    out = jnp.zeros((len(found),) + block.shape, dtype)
    for offset, value in found:
        start = ((place + offset) % len(found),) + (0,) * block.ndim
        out = lax.dynamic_update_slice(out, value.astype(dtype)[None], start)
    return out


def swap(value, mask):
    return lax.ppermute(value, "group", [(j, j ^ mask) for j in range(4)])


def spread(own):
    one = swap(own, 1)
    two = swap(own, 2)
    return [own, one, two, swap(two, 1)]


class Spread:
    def __init__(self, own):
        self.own, self.two = own, swap(own, 2)

    def step(self, order):
        self.other = swap(order(lambda *v: jnp.stack(v), self.own, self.two), 1)

    def parts(self):
        return self.own, self.other, self.two


class Collect:
    def __init__(self, order, keep, send):
        self.order, self.keep, self.got = order, keep, swap(send, 1)

    def step(self):
        def run(keep, got):
            return (keep[1].astype(F32) + got[1].astype(F32)).astype(BF16)

        self.other = swap(self.order(run, self.keep, self.got), 2)

    def terms(self):
        return self.keep, self.got, self.other


def after(value, *others):
    return lax.optimization_barrier((value,) + others)[0]


FIRST_HEADS = range(0, 8)
OTHER_HEADS = range(8, HEADS)


def make_body(replicas):
    ring_up = Ring(replicas, 1)
    ring_down = Ring(replicas, -1)

    def body(
        hidden_in,
        out_grad,
        positions,
        block_ids,
        gain_one,
        w_query,
        b_query,
        w_key,
        b_key,
        w_value,
        b_value,
        w_out,
        gain_two,
        w_gate,
        w_up,
        w_down,
    ):
        _, part, width = hidden_in.shape
        length = block_ids.shape[1]
        rows = w_gate.shape[0]
        ff = w_down.shape[0]
        half = replicas // 2
        chunk = 2 * rows // replicas
        me = lax.axis_index("group")
        place = ring_up.place()
        where = jnp.stack([me, place])
        order = Order()
        x_value, dy_own = hidden_in[0], out_grad[0]

        wq = Spread(w_query)
        first = Spread(order(pack, w_key, w_value, gain_one, b_query, gain_two, b_key, b_value))
        own, near, far_a, far_b = order(
            lambda gate, up: split(where, gate, up, replicas), w_gate, w_up
        )
        wq.step(order)
        far_a, far_b = swap(after(far_a, wq.two), 2), swap(after(far_b, wq.two), 3)
        first.step(order)
        x_late, spots, ids = order.hold(x_value, positions[0], block_ids.reshape(4, part))
        freqs = THETA ** (-(2.0 * jnp.arange(HEAD_DIM // 2, dtype=F32)) / HEAD_DIM)
        angles = spots.astype(F32)[:, None] * jnp.tile(freqs, LANES * 2 // HEAD_DIM)
        sign = jnp.where(jnp.arange(LANES) % HEAD_DIM < HEAD_DIM // 2, -1.0, 1.0)
        cosine = jnp.cos(angles)
        sine = jnp.sin(angles) * sign
        own_ids = pick(ids, me).reshape(part, 1)
        key_ids = jnp.concatenate([pick(ids, me ^ k) for k in range(4)]).reshape(1, length)

        kv, normed_one, vectors, w_kv = order(
            lambda *v: project_kv(where, *v), x_late, cosine, sine, *first.parts()
        )
        kv = Spread(kv)
        far = order(lambda *v: jnp.stack(v), far_a, far_b)
        pieces = Share(ring_up, order, place, far)
        kv.step(order)
        wo = Spread(after(w_out, kv.two))
        query, attended, lse, w_q, kv, mask = order(
            lambda *v: attend(FIRST_HEADS, where, *v[:6], v[6:9], v[9:]),
            normed_one,
            vectors,
            cosine,
            sine,
            own_ids,
            key_ids,
            *kv.parts(),
            *wq.parts(),
        )
        pieces.step()
        wo.step(order)
        dy = Spread(after(dy_own, wo.two))
        near = swap(after(near, query), 1)
        attended, lse, residual, normed_two, w_o = order(
            lambda *v: attend_rest(OTHER_HEADS, where, *v[:7], v[7:]),
            x_value,
            vectors,
            mask,
            query,
            kv,
            attended,
            lse,
            *wo.parts(),
        )
        while pieces.hop < replicas // 4:
            pieces.step()
        order.wait(*[value for _, _, value in pieces.found])
        (normed_late,) = order.hold(normed_two)
        one, two = swap(normed_late, 1), swap(normed_late, 2)
        shape = (2, 4, half, chunk, ff)
        moves = []
        for mat in range(2):
            for source in (0, 1):
                moves.append((source, lambda s, m=mat: m, lambda s, m=mat, k=source: (m, s[0] ^ k)))
        for i, (offset, mats, _) in enumerate(pieces.found):
            for slot in range(2):
                for n, mat in enumerate(mats):
                    put = lambda s, d=offset + half, m=mat, k=2 + slot: (m, s[0] ^ k, lax.rem(s[1] + d, half))
                    moves.append((2 + i, lambda s, j=slot, n=n: (j, n), put))
        w_both = order(
            lambda *v: arrange(where, v, shape, moves),
            *[v.reshape(shape[:1] + shape[2:]) for v in (own, near)],
            *[value for _, _, value in pieces.found],
        )
        w_both = w_both.reshape(2, width, ff)

        dy.step(order)
        grad_hidden, dy_a = order(functools.partial(back_units, 0), dy.own, dy.other, w_down)
        tok_a, hid_a, dgate_a, dup_a = order(units, normed_two, one, grad_hidden, w_both)
        three = swap(two, 1)
        grad_hidden, dy_b = order(functools.partial(back_units, 1), dy.two, dy.other, w_down)
        tok_b, hid_b, dgate_b, dup_b = order(units, two, three, grad_hidden, w_both)
        grad_gate, grad_up = order(
            lambda *v: weight_grads(v[:2], [v[2:4], v[4:6]]),
            tok_a,
            tok_b,
            dgate_a,
            dgate_b,
            dup_a,
            dup_b,
        )

        def take_units(p, gate, up):
            row = p % half
            return jnp.where(p < half, pick(gate, row, 1), pick(up, row, 1))

        shape = (4, half, chunk, ff)
        sum_units = RingSum(
            ring_up, order, place, take_units, grad_gate.reshape(shape), grad_up.reshape(shape)
        )
        sums = order(
            lambda *v: partial_sums(v[:4], v[4], width, True), dgate_a, dup_a, dgate_b, dup_b, w_both
        )
        to_normed = Collect(order, *sums)
        sum_units.step()
        to_normed.step()
        (grad_down,) = order(lambda *v: weight_grads(v[:2], [v[2:]]), hid_a, hid_b, dy_a, dy_b)
        grad_down = grad_down.reshape(replicas, ff // replicas, width)
        sum_down = RingSum(ring_down, order, place, lambda p, v: pick(v, p), grad_down)

        dresidual, dbranch, dattended, grad_gain_two = order(
            branch_back, *to_normed.terms(), residual, dy_own, vectors, w_o
        )
        sum_units.step()
        sum_down.step()
        args = (mask, query, kv, lse, dattended)
        dq_a, dkv = order(functools.partial(attend_back, FIRST_HEADS), *args)
        sum_units.step()
        sum_down.step()
        dq_b, dkv = order(functools.partial(attend_back, OTHER_HEADS), *args, dkv)
        dkv = dkv.astype(BF16).reshape(2, 2, part, 2 * KVD)
        to_kv = Collect(order, dkv[:, 0], dkv[:, 1])
        sum_down.step()
        mine = sum_units.total()
        to_kv.step()
        blocks = [pick(mine, me)] + [swap(pick(mine, me ^ k), k) for k in (1, 2, 3)]
        sums = order(lambda *v: partial_sums(v[:2], v[2], width, False), hid_a, hid_b, w_down)
        all_units = RingGather(ring_up, order, place, order(lambda *v: jnp.stack(v), *blocks))
        all_down = RingGather(ring_down, order, place, sum_down.total())
        in_grad, *packed = order(
            lambda *v: attention_grads(replicas, where, *v),
            x_value,
            normed_one,
            attended,
            dbranch,
            dresidual,
            dq_a,
            dq_b,
            *to_kv.terms(),
            cosine,
            sine,
            vectors,
            grad_gain_two,
            w_q,
            w_kv,
        )
        all_units.step()
        to_weights = Collect(order, *order.hold(*packed))
        all_down.step()
        to_weights.step()
        all_units.step()
        all_down.step()

        packed = order(
            lambda keep, got, other: (
                keep[0].astype(F32) + got[0].astype(F32) + other.astype(F32)
            ).astype(BF16),
            *to_weights.terms(),
        )
        sum_packed = RingSum(ring_down, order, place, lambda p, v: pick(v, p), packed)
        all_units.step()
        all_down.step()
        sum_packed.step()
        to_out = Collect(order, *order.hold(*sums))
        sum_packed.step()
        to_out.step()
        first = all_units.found[:5]
        offsets = [o for o, _ in first]
        joins = order(lambda *v: join(offsets, where, rows, replicas, v), *[b for _, b in first])
        sum_packed.step()
        layer_out = order(
            lambda x, keep, got, other: (
                x + keep[0].astype(F32) + got[0].astype(F32) + other.astype(F32)
            ).astype(BF16),
            residual,
            *to_out.terms(),
        )
        all_packed = RingGather(ring_down, order, place, sum_packed.total())
        all_packed.step()
        rest = all_units.finish()[5:]
        late = [o for o, _ in rest]
        joins = order(
            lambda a, b, *v: join(late, where, rows, replicas, v, a, b), *joins, *[b for _, b in rest]
        )
        out_gate, out_up = joined(*joins, rows)
        out_down = assemble(all_down.finish(), place, F32).reshape(ff, width)
        packed = assemble(all_packed.finish(), place, F32)
        values = packed[:, chunk, : VECTOR // replicas].reshape(VECTOR)
        packed = packed[:, :chunk].reshape(2, rows, width + KVD)
        sizes = (rows, rows, rows, KVD // 4, KVD // 4)
        g_one, g_bq, g_two, g_bk, g_bv = [values[s : s + n] for s, n in zip(SPOTS, sizes)]
        return (
            layer_out[None],
            in_grad[None],
            g_one,
            packed[0, :, :width],
            g_bq,
            packed[0, :, width:],
            g_bk,
            packed[1, :, width:],
            g_bv,
            packed[1, :, :width],
            g_two,
            out_gate,
            out_up,
            out_down,
        )

    return body


def solution(mesh):
    tokens = P("replica", "group", None)
    matrix = P("group", None)
    vector = P("group")
    weights = (
        vector,
        matrix,
        vector,
        matrix,
        vector,
        matrix,
        vector,
        matrix,
        vector,
        matrix,
        matrix,
        matrix,
    )
    in_specs = (tokens, tokens, P("replica", "group"), P("replica", None)) + weights
    out_specs = (tokens, tokens) + weights
    body = make_body(mesh.shape["replica"])
    return jax.shard_map(body, mesh=mesh, in_specs=in_specs, out_specs=out_specs, check_vma=False)
```

```python
import functools

import jax
import jax.numpy as jnp
from jax import lax
from jax.experimental import pallas as pl
from jax.experimental.pallas import tpu as pltpu
from jax.sharding import PartitionSpec as P

HEADS = 14
KV_HEADS = 2
HEAD_DIM = 64
GROUPS = HEADS // KV_HEADS
KVD = KV_HEADS * HEAD_DIM
FACTOR = 1.0 / HEAD_DIM**0.5
LANES = 128
HIDDEN_KEY = -1e30
SPOTS = (0, 256, 512, 768, 896)
VECTOR = 1024

EPSILON = 1e-06
THETA = 1000000.0

F32 = jnp.float32
BF16 = jnp.bfloat16

ANY = pl.BlockSpec(memory_space=pl.ANY)
VMEM = pl.BlockSpec(memory_space=pltpu.VMEM)
SMEM = pl.BlockSpec(memory_space=pltpu.SMEM)
LIMIT = pltpu.CompilerParams(vmem_limit_bytes=14 * 1024 * 1024)


def rms_scale(values):
    return lax.rsqrt(jnp.mean(values * values, axis=-1, keepdims=True) + EPSILON)


def mm(left, right):
    return jnp.dot(left, right, preferred_element_type=F32)


def mm_nt(left, right):
    return lax.dot_general(left, right, (((1,), (1,)), ((), ())), preferred_element_type=F32)


def mm_tn(left, right):
    return lax.dot_general(left, right, (((0,), (0,)), ((), ())), preferred_element_type=F32)


def pick(stack, index, axis=0):
    return lax.dynamic_index_in_dim(
        stack, index, axis, keepdims=False, allow_negative_indices=False
    )


def cost(flops, moved, special=0):
    return pl.CostEstimate(flops=int(flops), bytes_accessed=int(moved), transcendentals=int(special))


def turn_back(values, sine):
    wide = values.shape[1]
    lane = lax.broadcasted_iota(jnp.int32, values.shape, 1) % HEAD_DIM
    ahead = pltpu.roll(values, wide - HEAD_DIM // 2, 1)
    behind = pltpu.roll(values, HEAD_DIM // 2, 1)
    return jnp.where(lane < HEAD_DIM // 2, ahead, behind) * sine


def split_kernel(where, gate, up, own, near, far_a, far_b, *, chunk, ff, step):
    me, place = where[0], where[1]
    half = gate.shape[0] // chunk
    for j in range(4):
        columns = pl.ds(j * ff, ff)
        for target, out in ((me, own), (me ^ 1, near)):

            @pl.when(target == j)
            def _(out=out, columns=columns):
                @pl.loop(0, gate.shape[0] // step)
                def _(i):
                    rows = pl.ds(pl.multiple_of(i * step, step), step)
                    out[0, rows, :] = gate[rows, columns]
                    out[1, rows, :] = up[rows, columns]

        for k, far in ((2, far_a), (3, far_b)):

            @pl.when((me ^ k) == j)
            def _(far=far, columns=columns):
                rows = pl.ds(pl.multiple_of(lax.rem(place, half) * chunk, 8), chunk)
                far[0] = gate[rows, columns]
                far[1] = up[rows, columns]


def pack_kernel(key, value, *refs):
    out = refs[-1]
    rows = key.shape[0]
    out[0:rows, 0:KVD] = key[...]
    out[0:rows, KVD:] = value[...]
    out[rows:, :] = jnp.zeros((out.shape[0] - rows, 2 * KVD), BF16)
    for i, ref in enumerate(refs[:-1]):
        size = ref.shape[0]
        out[rows + 8 * i : rows + 8 * i + 1, 0:size] = ref[...].reshape(1, size)


def pack(key, value, *vectors):
    rows = key.shape[0]
    return pl.pallas_call(
        pack_kernel,
        out_shape=jax.ShapeDtypeStruct((rows + 8 * len(vectors), 2 * KVD), BF16),
        in_specs=[VMEM] * (2 + len(vectors)),
        out_specs=VMEM,
        cost_estimate=cost(0, 8 * rows * KVD),
        name="pack",
    )(key, value, *vectors)


def split(where, gate, up, replicas):
    rows = gate.shape[0]
    ff = gate.shape[1] // 4
    chunk = 2 * rows // replicas
    if chunk % 8:
        me, place = where[0], where[1]
        both = jnp.stack([gate, up]).reshape(2, rows, 4, ff).transpose(2, 0, 1, 3)
        far = [pick(both, me ^ k).reshape(2, replicas // 2, chunk, ff) for k in (2, 3)]
        spot = place % (replicas // 2)
        return pick(both, me), pick(both, me ^ 1), pick(far[0], spot, 1), pick(far[1], spot, 1)
    shape = jax.ShapeDtypeStruct((2, rows, ff), BF16)
    piece = jax.ShapeDtypeStruct((2, chunk, ff), BF16)
    return pl.pallas_call(
        functools.partial(split_kernel, chunk=chunk, ff=ff, step=32),
        out_shape=(shape, shape, piece, piece),
        in_specs=[SMEM, VMEM, VMEM],
        out_specs=(VMEM,) * 4,
        compiler_params=LIMIT,
        cost_estimate=cost(0, 16 * rows * ff),
        name="split",
    )(where, gate, up)


def arrange_kernel(where, *refs, moves):
    out, sems = refs[-2], refs[-1]
    copies = []
    for i, (source, take, put) in enumerate(moves):
        copy = pltpu.make_async_copy(refs[source].at[take(where)], out.at[put(where)], sems.at[i])
        copy.start()
        copies.append(copy)
    for copy in copies:
        copy.wait()


def arrange(where, sources, shape, moves):
    size = 1
    for extent in shape:
        size *= extent
    return pl.pallas_call(
        functools.partial(arrange_kernel, moves=moves),
        out_shape=jax.ShapeDtypeStruct(shape, BF16),
        in_specs=[SMEM] + [ANY] * len(sources),
        out_specs=VMEM,
        scratch_shapes=[pltpu.SemaphoreType.DMA((len(moves),))],
        compiler_params=LIMIT,
        cost_estimate=cost(0, 4 * size),
        name="arrange",
    )(where, *sources)


def join_kernel(where, *refs, offsets, half, ff):
    count = len(offsets)
    pieces = refs[:count]
    gate, up, slab, sems = refs[-4:]
    me = where[0]
    chunk = pieces[0].shape[1]

    def spot(i):
        return lax.rem(where[1] + offsets[i] + 2 * half, 2 * half)

    def copy(i, out):
        row = pl.multiple_of(lax.rem(spot(i), half) * chunk, 8)
        return pltpu.make_async_copy(slab.at[i % 2], out.at[pl.ds(row, chunk), :], sems.at[i])

    for i in range(count):
        if i >= 2:
            copy(i - 2, gate).wait()
        for j in range(4):
            slab[i % 2, :, pl.ds(j * ff, ff)] = pieces[i][me ^ j].astype(F32)

        @pl.when(spot(i) < half)
        def _(i=i):
            copy(i, gate).start()

        @pl.when(spot(i) >= half)
        def _(i=i):
            copy(i, up).start()

    for i in range(count - 2, count):
        copy(i, gate).wait()


def join(offsets, where, rows, replicas, values, *before):
    count = len(offsets)
    _, chunk, ff = values[0].shape
    half = replicas // 2
    if chunk % 8:
        got = before[0] if before else jnp.zeros((replicas, chunk, 4, ff), F32)
        for offset, value in zip(offsets, values):
            value = jnp.stack([pick(value, where[0] ^ j) for j in range(4)], axis=1)
            spot = (where[1] + offset) % replicas
            got = lax.dynamic_update_slice(got, value.astype(F32)[None], (spot, 0, 0, 0))
        return got, got
    shape = jax.ShapeDtypeStruct((rows, 4 * ff), F32)
    return pl.pallas_call(
        functools.partial(join_kernel, offsets=offsets, half=half, ff=ff),
        out_shape=(shape, shape),
        in_specs=[SMEM] + [VMEM] * count + [ANY] * len(before),
        out_specs=(ANY, ANY),
        scratch_shapes=[pltpu.VMEM((2, chunk, 4 * ff), F32), pltpu.SemaphoreType.DMA((count,))],
        input_output_aliases={1 + count: 0, 2 + count: 1} if before else {},
        compiler_params=LIMIT,
        cost_estimate=cost(0, 48 * rows * ff * count // replicas),
        name="join",
    )(where, *values, *before)


def joined(gate, up, rows):
    if gate.ndim == 2:
        return gate, up
    gate = gate.reshape(2, rows, -1)
    return gate[0], gate[1]


def load_rows(where, blocks, out, sems, first):
    rows = blocks[0].shape[0]
    copies = []
    for k, block in enumerate(blocks):
        row = pl.multiple_of((where[0] ^ k) * rows, 8)
        copies.append(pltpu.make_async_copy(block, out.at[pl.ds(row, rows), :], sems.at[first + k]))
        copies[-1].start()
    return copies


def order_vec(me, blocks, row, size, out, to):
    parts = [b[row : row + 1, 0:size].astype(F32) for b in blocks]
    odd = jnp.full(parts[0].shape, me % 2, jnp.int32) == 1
    far = jnp.full(parts[0].shape, me // 2, jnp.int32) == 1
    for j in range(4):
        same = jnp.where(odd, parts[j ^ 1], parts[j])
        other = jnp.where(odd, parts[j ^ 3], parts[j ^ 2])
        out[pl.ds(to, 1), pl.ds(j * size, size)] = jnp.where(far, other, same)


def four(own, other, two):
    return (own, other.at[0], two, other.at[1])


def kv_kernel(where, hidden, cosine, sine, own, other, two, kv, normed_out, vectors, weights):
    blocks = four(own, other, two)
    width = hidden.shape[1]
    rows = width // 4
    vectors[...] = jnp.zeros_like(vectors)
    for i, size in enumerate((rows, rows, rows, KVD // 4, KVD // 4)):
        order_vec(where[0], blocks, rows + 8 * i, size, vectors, i)
    for k, block in enumerate(blocks):
        row = pl.multiple_of((where[0] ^ k) * rows, 8)
        weights[pl.ds(row, rows), :] = block[0:rows, :]
    x = hidden[...].astype(F32)
    normed = (x * rms_scale(x) * vectors[0:1, 0:width]).astype(BF16)
    normed_out[...] = normed
    both = mm(normed, weights[...])
    key = both[:, :KVD] + vectors[3:4, 0:KVD]
    key = key * cosine[...] + turn_back(key, sine[...])
    kv[:, 0:KVD] = key.astype(BF16)
    kv[:, KVD : 2 * KVD] = (both[:, KVD:] + vectors[4:5, 0:KVD]).astype(BF16)


def project_kv(where, hidden, cosine, sine, *blocks):
    part, width = hidden.shape
    return pl.pallas_call(
        kv_kernel,
        out_shape=(
            jax.ShapeDtypeStruct((part, 2 * KVD), BF16),
            jax.ShapeDtypeStruct((part, width), BF16),
            jax.ShapeDtypeStruct((8, width), F32),
            jax.ShapeDtypeStruct((width, 2 * KVD), BF16),
        ),
        in_specs=[SMEM] + [VMEM] * 6,
        out_specs=(VMEM,) * 4,
        compiler_params=LIMIT,
        cost_estimate=cost(4 * part * width * KVD, 4 * part * width),
        name="kv",
    )(where, hidden, cosine, sine, *blocks)


def heads_forward(heads, query, kv, mask, attended, logs, first):
    lane = lax.broadcasted_iota(jnp.int32, logs.shape, 1)
    for h in heads:
        g = h // GROUPS
        keys = kv[:, pl.ds(g * HEAD_DIM, HEAD_DIM)]
        values = kv[:, pl.ds(KVD + g * HEAD_DIM, HEAD_DIM)]
        lanes = pl.ds(h * HEAD_DIM, HEAD_DIM)
        scores = mm_nt(query[:, lanes], keys) + mask[...]
        top = jnp.max(scores, axis=-1, keepdims=True)
        raised = jnp.exp(scores - top)
        total = jnp.sum(raised, axis=-1, keepdims=True)
        logs = jnp.where(lane == h, top + jnp.log(total), logs)
        probs = (raised * (1.0 / total)).astype(BF16)
        attended[:, pl.ds(h * HEAD_DIM - first, HEAD_DIM)] = mm(probs, values).astype(BF16)
    return logs


def attend_kernel(where, normed_one, vectors, cosine, sine, own_ids, key_ids, *refs, heads):
    blocks, wq = four(*refs[0:3]), four(*refs[3:6])
    query, attended, lse, w_q, kv, mask, sems = refs[6:]
    part, width = normed_one.shape
    copies = load_rows(where, wq, w_q, sems, 0)
    for k, block in enumerate(blocks):
        kv[pl.ds(k * part, part), :] = block[...]
    square = (part, part)
    diagonal = lax.broadcasted_iota(jnp.int32, square, 0) == lax.broadcasted_iota(jnp.int32, square, 1)
    own = jnp.where(diagonal, own_ids[...].astype(F32), 0.0)
    own = jnp.sum(own, axis=1, keepdims=True)
    mask[...] = jnp.where(key_ids[...].astype(F32) <= own, 0.0, HIDDEN_KEY)
    cos, sin = cosine[...], sine[...]
    for copy in copies:
        copy.wait()
    for first in range(0, width, LANES):
        lanes = pl.ds(first, LANES)
        value = mm(normed_one[...], w_q[:, lanes]) + vectors[1:2, lanes]
        value = value * cos + turn_back(value, sin)
        query[:, lanes] = (value.astype(BF16).astype(F32) * FACTOR).astype(BF16)
    logs = jnp.zeros((part, LANES), F32)
    lse[...] = heads_forward(heads, query, kv, mask, attended, logs, 0)


def attend(heads, where, normed_one, vectors, cosine, sine, own_ids, key_ids, kv, wq):
    part, width = normed_one.shape
    length = key_ids.shape[1]
    work = part * length * len(heads)
    return pl.pallas_call(
        functools.partial(attend_kernel, heads=heads),
        out_shape=(
            jax.ShapeDtypeStruct((part, width), BF16),
            jax.ShapeDtypeStruct((part, len(heads) * HEAD_DIM), BF16),
            jax.ShapeDtypeStruct((part, LANES), F32),
            jax.ShapeDtypeStruct((width, width), BF16),
            jax.ShapeDtypeStruct((length, 2 * KVD), BF16),
            jax.ShapeDtypeStruct((part, length), F32),
        ),
        in_specs=[SMEM] + [VMEM] * 9 + [ANY] * 3,
        out_specs=(VMEM,) * 6,
        scratch_shapes=[pltpu.SemaphoreType.DMA((4,))],
        compiler_params=LIMIT,
        cost_estimate=cost(4 * work * HEAD_DIM + 2 * part * width * width, 8 * part * width, work),
        name="attend",
    )(where, normed_one, vectors, cosine, sine, own_ids, key_ids, *kv, *wq)


def residual_kernel(where, hidden, vectors, mask, query, kv, before, lse_before, *refs, heads):
    wo = four(*refs[0:3])
    attended, lse, residual, normed, w_o, sems = refs[3:]
    first = before.shape[1]
    late = load_rows(where, wo, w_o, sems, 0)
    attended[:, 0:first] = before[...]
    lse[...] = heads_forward(heads, query, kv, mask, attended, lse_before[...], 0)
    for copy in late:
        copy.wait()
    value = hidden[...].astype(F32) + mm(attended[...], w_o[...])
    residual[...] = value
    normed[...] = (value * rms_scale(value) * vectors[2:3, :]).astype(BF16)


def attend_rest(heads, where, hidden, vectors, mask, query, kv, before, lse, wo):
    part, width = hidden.shape
    work = part * kv.shape[0] * len(heads)
    tokens = jax.ShapeDtypeStruct((part, width), BF16)
    return pl.pallas_call(
        functools.partial(residual_kernel, heads=heads),
        out_shape=(
            tokens,
            jax.ShapeDtypeStruct((part, LANES), F32),
            jax.ShapeDtypeStruct((part, width), F32),
            tokens,
            jax.ShapeDtypeStruct((width, width), BF16),
        ),
        in_specs=[SMEM] + [VMEM] * 7 + [ANY] * 3,
        out_specs=(VMEM,) * 5,
        scratch_shapes=[pltpu.SemaphoreType.DMA((4,))],
        compiler_params=LIMIT,
        cost_estimate=cost(4 * work * HEAD_DIM + 2 * part * width * width, 8 * part * width, work),
        name="attend_rest",
    )(where, hidden, vectors, mask, query, kv, before, lse, *wo)


def units_kernel(one, two, grad_hidden, weights, tokens, hidden, dgate, dup):
    part = one.shape[0]
    tokens[0:part, :] = one[...]
    tokens[part:, :] = two[...]
    value = tokens[...]
    gate = mm(value, weights[0])
    up = mm(value, weights[1])
    back = grad_hidden[...]
    sigma = jax.nn.sigmoid(gate)
    active = gate * sigma
    hidden[...] = (active * up).astype(BF16)
    dup[...] = (back * active).astype(BF16)
    dgate[...] = (back * up * sigma * (1.0 + gate * (1.0 - sigma))).astype(BF16)


def back_units_kernel(dy_one, dy_two, w_down, out, dy, *, slot):
    part = dy_one.shape[0]
    dy[0:part, :] = dy_one[...]
    dy[part:, :] = dy_two[slot]
    out[...] = mm_nt(dy[...], w_down[...])


def back_units(slot, dy_one, dy_two, w_down):
    part, width = dy_one.shape
    ff = w_down.shape[0]
    return pl.pallas_call(
        functools.partial(back_units_kernel, slot=slot),
        out_shape=(
            jax.ShapeDtypeStruct((2 * part, ff), F32),
            jax.ShapeDtypeStruct((2 * part, width), BF16),
        ),
        in_specs=[VMEM] * 3,
        out_specs=(VMEM, VMEM),
        compiler_params=LIMIT,
        cost_estimate=cost(4 * part * width * ff, 2 * width * ff + 8 * part * ff),
        name="back_units",
    )(dy_one, dy_two, w_down)


def units(one, two, grad_hidden, weights):
    part, width = one.shape
    ff = weights.shape[2]
    shape = jax.ShapeDtypeStruct((2 * part, ff), BF16)
    return pl.pallas_call(
        units_kernel,
        out_shape=(jax.ShapeDtypeStruct((2 * part, width), BF16), shape, shape, shape),
        in_specs=[VMEM] * 4,
        out_specs=(VMEM,) * 4,
        compiler_params=LIMIT,
        cost_estimate=cost(8 * part * width * ff, 6 * width * ff, 2 * part * ff),
        name="units",
    )(one, two, grad_hidden, weights)


def weight_kernel(*refs, count):
    left_a, left_b = refs[0:2]
    rights = refs[2 : 2 + 2 * count]
    outs = refs[2 + 2 * count :]
    for i, out in enumerate(outs):
        total = mm_tn(left_a[...], rights[2 * i][...]) + mm_tn(left_b[...], rights[2 * i + 1][...])
        out[...] = total.astype(BF16)


def weight_grads(left, rights):
    tall = left[0].shape[1]
    wide = rights[0][0].shape[1]
    count = len(rights)
    shape = jax.ShapeDtypeStruct((tall, wide), BF16)
    return pl.pallas_call(
        functools.partial(weight_kernel, count=count),
        out_shape=(shape,) * count,
        in_specs=[VMEM] * (2 + 2 * count),
        out_specs=(VMEM,) * count,
        compiler_params=LIMIT,
        cost_estimate=cost(4 * count * left[0].shape[0] * tall * wide, 6 * count * tall * wide),
        name="weight_grads",
    )(*left, *[r for pair in rights for r in pair])


def partial_kernel(*refs, mats, transposed):
    lefts = refs[: 2 * mats]
    weights, keep, send = refs[2 * mats :]
    part = keep.shape[1]
    for chip in range(2):
        if transposed:
            total = mm_nt(lefts[2 * chip][...], weights[0])
            total += mm_nt(lefts[2 * chip + 1][...], weights[1])
        else:
            total = mm(lefts[chip][...], weights[...])
        keep[chip] = total[:part].astype(BF16)
        send[chip] = total[part:].astype(BF16)


def partial_sums(lefts, weights, width, transposed):
    rows = lefts[0].shape[0]
    mats = len(lefts) // 2
    shape = jax.ShapeDtypeStruct((2, rows // 2, width), BF16)
    return pl.pallas_call(
        functools.partial(partial_kernel, mats=mats, transposed=transposed),
        out_shape=(shape, shape),
        in_specs=[VMEM] * (2 * mats + 1),
        out_specs=(VMEM, VMEM),
        compiler_params=LIMIT,
        cost_estimate=cost(4 * mats * rows * lefts[0].shape[1] * width, 8 * mats * rows * width),
        name="partial_sums",
    )(*lefts, weights)


def branch_kernel(own, near, far, residual, dy, vectors, w_o, dresidual, dbranch, dattended, gain):
    value = residual[...]
    scale = rms_scale(value)
    unit = value * scale
    grad = own[0].astype(F32) + near[0].astype(F32) + far[...].astype(F32)
    gain[...] = jnp.sum(grad * unit, axis=0, keepdims=True)
    inner = grad * vectors[2:3, :]
    total = scale * (inner - unit * jnp.mean(inner * unit, axis=-1, keepdims=True))
    total = dy[...].astype(F32) + total
    dresidual[...] = total
    low = total.astype(BF16)
    dbranch[...] = low
    dattended[...] = mm_nt(low, w_o[...]).astype(BF16)


def branch_back(own, near, far, residual, dy, vectors, w_o):
    part, width = residual.shape
    tokens = jax.ShapeDtypeStruct((part, width), BF16)
    return pl.pallas_call(
        branch_kernel,
        out_shape=(
            jax.ShapeDtypeStruct((part, width), F32),
            tokens,
            tokens,
            jax.ShapeDtypeStruct((1, width), F32),
        ),
        in_specs=[VMEM] * 7,
        out_specs=(VMEM,) * 4,
        compiler_params=LIMIT,
        cost_estimate=cost(2 * part * width * width, 20 * part * width),
        name="branch_back",
    )(own, near, far, residual, dy, vectors, w_o)


def back_kernel(mask, query, kv, lse, dattended, *refs, heads, first):
    dquery, dkv = refs[-2:]
    logs = lse[...]
    lane = lax.broadcasted_iota(jnp.int32, logs.shape, 1)
    if len(refs) > 2:
        dkv[...] = refs[0][...]
    else:
        dkv[...] = jnp.zeros_like(dkv)
    for h in heads:
        g = h // GROUPS
        k_lanes = pl.ds(g * HEAD_DIM, HEAD_DIM)
        v_lanes = pl.ds(KVD + g * HEAD_DIM, HEAD_DIM)
        lanes = pl.ds(h * HEAD_DIM, HEAD_DIM)
        q, do = query[:, lanes], dattended[:, lanes]
        keys, values = kv[:, k_lanes], kv[:, v_lanes]
        log = jnp.sum(jnp.where(lane == h, logs, 0.0), axis=-1, keepdims=True)
        probs = jnp.exp(mm_nt(q, keys) + mask[...] - log)
        dprobs = mm_nt(do, values)
        total = jnp.sum(probs * dprobs, axis=-1, keepdims=True)
        dscores = (probs * (dprobs - total)).astype(BF16)
        dquery[:, pl.ds(h * HEAD_DIM - first, HEAD_DIM)] = mm(dscores, keys) * FACTOR
        dkv[:, k_lanes] += mm_tn(dscores, q)
        dkv[:, v_lanes] += mm_tn(probs.astype(BF16), do)


def attend_back(heads, mask, query, kv, lse, dattended, *before):
    part = query.shape[0]
    length = kv.shape[0]
    first = heads[0] * HEAD_DIM
    work = part * length * len(heads)
    return pl.pallas_call(
        functools.partial(back_kernel, heads=heads, first=first),
        out_shape=(
            jax.ShapeDtypeStruct((part, len(heads) * HEAD_DIM), F32),
            jax.ShapeDtypeStruct((length, 2 * KVD), F32),
        ),
        in_specs=[VMEM] * (5 + len(before)),
        out_specs=(VMEM, VMEM),
        compiler_params=LIMIT,
        cost_estimate=cost(10 * work * HEAD_DIM, 8 * length * KVD, work),
        name="attend_back",
    )(mask, query, kv, lse, dattended, *before)


def deal(me, weights, per, keep, send):
    count = keep.shape[1]
    for k in range(4):
        out = (keep, send)[k % 2]
        for r in range(count):
            out[k // 2, r, 0:per, :] = weights[me ^ k, pl.ds(r * per, per), :].astype(BF16)


def out_grads_kernel(where, attended, dbranch, keep, send, weights):
    rows, width = weights.shape[1:]
    per = rows // keep.shape[1]
    weights[...] = mm_tn(attended[...], dbranch[...]).reshape(4, rows, width)
    if per < keep.shape[2]:
        keep[...] = jnp.zeros(keep.shape, BF16)
        send[...] = jnp.zeros(send.shape, BF16)
    deal(where[0], weights, per, keep, send)


def out_grads(replicas, where, attended, dbranch):
    part, width = attended.shape
    rows = width // 4
    tall = padded(rows, replicas)
    shape = jax.ShapeDtypeStruct((2, replicas, tall, width), BF16)
    return pl.pallas_call(
        out_grads_kernel,
        out_shape=(shape, shape),
        in_specs=[SMEM] + [VMEM] * 2,
        out_specs=(VMEM, VMEM),
        scratch_shapes=[pltpu.VMEM((4, rows, width), F32)],
        compiler_params=LIMIT,
        cost_estimate=cost(2 * part * width * width, 8 * width * width),
        name="out_grads",
    )(where, attended, dbranch)


def padded(rows, replicas):
    return -(-(rows // replicas + 1) // 8) * 8


def grads_kernel(where, hidden, normed, dresidual, dq_a, dq_b, own, near, far, cosine, sine, vectors, gain_two, w_q, w_kv, in_grad, keep, send, dpre, weights, values):
    me = where[0]
    part, width = hidden.shape
    rows = width // 4
    total_wide = width + 2 * KVD
    cos, sin = cosine[...], sine[...]
    split_at = dq_a.shape[1]
    grad = own[0].astype(F32) + near[0].astype(F32) + far[...].astype(F32)
    for first in range(0, width + KVD, LANES):
        if first < split_at:
            value = dq_a[:, pl.ds(first, LANES)]
        elif first < width:
            value = dq_b[:, pl.ds(first - split_at, LANES)]
        else:
            value = grad[:, :KVD]
        dpre[:, pl.ds(first, LANES)] = (value * cos - turn_back(value, sin)).astype(BF16)
    dpre[:, pl.ds(width + KVD, KVD)] = grad[:, KVD:].astype(BF16)
    bias = jnp.sum(dpre[...].astype(F32), axis=0, keepdims=True)

    x = hidden[...].astype(F32)
    scale = rms_scale(x)
    unit = x * scale
    back = mm_nt(dpre[:, 0:width], w_q[...]) + mm_nt(dpre[:, pl.ds(width, 2 * KVD)], w_kv[...])
    gain_one = jnp.sum(back * unit, axis=0, keepdims=True)
    inner = back * vectors[0:1, :]
    total = scale * (inner - unit * jnp.mean(inner * unit, axis=-1, keepdims=True))
    in_grad[...] = (dresidual[...] + total).astype(BF16)

    cut = width + KVD
    weights[...] = mm_tn(normed[...], dpre[...]).reshape(4, rows, total_wide)
    sizes = (rows, rows, rows, KVD // 4, KVD // 4)
    sources = (gain_one, bias[:, :width], gain_two[...], bias[:, width:cut], bias[:, cut:])
    values[...] = jnp.zeros_like(values)
    for j in range(4):
        for spot, size, source in zip(SPOTS, sizes, sources):
            values[j, 0:1, pl.ds(spot, size)] = source[:, j * size : (j + 1) * size]
    count = keep.shape[1]
    per = rows // count
    each = VECTOR // count
    keep[...] = jnp.zeros(keep.shape, BF16)
    send[...] = jnp.zeros(send.shape, BF16)
    deal(me, weights, per, keep, send)
    for k in range(4):
        out = (keep, send)[k % 2]
        for r in range(count):
            line = values[me ^ k, 0:1, pl.ds(r * each, each)]
            out[k // 2, r, per : per + 1, 0:each] = line.astype(BF16)


def attention_grads(replicas, where, hidden, *args):
    part, width = hidden.shape
    rows = width // 4
    wide = width + 2 * KVD
    shape = jax.ShapeDtypeStruct((2, replicas, padded(rows, replicas), wide), BF16)
    return pl.pallas_call(
        grads_kernel,
        out_shape=(jax.ShapeDtypeStruct((part, width), BF16), shape, shape),
        in_specs=[SMEM] + [VMEM] * 14,
        out_specs=(VMEM,) * 3,
        scratch_shapes=[
            pltpu.VMEM((part, wide), BF16),
            pltpu.VMEM((4, rows, wide), F32),
            pltpu.VMEM((4, 8, VECTOR), F32),
        ],
        compiler_params=LIMIT,
        cost_estimate=cost(8 * part * width * width, 20 * width * width),
        name="attention_grads",
    )(where, hidden, *args)


def split_grads_kernel(where, *refs, offsets, per):
    count = len(offsets)
    pieces = refs[:count]
    query, key, value, out, vectors, held = refs[count:]
    width = query.shape[1]
    each = VECTOR // count
    for offset, piece in zip(offsets, pieces):
        held[lax.rem(where[1] + offset + count, count)] = piece[...].astype(F32)
    for s in range(count):
        rows = pl.ds(s * per, per)
        query[rows, :] = held[s, 0:per, 0:width]
        key[rows, :] = held[s, 0:per, width : width + KVD]
        value[rows, :] = held[s, 0:per, width + KVD : width + 2 * KVD]
        out[rows, :] = held[s, 0:per, width + 2 * KVD :]
        vectors[0:1, pl.ds(s * each, each)] = held[s, per : per + 1, 0:each]


def split_grads(found, where, rows, width):
    offsets = [offset for offset, _ in found]
    count = len(found)
    tall, wide = found[0][1].shape
    shape = lambda columns: jax.ShapeDtypeStruct((rows, columns), F32)
    return pl.pallas_call(
        functools.partial(split_grads_kernel, offsets=offsets, per=rows // count),
        out_shape=(
            shape(width),
            shape(KVD),
            shape(KVD),
            shape(width),
            jax.ShapeDtypeStruct((1, VECTOR), F32),
        ),
        in_specs=[SMEM] + [VMEM] * count,
        out_specs=(VMEM,) * 5,
        scratch_shapes=[pltpu.VMEM((count, tall, wide), F32)],
        compiler_params=LIMIT,
        cost_estimate=cost(0, 6 * rows * wide),
        name="split_grads",
    )(where, *[value for _, value in found])


def stack_rows_kernel(where, *refs, offsets):
    count = len(offsets)
    out = refs[count]
    rows = refs[0].shape[0]
    for offset, piece in zip(offsets, refs[:count]):
        row = pl.multiple_of(lax.rem(where[1] + offset + count, count) * rows, 8)
        out[pl.ds(row, rows), :] = piece[...].astype(F32)


def stack_rows(found, where, place):
    offsets = [offset for offset, _ in found]
    count = len(found)
    rows, width = found[0][1].shape
    if rows % 8:
        return assemble(found, place, F32).reshape(count * rows, width)
    return pl.pallas_call(
        functools.partial(stack_rows_kernel, offsets=offsets),
        out_shape=jax.ShapeDtypeStruct((count * rows, width), F32),
        in_specs=[SMEM] + [VMEM] * count,
        out_specs=VMEM,
        compiler_params=LIMIT,
        cost_estimate=cost(0, 6 * count * rows * width),
        name="stack_rows",
    )(where, *[value for _, value in found])


class Order:
    def __init__(self):
        self.last = None

    def __call__(self, run, *values):
        values = self.hold(*values)
        found = run(*values)
        self.last = tuple(found) if isinstance(found, (tuple, list)) else (found,)
        return found

    def wait(self, *values):
        self.last = (*(self.last or ()), *values)

    def hold(self, *values):
        if self.last is None:
            return values
        return lax.optimization_barrier((*values, *self.last))[: len(values)]


class Ring:
    def __init__(self, count, lead):
        self.count = count
        self.lead = lead
        self.order = [0, 2, 4, 6, 7, 5, 3, 1] if count == 8 else list(range(count))
        self.plus = count // 2
        self.minus = count - 1 - self.plus

    def place(self):
        replica = lax.axis_index("replica")
        if self.count == 8:
            line, side = replica // 2, replica % 2
            return jnp.where(side == 0, line, 7 - line)
        return replica

    def replica(self, place):
        if self.count == 8:
            return jnp.where(place < 4, 2 * place, 15 - 2 * place)
        return place

    def move(self, value, step):
        n = self.count
        pairs = [(self.order[p], self.order[(p + step) % n]) for p in range(n)]
        return lax.ppermute(value, "replica", pairs)

    def both(self):
        return ((self.plus, self.lead), (self.minus, -self.lead))


class RingSum:
    def __init__(self, ring, order, take, *arrays):
        self.ring, self.order, self.take, self.arrays = ring, order, take, arrays
        self.left = [hops for hops, _ in ring.both()]
        self.arrived = []
        self.moving = self._send(None)

    def _send(self, moving):
        ring = self.ring
        active = [i for i in range(2) if self.left[i] > 0]

        def run(*values):
            parts = []
            for n, i in enumerate(active):
                step = ring.both()[i][1]
                part = self.take(step * self.left[i], *values[: len(self.arrays)])
                if moving is not None:
                    got = values[len(self.arrays) + n]
                    part = (part.astype(F32) + got.astype(F32)).astype(BF16)
                parts.append(part)
            return parts

        got = [] if moving is None else [moving[i] for i in active]
        parts = self.order(run, *self.arrays, *got)
        sent = [None, None]
        for part, i in zip(parts, active):
            sent[i] = ring.move(part, ring.both()[i][1])
            self.left[i] -= 1
            if self.left[i] == 0:
                self.arrived.append(sent[i])
        return sent

    def step(self):
        self.moving = self._send(self.moving)

    def total(self):
        while max(self.left) > 0:
            self.step()
        count = len(self.arrays)

        def run(*values):
            own = self.take(0, *values[:count]).astype(F32)
            return sum((v.astype(F32) for v in values[count:]), own).astype(BF16)

        return self.order(run, *self.arrays, *self.arrived)


class RingGather:
    def __init__(self, ring, order, own):
        self.ring, self.order = ring, order
        self.found = [(0, own)]
        self.hop = 0
        self.moving = [own, own]
        self._send()

    def _send(self):
        self.hop += 1
        for i, (hops, step) in enumerate(self.ring.both()):
            if self.hop <= hops:
                self.moving[i] = self.ring.move(self.moving[i], step)
                self.found.append((-step * self.hop, self.moving[i]))

    def step(self):
        if self.hop < self.ring.plus:
            self.moving = list(self.order(lambda *v: v, *self.moving))
            self._send()

    def take(self, first, last):
        found = self.found[first:last]
        values = self.order(lambda *v: v, *[value for _, value in found])
        self.found[first:last] = [(offset, value) for (offset, _), value in zip(found, values)]

    def finish(self):
        while self.hop < self.ring.plus:
            self.step()
        return self.found


class Share:
    def __init__(self, ring, order, own):
        self.ring, self.order = ring, order
        self.found = [(0, (0, 1), own)]
        self.hop = 0
        self.moving = [own, own]
        self._send()

    def _send(self):
        self.hop += 1
        for i, step in enumerate((1, -1)):
            halves = (0, 1)
            if self.hop == self.ring.count // 4:
                halves = (i,)
                self.moving[i] = self.moving[i][:, i : i + 1]
            self.moving[i] = self.ring.move(self.moving[i], step)
            self.found.append((-step * self.hop, halves, self.moving[i]))

    def step(self):
        self.moving = list(self.order(lambda *v: v, *self.moving))
        self._send()


def assemble(found, place, dtype):
    block = found[0][1]
    out = jnp.zeros((len(found),) + block.shape, dtype)
    for offset, value in found:
        start = ((place + offset) % len(found),) + (0,) * block.ndim
        out = lax.dynamic_update_slice(out, value.astype(dtype)[None], start)
    return out


def swap(value, mask):
    return lax.ppermute(value, "group", [(j, j ^ mask) for j in range(4)])


def spread(own):
    one = swap(own, 1)
    two = swap(own, 2)
    return [own, one, two, swap(two, 1)]


class Spread:
    def __init__(self, own):
        self.own, self.two = own, swap(own, 2)

    def step(self, order):
        self.other = swap(order(lambda *v: jnp.stack(v), self.own, self.two), 1)

    def parts(self):
        return self.own, self.other, self.two


class Collect:
    def __init__(self, order, keep, send):
        self.order, self.keep, self.got = order, keep, swap(send, 1)

    def step(self):
        def run(keep, got):
            return (keep[1].astype(F32) + got[1].astype(F32)).astype(BF16)

        self.other = swap(self.order(run, self.keep, self.got), 2)

    def terms(self):
        return self.keep, self.got, self.other


def after(value, *others):
    return lax.optimization_barrier((value,) + others)[0]


FIRST_HEADS = range(0, 8)
OTHER_HEADS = range(8, HEADS)


def make_body(replicas):
    ring_up = Ring(replicas, 1)
    ring_down = Ring(replicas, -1)

    def body(
        hidden_in,
        out_grad,
        positions,
        block_ids,
        gain_one,
        w_query,
        b_query,
        w_key,
        b_key,
        w_value,
        b_value,
        w_out,
        gain_two,
        w_gate,
        w_up,
        w_down,
    ):
        _, part, width = hidden_in.shape
        length = block_ids.shape[1]
        rows = w_gate.shape[0]
        ff = w_down.shape[0]
        half = replicas // 2
        chunk = 2 * rows // replicas
        me = lax.axis_index("group")
        place = ring_up.place()
        where = jnp.stack([me, place])
        order = Order()
        x_value, dy_own = hidden_in[0], out_grad[0]

        packed = order(pack, w_key, w_value, gain_one, b_query, gain_two, b_key, b_value)
        first = Spread(packed)
        wq = Spread(after(w_query, packed))
        offsets = range(-half, half + 1)
        early = [lax.rem(place + (o + replicas), replicas) for o in offsets]
        early += [lax.rem(p, half) for p in early]
        early += [p < half for p in early[: len(offsets)]]
        early += [me ^ k for k in range(4)]
        freqs = THETA ** (-(2.0 * jnp.arange(HEAD_DIM // 2, dtype=F32)) / HEAD_DIM)
        angles = positions[0].astype(F32)[:, None] * jnp.tile(freqs, LANES * 2 // HEAD_DIM)
        sign = jnp.where(jnp.arange(LANES) % HEAD_DIM < HEAD_DIM // 2, -1.0, 1.0)
        ids = block_ids.reshape(4, part)
        own_ids = pick(ids, me).reshape(1, part)
        key_ids = jnp.concatenate([pick(ids, me ^ k) for k in range(4)]).reshape(1, length)
        early += [jnp.cos(angles), jnp.sin(angles) * sign, own_ids, key_ids, where]
        early = lax.optimization_barrier(tuple(early))
        order.wait(*early)
        *early, cosine, sine, own_ids, key_ids, where = early
        count = len(offsets)
        places = dict(zip(offsets, early[:count]))
        rows_at = dict(zip(offsets, early[count : 2 * count]))
        first_half = dict(zip(offsets, early[2 * count : 3 * count]))
        member = early[3 * count :]
        own, near, far_a, far_b = order(
            lambda gate, up: split(where, gate, up, replicas), w_gate, w_up
        )
        first.step(order)
        far_a, far_b = swap(after(far_a, first.two), 2), swap(after(far_b, first.two), 3)
        kv, normed_one, vectors, w_kv = order(
            lambda *v: project_kv(where, *v), x_value, cosine, sine, *first.parts()
        )
        kv = Spread(kv)
        wq.step(order)
        far = order(lambda *v: jnp.stack(v), far_a, far_b)
        pieces = Share(ring_up, order, far)
        kv.step(order)
        wo = Spread(after(w_out, kv.two))
        query, attended, lse, w_q, kv, mask = order(
            lambda *v: attend(FIRST_HEADS, where, *v[:6], v[6:9], v[9:]),
            normed_one,
            vectors,
            cosine,
            sine,
            own_ids,
            key_ids,
            *kv.parts(),
            *wq.parts(),
        )
        pieces.step()
        wo.step(order)
        dy = Spread(after(dy_own, wo.two))
        near = swap(after(near, query), 1)
        attended, lse, residual, normed_two, w_o = order(
            lambda *v: attend_rest(OTHER_HEADS, where, *v[:7], v[7:]),
            x_value,
            vectors,
            mask,
            query,
            kv,
            attended,
            lse,
            *wo.parts(),
        )
        while pieces.hop < replicas // 4:
            pieces.step()
        order.wait(*[value for _, _, value in pieces.found])
        (normed_late,) = order.hold(normed_two)
        one, two = swap(normed_late, 1), swap(normed_late, 2)
        shape = (2, 4, half, chunk, ff)
        moves = []
        for mat in range(2):
            for source in (0, 1):
                moves.append((source, lambda s, m=mat: m, lambda s, m=mat, k=source: (m, s[0] ^ k)))
        for i, (offset, mats, _) in enumerate(pieces.found):
            for slot in range(2):
                for n, mat in enumerate(mats):
                    put = lambda s, d=offset + half, m=mat, k=2 + slot: (m, s[0] ^ k, lax.rem(s[1] + d, half))
                    moves.append((2 + i, lambda s, j=slot, n=n: (j, n), put))
        w_both = order(
            lambda *v: arrange(where, v, shape, moves),
            *[v.reshape(shape[:1] + shape[2:]) for v in (own, near)],
            *[value for _, _, value in pieces.found],
        )
        w_both = w_both.reshape(2, width, ff)

        dy.step(order)
        grad_hidden, dy_a = order(functools.partial(back_units, 0), dy.own, dy.other, w_down)
        tok_a, hid_a, dgate_a, dup_a = order(units, normed_two, one, grad_hidden, w_both)
        three = swap(order.hold(two)[0], 1)
        grad_hidden, dy_b = order(functools.partial(back_units, 1), dy.two, dy.other, w_down)
        tok_b, hid_b, dgate_b, dup_b = order(units, two, three, grad_hidden, w_both)
        grad_gate, grad_up = order(
            lambda *v: weight_grads(v[:2], [v[2:4], v[4:6]]),
            tok_a,
            tok_b,
            dgate_a,
            dgate_b,
            dup_a,
            dup_b,
        )

        def take_units(offset, gate, up):
            row = rows_at[offset]
            return jnp.where(first_half[offset], pick(gate, row, 1), pick(up, row, 1))

        def take_rows(offset, value):
            return pick(value, places[offset])

        shape = (4, half, chunk, ff)
        sum_units = RingSum(
            ring_up, order, take_units, grad_gate.reshape(shape), grad_up.reshape(shape)
        )
        sums = order(
            lambda *v: partial_sums(v[:4], v[4], width, True), dgate_a, dup_a, dgate_b, dup_b, w_both
        )
        to_normed = Collect(order, *sums)
        sum_units.step()
        to_normed.step()
        (grad_down,) = order(lambda *v: weight_grads(v[:2], [v[2:]]), hid_a, hid_b, dy_a, dy_b)
        grad_down = grad_down.reshape(replicas, ff // replicas, width)
        sum_down = RingSum(ring_down, order, take_rows, grad_down)

        dresidual, dbranch, dattended, grad_gain_two = order(
            branch_back, *to_normed.terms(), residual, dy_own, vectors, w_o
        )
        to_w_out = Collect(
            order, *order(lambda *v: out_grads(replicas, where, *v), attended, dbranch)
        )
        args = (mask, query, kv, lse, dattended)
        dq_a, dkv = order(functools.partial(attend_back, FIRST_HEADS), *args)
        sum_units.step()
        sum_down.step()
        to_w_out.step()
        dq_b, dkv = order(functools.partial(attend_back, OTHER_HEADS), *args, dkv)
        dkv = dkv.astype(BF16).reshape(2, 2, part, 2 * KVD)
        to_kv = Collect(order, dkv[:, 0], dkv[:, 1])
        sum_units.step()
        to_kv.step()
        sum_down.step()
        order.wait(to_w_out.other)
        in_grad, *packed = order(
            lambda *v: attention_grads(replicas, where, *v),
            x_value,
            normed_one,
            dresidual,
            dq_a,
            dq_b,
            *to_kv.terms(),
            cosine,
            sine,
            vectors,
            grad_gain_two,
            w_q,
            w_kv,
        )
        to_weights = Collect(order, *packed)
        mine = sum_units.total()
        blocks = [pick(mine, member[0])]
        blocks += [swap(pick(mine, member[k]), k) for k in (1, 2, 3)]
        to_weights.step()
        sum_down.step()
        all_units = RingGather(ring_up, order, order(lambda *v: jnp.stack(v), *blocks))
        sums = order(lambda *v: partial_sums(v[:2], v[2], width, False), hid_a, hid_b, w_down)
        all_down = RingGather(ring_down, order, sum_down.total())
        all_units.step()

        def total(*terms):
            one, two = [
                keep[0].astype(F32) + got[0].astype(F32) + other.astype(F32)
                for keep, got, other in (terms[:3], terms[3:])
            ]
            return jnp.concatenate([one, two], axis=2).astype(BF16)

        packed = order(total, *to_weights.terms(), *to_w_out.terms())
        sum_packed = RingSum(ring_down, order, take_rows, packed)
        all_down.step()
        sum_packed.step()
        all_units.step()
        sum_packed.step()
        all_down.step()
        sum_packed.step()
        all_units.step()
        all_packed = RingGather(ring_down, order, sum_packed.total())
        all_down.step()
        first = all_units.found[:5]
        early = [o for o, _ in first]
        joins = order(lambda *v: join(early, where, rows, replicas, v), *[b for _, b in first])
        all_packed.step()
        rest = all_units.finish()[5:]
        late = [o for o, _ in rest]
        joins = order(
            lambda a, b, *v: join(late, where, rows, replicas, v, a, b), *joins, *[b for _, b in rest]
        )
        down = all_down.finish()
        out_down = order(
            lambda *v: stack_rows([(o, b) for (o, _), b in zip(down, v)], where, place),
            *[b for _, b in down],
        )
        to_out = Collect(order, *order.hold(*sums))
        all_packed.step()
        to_out.step()
        all_packed.step()
        layer_out = order(
            lambda x, keep, got, other: (
                x + keep[0].astype(F32) + got[0].astype(F32) + other.astype(F32)
            ).astype(BF16),
            residual,
            *to_out.terms(),
        )
        out_gate, out_up = joined(*joins, rows)
        found = all_packed.finish()
        g_w_query, g_w_key, g_w_value, g_w_out, values = order(
            lambda *v: split_grads([(o, b) for (o, _), b in zip(found, v)], where, rows, width),
            *[b for _, b in found],
        )
        values = values.reshape(VECTOR)
        sizes = (rows, rows, rows, KVD // 4, KVD // 4)
        g_one, g_bq, g_two, g_bk, g_bv = [values[s : s + n] for s, n in zip(SPOTS, sizes)]
        return (
            layer_out[None],
            in_grad[None],
            g_one,
            g_w_query,
            g_bq,
            g_w_key,
            g_bk,
            g_w_value,
            g_bv,
            g_w_out,
            g_two,
            out_gate,
            out_up,
            out_down,
        )

    return body


def solution(mesh):
    tokens = P("replica", "group", None)
    matrix = P("group", None)
    vector = P("group")
    weights = (
        vector,
        matrix,
        vector,
        matrix,
        vector,
        matrix,
        vector,
        matrix,
        vector,
        matrix,
        matrix,
        matrix,
    )
    in_specs = (tokens, tokens, P("replica", "group"), P("replica", None)) + weights
    out_specs = (tokens, tokens) + weights
    body = make_body(mesh.shape["replica"])
    return jax.shard_map(body, mesh=mesh, in_specs=in_specs, out_specs=out_specs, check_vma=False)
```

```python
import functools

import jax
import jax.numpy as jnp
from jax import lax
from jax.experimental import pallas as pl
from jax.experimental.pallas import tpu as pltpu
from jax.sharding import PartitionSpec as P

HEADS = 14
KV_HEADS = 2
HEAD_DIM = 64
GROUPS = HEADS // KV_HEADS
KVD = KV_HEADS * HEAD_DIM
FACTOR = 1.0 / HEAD_DIM**0.5
LANES = 128
HIDDEN_KEY = -1e30
SPOTS = (0, 256, 512, 768, 896)
VECTOR = 1024

EPSILON = 1e-06
THETA = 1000000.0

F32 = jnp.float32
BF16 = jnp.bfloat16

ANY = pl.BlockSpec(memory_space=pl.ANY)
VMEM = pl.BlockSpec(memory_space=pltpu.VMEM)
SMEM = pl.BlockSpec(memory_space=pltpu.SMEM)
LIMIT = pltpu.CompilerParams(vmem_limit_bytes=14 * 1024 * 1024)


def rms_scale(values):
    return lax.rsqrt(jnp.mean(values * values, axis=-1, keepdims=True) + EPSILON)


def mm(left, right):
    return jnp.dot(left, right, preferred_element_type=F32)


def mm_nt(left, right):
    return lax.dot_general(left, right, (((1,), (1,)), ((), ())), preferred_element_type=F32)


def mm_tn(left, right):
    return lax.dot_general(left, right, (((0,), (0,)), ((), ())), preferred_element_type=F32)


def pick(stack, index, axis=0):
    return lax.dynamic_index_in_dim(
        stack, index, axis, keepdims=False, allow_negative_indices=False
    )


def cost(flops, moved, special=0):
    return pl.CostEstimate(flops=int(flops), bytes_accessed=int(moved), transcendentals=int(special))


def turn_back(values, sine):
    wide = values.shape[1]
    lane = lax.broadcasted_iota(jnp.int32, values.shape, 1) % HEAD_DIM
    ahead = pltpu.roll(values, wide - HEAD_DIM // 2, 1)
    behind = pltpu.roll(values, HEAD_DIM // 2, 1)
    return jnp.where(lane < HEAD_DIM // 2, ahead, behind) * sine


def split_kernel(where, gate, up, own, near, far_a, far_b, *, chunk, ff, step):
    me, place = where[0], where[1]
    half = gate.shape[0] // chunk
    for j in range(4):
        columns = pl.ds(j * ff, ff)
        for target, out in ((me, own), (me ^ 1, near)):

            @pl.when(target == j)
            def _(out=out, columns=columns):
                @pl.loop(0, gate.shape[0] // step)
                def _(i):
                    rows = pl.ds(pl.multiple_of(i * step, step), step)
                    out[0, rows, :] = gate[rows, columns]
                    out[1, rows, :] = up[rows, columns]

        for k, far in ((2, far_a), (3, far_b)):

            @pl.when((me ^ k) == j)
            def _(far=far, columns=columns):
                rows = pl.ds(pl.multiple_of(lax.rem(place, half) * chunk, 8), chunk)
                far[0] = gate[rows, columns]
                far[1] = up[rows, columns]


def pack_kernel(key, value, *refs):
    out = refs[-1]
    rows = key.shape[0]
    out[0:rows, 0:KVD] = key[...]
    out[0:rows, KVD:] = value[...]
    out[rows:, :] = jnp.zeros((out.shape[0] - rows, 2 * KVD), BF16)
    for i, ref in enumerate(refs[:-1]):
        size = ref.shape[0]
        out[rows + 8 * i : rows + 8 * i + 1, 0:size] = ref[...].reshape(1, size)


def pack(key, value, *vectors):
    rows = key.shape[0]
    return pl.pallas_call(
        pack_kernel,
        out_shape=jax.ShapeDtypeStruct((rows + 8 * len(vectors), 2 * KVD), BF16),
        in_specs=[VMEM] * (2 + len(vectors)),
        out_specs=VMEM,
        cost_estimate=cost(0, 8 * rows * KVD),
        name="pack",
    )(key, value, *vectors)


def split(where, gate, up, replicas):
    rows = gate.shape[0]
    ff = gate.shape[1] // 4
    chunk = 2 * rows // replicas
    if chunk % 8:
        me, place = where[0], where[1]
        both = jnp.stack([gate, up]).reshape(2, rows, 4, ff).transpose(2, 0, 1, 3)
        far = [pick(both, me ^ k).reshape(2, replicas // 2, chunk, ff) for k in (2, 3)]
        spot = place % (replicas // 2)
        return pick(both, me), pick(both, me ^ 1), pick(far[0], spot, 1), pick(far[1], spot, 1)
    shape = jax.ShapeDtypeStruct((2, rows, ff), BF16)
    piece = jax.ShapeDtypeStruct((2, chunk, ff), BF16)
    return pl.pallas_call(
        functools.partial(split_kernel, chunk=chunk, ff=ff, step=32),
        out_shape=(shape, shape, piece, piece),
        in_specs=[SMEM, VMEM, VMEM],
        out_specs=(VMEM,) * 4,
        compiler_params=LIMIT,
        cost_estimate=cost(0, 16 * rows * ff),
        name="split",
    )(where, gate, up)


def arrange_kernel(where, *refs, moves):
    out, sems = refs[-2], refs[-1]
    copies = []
    for i, (source, take, put) in enumerate(moves):
        copy = pltpu.make_async_copy(refs[source].at[take(where)], out.at[put(where)], sems.at[i])
        copy.start()
        copies.append(copy)
    for copy in copies:
        copy.wait()


def arrange(where, sources, shape, moves):
    size = 1
    for extent in shape:
        size *= extent
    return pl.pallas_call(
        functools.partial(arrange_kernel, moves=moves),
        out_shape=jax.ShapeDtypeStruct(shape, BF16),
        in_specs=[SMEM] + [ANY] * len(sources),
        out_specs=VMEM,
        scratch_shapes=[pltpu.SemaphoreType.DMA((len(moves),))],
        compiler_params=LIMIT,
        cost_estimate=cost(0, 4 * size),
        name="arrange",
    )(where, *sources)


def join_kernel(where, *refs, offsets, half, ff):
    count = len(offsets)
    pieces = refs[:count]
    gate, up, slab, sems = refs[-4:]
    me = where[0]
    chunk = pieces[0].shape[1]

    def spot(i):
        return lax.rem(where[1] + offsets[i] + 2 * half, 2 * half)

    def copy(i, out):
        row = pl.multiple_of(lax.rem(spot(i), half) * chunk, 8)
        return pltpu.make_async_copy(slab.at[i % 2], out.at[pl.ds(row, chunk), :], sems.at[i])

    for i in range(count):
        if i >= 2:
            copy(i - 2, gate).wait()
        for j in range(4):
            slab[i % 2, :, pl.ds(j * ff, ff)] = pieces[i][me ^ j].astype(F32)

        @pl.when(spot(i) < half)
        def _(i=i):
            copy(i, gate).start()

        @pl.when(spot(i) >= half)
        def _(i=i):
            copy(i, up).start()

    for i in range(count - 2, count):
        copy(i, gate).wait()


def join(offsets, where, rows, replicas, values, *before):
    count = len(offsets)
    _, chunk, ff = values[0].shape
    half = replicas // 2
    if chunk % 8:
        got = before[0] if before else jnp.zeros((replicas, chunk, 4, ff), F32)
        for offset, value in zip(offsets, values):
            value = jnp.stack([pick(value, where[0] ^ j) for j in range(4)], axis=1)
            spot = (where[1] + offset) % replicas
            got = lax.dynamic_update_slice(got, value.astype(F32)[None], (spot, 0, 0, 0))
        return got, got
    shape = jax.ShapeDtypeStruct((rows, 4 * ff), F32)
    return pl.pallas_call(
        functools.partial(join_kernel, offsets=offsets, half=half, ff=ff),
        out_shape=(shape, shape),
        in_specs=[SMEM] + [VMEM] * count + [ANY] * len(before),
        out_specs=(ANY, ANY),
        scratch_shapes=[pltpu.VMEM((2, chunk, 4 * ff), F32), pltpu.SemaphoreType.DMA((count,))],
        input_output_aliases={1 + count: 0, 2 + count: 1} if before else {},
        compiler_params=LIMIT,
        cost_estimate=cost(0, 48 * rows * ff * count // replicas),
        name="join",
    )(where, *values, *before)


def joined(gate, up, rows):
    if gate.ndim == 2:
        return gate, up
    gate = gate.reshape(2, rows, -1)
    return gate[0], gate[1]


def load_rows(where, blocks, out, sems, first):
    rows = blocks[0].shape[0]
    copies = []
    for k, block in enumerate(blocks):
        row = pl.multiple_of((where[0] ^ k) * rows, 8)
        copies.append(pltpu.make_async_copy(block, out.at[pl.ds(row, rows), :], sems.at[first + k]))
        copies[-1].start()
    return copies


def order_vec(me, blocks, row, size, out, to):
    parts = [b[row : row + 1, 0:size].astype(F32) for b in blocks]
    odd = jnp.full(parts[0].shape, me % 2, jnp.int32) == 1
    far = jnp.full(parts[0].shape, me // 2, jnp.int32) == 1
    for j in range(4):
        same = jnp.where(odd, parts[j ^ 1], parts[j])
        other = jnp.where(odd, parts[j ^ 3], parts[j ^ 2])
        out[pl.ds(to, 1), pl.ds(j * size, size)] = jnp.where(far, other, same)


def four(own, other, two):
    return (own, other.at[0], two, other.at[1])


def kv_kernel(where, hidden, cosine, sine, own, other, two, kv, normed_out, vectors, weights):
    blocks = four(own, other, two)
    width = hidden.shape[1]
    rows = width // 4
    vectors[...] = jnp.zeros_like(vectors)
    for i, size in enumerate((rows, rows, rows, KVD // 4, KVD // 4)):
        order_vec(where[0], blocks, rows + 8 * i, size, vectors, i)
    for k, block in enumerate(blocks):
        row = pl.multiple_of((where[0] ^ k) * rows, 8)
        weights[pl.ds(row, rows), :] = block[0:rows, :]
    x = hidden[...].astype(F32)
    normed = (x * rms_scale(x) * vectors[0:1, 0:width]).astype(BF16)
    normed_out[...] = normed
    both = mm(normed, weights[...])
    key = both[:, :KVD] + vectors[3:4, 0:KVD]
    key = key * cosine[...] + turn_back(key, sine[...])
    kv[:, 0:KVD] = key.astype(BF16)
    kv[:, KVD : 2 * KVD] = (both[:, KVD:] + vectors[4:5, 0:KVD]).astype(BF16)


def project_kv(where, hidden, cosine, sine, *blocks):
    part, width = hidden.shape
    return pl.pallas_call(
        kv_kernel,
        out_shape=(
            jax.ShapeDtypeStruct((part, 2 * KVD), BF16),
            jax.ShapeDtypeStruct((part, width), BF16),
            jax.ShapeDtypeStruct((8, width), F32),
            jax.ShapeDtypeStruct((width, 2 * KVD), BF16),
        ),
        in_specs=[SMEM] + [VMEM] * 6,
        out_specs=(VMEM,) * 4,
        compiler_params=LIMIT,
        cost_estimate=cost(4 * part * width * KVD, 4 * part * width),
        name="kv",
    )(where, hidden, cosine, sine, *blocks)


def heads_forward(heads, query, kv, mask, attended, logs, first):
    lane = lax.broadcasted_iota(jnp.int32, logs.shape, 1)
    for h in heads:
        g = h // GROUPS
        keys = kv[:, pl.ds(g * HEAD_DIM, HEAD_DIM)]
        values = kv[:, pl.ds(KVD + g * HEAD_DIM, HEAD_DIM)]
        lanes = pl.ds(h * HEAD_DIM, HEAD_DIM)
        scores = mm_nt(query[:, lanes], keys) + mask[...]
        top = jnp.max(scores, axis=-1, keepdims=True)
        raised = jnp.exp(scores - top)
        total = jnp.sum(raised, axis=-1, keepdims=True)
        logs = jnp.where(lane == h, top + jnp.log(total), logs)
        probs = (raised * (1.0 / total)).astype(BF16)
        attended[:, pl.ds(h * HEAD_DIM - first, HEAD_DIM)] = mm(probs, values).astype(BF16)
    return logs


def attend_kernel(where, normed_one, vectors, cosine, sine, own_ids, key_ids, *refs, heads):
    blocks, wq = four(*refs[0:3]), four(*refs[3:6])
    query, attended, lse, w_q, kv, mask, sems = refs[6:]
    part, width = normed_one.shape
    copies = load_rows(where, wq, w_q, sems, 0)
    for k, block in enumerate(blocks):
        kv[pl.ds(k * part, part), :] = block[...]
    square = (part, part)
    diagonal = lax.broadcasted_iota(jnp.int32, square, 0) == lax.broadcasted_iota(jnp.int32, square, 1)
    own = jnp.where(diagonal, own_ids[...].astype(F32), 0.0)
    own = jnp.sum(own, axis=1, keepdims=True)
    mask[...] = jnp.where(key_ids[...].astype(F32) <= own, 0.0, HIDDEN_KEY)
    cos, sin = cosine[...], sine[...]
    for copy in copies:
        copy.wait()
    for first in range(0, width, LANES):
        lanes = pl.ds(first, LANES)
        value = mm(normed_one[...], w_q[:, lanes]) + vectors[1:2, lanes]
        value = value * cos + turn_back(value, sin)
        query[:, lanes] = (value.astype(BF16).astype(F32) * FACTOR).astype(BF16)
    logs = jnp.zeros((part, LANES), F32)
    lse[...] = heads_forward(heads, query, kv, mask, attended, logs, 0)


def attend(heads, where, normed_one, vectors, cosine, sine, own_ids, key_ids, kv, wq):
    part, width = normed_one.shape
    length = key_ids.shape[1]
    work = part * length * len(heads)
    return pl.pallas_call(
        functools.partial(attend_kernel, heads=heads),
        out_shape=(
            jax.ShapeDtypeStruct((part, width), BF16),
            jax.ShapeDtypeStruct((part, len(heads) * HEAD_DIM), BF16),
            jax.ShapeDtypeStruct((part, LANES), F32),
            jax.ShapeDtypeStruct((width, width), BF16),
            jax.ShapeDtypeStruct((length, 2 * KVD), BF16),
            jax.ShapeDtypeStruct((part, length), F32),
        ),
        in_specs=[SMEM] + [VMEM] * 9 + [ANY] * 3,
        out_specs=(VMEM,) * 6,
        scratch_shapes=[pltpu.SemaphoreType.DMA((4,))],
        compiler_params=LIMIT,
        cost_estimate=cost(4 * work * HEAD_DIM + 2 * part * width * width, 8 * part * width, work),
        name="attend",
    )(where, normed_one, vectors, cosine, sine, own_ids, key_ids, *kv, *wq)


def residual_kernel(where, hidden, vectors, mask, query, kv, before, lse_before, *refs, heads):
    wo = four(*refs[0:3])
    attended, lse, residual, normed, w_o, sems = refs[3:]
    first = before.shape[1]
    late = load_rows(where, wo, w_o, sems, 0)
    attended[:, 0:first] = before[...]
    lse[...] = heads_forward(heads, query, kv, mask, attended, lse_before[...], 0)
    for copy in late:
        copy.wait()
    value = hidden[...].astype(F32) + mm(attended[...], w_o[...])
    residual[...] = value
    normed[...] = (value * rms_scale(value) * vectors[2:3, :]).astype(BF16)


def attend_rest(heads, where, hidden, vectors, mask, query, kv, before, lse, wo):
    part, width = hidden.shape
    work = part * kv.shape[0] * len(heads)
    tokens = jax.ShapeDtypeStruct((part, width), BF16)
    return pl.pallas_call(
        functools.partial(residual_kernel, heads=heads),
        out_shape=(
            tokens,
            jax.ShapeDtypeStruct((part, LANES), F32),
            jax.ShapeDtypeStruct((part, width), F32),
            tokens,
            jax.ShapeDtypeStruct((width, width), BF16),
        ),
        in_specs=[SMEM] + [VMEM] * 7 + [ANY] * 3,
        out_specs=(VMEM,) * 5,
        scratch_shapes=[pltpu.SemaphoreType.DMA((4,))],
        compiler_params=LIMIT,
        cost_estimate=cost(4 * work * HEAD_DIM + 2 * part * width * width, 8 * part * width, work),
        name="attend_rest",
    )(where, hidden, vectors, mask, query, kv, before, lse, *wo)


def units_kernel(one, two, grad_hidden, weights, tokens, hidden, dgate, dup):
    part = one.shape[0]
    tokens[0:part, :] = one[...]
    tokens[part:, :] = two[...]
    value = tokens[...]
    gate = mm(value, weights[0])
    up = mm(value, weights[1])
    back = grad_hidden[...]
    sigma = jax.nn.sigmoid(gate)
    active = gate * sigma
    hidden[...] = (active * up).astype(BF16)
    dup[...] = (back * active).astype(BF16)
    dgate[...] = (back * up * sigma * (1.0 + gate * (1.0 - sigma))).astype(BF16)


def back_units_kernel(dy_one, dy_two, w_down, out, dy, *, slot):
    part = dy_one.shape[0]
    dy[0:part, :] = dy_one[...]
    dy[part:, :] = dy_two[slot]
    out[...] = mm_nt(dy[...], w_down[...])


def back_units(slot, dy_one, dy_two, w_down):
    part, width = dy_one.shape
    ff = w_down.shape[0]
    return pl.pallas_call(
        functools.partial(back_units_kernel, slot=slot),
        out_shape=(
            jax.ShapeDtypeStruct((2 * part, ff), F32),
            jax.ShapeDtypeStruct((2 * part, width), BF16),
        ),
        in_specs=[VMEM] * 3,
        out_specs=(VMEM, VMEM),
        compiler_params=LIMIT,
        cost_estimate=cost(4 * part * width * ff, 2 * width * ff + 8 * part * ff),
        name="back_units",
    )(dy_one, dy_two, w_down)


def units(one, two, grad_hidden, weights):
    part, width = one.shape
    ff = weights.shape[2]
    shape = jax.ShapeDtypeStruct((2 * part, ff), BF16)
    return pl.pallas_call(
        units_kernel,
        out_shape=(jax.ShapeDtypeStruct((2 * part, width), BF16), shape, shape, shape),
        in_specs=[VMEM] * 4,
        out_specs=(VMEM,) * 4,
        compiler_params=LIMIT,
        cost_estimate=cost(8 * part * width * ff, 6 * width * ff, 2 * part * ff),
        name="units",
    )(one, two, grad_hidden, weights)


def weight_kernel(*refs, count):
    left_a, left_b = refs[0:2]
    rights = refs[2 : 2 + 2 * count]
    outs = refs[2 + 2 * count :]
    for i, out in enumerate(outs):
        total = mm_tn(left_a[...], rights[2 * i][...]) + mm_tn(left_b[...], rights[2 * i + 1][...])
        out[...] = total.astype(BF16)


def weight_grads(left, rights):
    tall = left[0].shape[1]
    wide = rights[0][0].shape[1]
    count = len(rights)
    shape = jax.ShapeDtypeStruct((tall, wide), BF16)
    return pl.pallas_call(
        functools.partial(weight_kernel, count=count),
        out_shape=(shape,) * count,
        in_specs=[VMEM] * (2 + 2 * count),
        out_specs=(VMEM,) * count,
        compiler_params=LIMIT,
        cost_estimate=cost(4 * count * left[0].shape[0] * tall * wide, 6 * count * tall * wide),
        name="weight_grads",
    )(*left, *[r for pair in rights for r in pair])


def partial_kernel(*refs, mats, transposed):
    lefts = refs[: 2 * mats]
    weights, keep, send = refs[2 * mats :]
    part = keep.shape[1]
    for chip in range(2):
        if transposed:
            total = mm_nt(lefts[2 * chip][...], weights[0])
            total += mm_nt(lefts[2 * chip + 1][...], weights[1])
        else:
            total = mm(lefts[chip][...], weights[...])
        keep[chip] = total[:part].astype(BF16)
        send[chip] = total[part:].astype(BF16)


def partial_sums(lefts, weights, width, transposed):
    rows = lefts[0].shape[0]
    mats = len(lefts) // 2
    shape = jax.ShapeDtypeStruct((2, rows // 2, width), BF16)
    return pl.pallas_call(
        functools.partial(partial_kernel, mats=mats, transposed=transposed),
        out_shape=(shape, shape),
        in_specs=[VMEM] * (2 * mats + 1),
        out_specs=(VMEM, VMEM),
        compiler_params=LIMIT,
        cost_estimate=cost(4 * mats * rows * lefts[0].shape[1] * width, 8 * mats * rows * width),
        name="partial_sums",
    )(*lefts, weights)


def branch_kernel(own, near, far, residual, dy, vectors, w_o, dresidual, dbranch, dattended, gain):
    value = residual[...]
    scale = rms_scale(value)
    unit = value * scale
    grad = own[0].astype(F32) + near[0].astype(F32) + far[...].astype(F32)
    gain[...] = jnp.sum(grad * unit, axis=0, keepdims=True)
    inner = grad * vectors[2:3, :]
    total = scale * (inner - unit * jnp.mean(inner * unit, axis=-1, keepdims=True))
    total = dy[...].astype(F32) + total
    dresidual[...] = total
    low = total.astype(BF16)
    dbranch[...] = low
    dattended[...] = mm_nt(low, w_o[...]).astype(BF16)


def branch_back(own, near, far, residual, dy, vectors, w_o):
    part, width = residual.shape
    tokens = jax.ShapeDtypeStruct((part, width), BF16)
    return pl.pallas_call(
        branch_kernel,
        out_shape=(
            jax.ShapeDtypeStruct((part, width), F32),
            tokens,
            tokens,
            jax.ShapeDtypeStruct((1, width), F32),
        ),
        in_specs=[VMEM] * 7,
        out_specs=(VMEM,) * 4,
        compiler_params=LIMIT,
        cost_estimate=cost(2 * part * width * width, 20 * part * width),
        name="branch_back",
    )(own, near, far, residual, dy, vectors, w_o)


def back_kernel(mask, query, kv, lse, dattended, *refs, heads, first):
    dquery, dkv = refs[-2:]
    logs = lse[...]
    lane = lax.broadcasted_iota(jnp.int32, logs.shape, 1)
    if len(refs) > 2:
        dkv[...] = refs[0][...]
    else:
        dkv[...] = jnp.zeros_like(dkv)
    for h in heads:
        g = h // GROUPS
        k_lanes = pl.ds(g * HEAD_DIM, HEAD_DIM)
        v_lanes = pl.ds(KVD + g * HEAD_DIM, HEAD_DIM)
        lanes = pl.ds(h * HEAD_DIM, HEAD_DIM)
        q, do = query[:, lanes], dattended[:, lanes]
        keys, values = kv[:, k_lanes], kv[:, v_lanes]
        log = jnp.sum(jnp.where(lane == h, logs, 0.0), axis=-1, keepdims=True)
        probs = jnp.exp(mm_nt(q, keys) + mask[...] - log)
        dprobs = mm_nt(do, values)
        total = jnp.sum(probs * dprobs, axis=-1, keepdims=True)
        dscores = (probs * (dprobs - total)).astype(BF16)
        dquery[:, pl.ds(h * HEAD_DIM - first, HEAD_DIM)] = mm(dscores, keys) * FACTOR
        dkv[:, k_lanes] += mm_tn(dscores, q)
        dkv[:, v_lanes] += mm_tn(probs.astype(BF16), do)


def attend_back(heads, mask, query, kv, lse, dattended, *before):
    part = query.shape[0]
    length = kv.shape[0]
    first = heads[0] * HEAD_DIM
    work = part * length * len(heads)
    return pl.pallas_call(
        functools.partial(back_kernel, heads=heads, first=first),
        out_shape=(
            jax.ShapeDtypeStruct((part, len(heads) * HEAD_DIM), F32),
            jax.ShapeDtypeStruct((length, 2 * KVD), F32),
        ),
        in_specs=[VMEM] * (5 + len(before)),
        out_specs=(VMEM, VMEM),
        compiler_params=LIMIT,
        cost_estimate=cost(10 * work * HEAD_DIM, 8 * length * KVD, work),
        name="attend_back",
    )(mask, query, kv, lse, dattended, *before)


def deal(me, weights, per, keep, send):
    count = keep.shape[1]
    for k in range(4):
        out = (keep, send)[k % 2]
        for r in range(count):
            out[k // 2, r, 0:per, :] = weights[me ^ k, pl.ds(r * per, per), :].astype(BF16)


def out_grads_kernel(where, attended, dbranch, keep, send, weights):
    rows, width = weights.shape[1:]
    per = rows // keep.shape[1]
    weights[...] = mm_tn(attended[...], dbranch[...]).reshape(4, rows, width)
    if per < keep.shape[2]:
        keep[...] = jnp.zeros(keep.shape, BF16)
        send[...] = jnp.zeros(send.shape, BF16)
    deal(where[0], weights, per, keep, send)


def out_grads(replicas, where, attended, dbranch):
    part, width = attended.shape
    rows = width // 4
    tall = padded(rows, replicas)
    shape = jax.ShapeDtypeStruct((2, replicas, tall, width), BF16)
    return pl.pallas_call(
        out_grads_kernel,
        out_shape=(shape, shape),
        in_specs=[SMEM] + [VMEM] * 2,
        out_specs=(VMEM, VMEM),
        scratch_shapes=[pltpu.VMEM((4, rows, width), F32)],
        compiler_params=LIMIT,
        cost_estimate=cost(2 * part * width * width, 8 * width * width),
        name="out_grads",
    )(where, attended, dbranch)


def padded(rows, replicas):
    return -(-(rows // replicas + 1) // 8) * 8


def grads_kernel(where, hidden, normed, dresidual, dq_a, dq_b, own, near, far, cosine, sine, vectors, gain_two, w_q, w_kv, in_grad, keep, send, dpre, weights, values):
    me = where[0]
    part, width = hidden.shape
    rows = width // 4
    total_wide = width + 2 * KVD
    cos, sin = cosine[...], sine[...]
    split_at = dq_a.shape[1]
    grad = own[0].astype(F32) + near[0].astype(F32) + far[...].astype(F32)
    for first in range(0, width + KVD, LANES):
        if first < split_at:
            value = dq_a[:, pl.ds(first, LANES)]
        elif first < width:
            value = dq_b[:, pl.ds(first - split_at, LANES)]
        else:
            value = grad[:, :KVD]
        dpre[:, pl.ds(first, LANES)] = (value * cos - turn_back(value, sin)).astype(BF16)
    dpre[:, pl.ds(width + KVD, KVD)] = grad[:, KVD:].astype(BF16)
    bias = jnp.sum(dpre[...].astype(F32), axis=0, keepdims=True)

    x = hidden[...].astype(F32)
    scale = rms_scale(x)
    unit = x * scale
    back = mm_nt(dpre[:, 0:width], w_q[...]) + mm_nt(dpre[:, pl.ds(width, 2 * KVD)], w_kv[...])
    gain_one = jnp.sum(back * unit, axis=0, keepdims=True)
    inner = back * vectors[0:1, :]
    total = scale * (inner - unit * jnp.mean(inner * unit, axis=-1, keepdims=True))
    in_grad[...] = (dresidual[...] + total).astype(BF16)

    cut = width + KVD
    weights[...] = mm_tn(normed[...], dpre[...]).reshape(4, rows, total_wide)
    sizes = (rows, rows, rows, KVD // 4, KVD // 4)
    sources = (gain_one, bias[:, :width], gain_two[...], bias[:, width:cut], bias[:, cut:])
    values[...] = jnp.zeros_like(values)
    for j in range(4):
        for spot, size, source in zip(SPOTS, sizes, sources):
            values[j, 0:1, pl.ds(spot, size)] = source[:, j * size : (j + 1) * size]
    count = keep.shape[1]
    per = rows // count
    each = VECTOR // count
    keep[...] = jnp.zeros(keep.shape, BF16)
    send[...] = jnp.zeros(send.shape, BF16)
    deal(me, weights, per, keep, send)
    for k in range(4):
        out = (keep, send)[k % 2]
        for r in range(count):
            line = values[me ^ k, 0:1, pl.ds(r * each, each)]
            out[k // 2, r, per : per + 1, 0:each] = line.astype(BF16)


def attention_grads(replicas, where, hidden, *args):
    part, width = hidden.shape
    rows = width // 4
    wide = width + 2 * KVD
    shape = jax.ShapeDtypeStruct((2, replicas, padded(rows, replicas), wide), BF16)
    return pl.pallas_call(
        grads_kernel,
        out_shape=(jax.ShapeDtypeStruct((part, width), BF16), shape, shape),
        in_specs=[SMEM] + [VMEM] * 14,
        out_specs=(VMEM,) * 3,
        scratch_shapes=[
            pltpu.VMEM((part, wide), BF16),
            pltpu.VMEM((4, rows, wide), F32),
            pltpu.VMEM((4, 8, VECTOR), F32),
        ],
        compiler_params=LIMIT,
        cost_estimate=cost(8 * part * width * width, 20 * width * width),
        name="attention_grads",
    )(where, hidden, *args)


def split_grads_kernel(where, *refs, offsets, per):
    count = len(offsets)
    pieces = refs[:count]
    query, key, value, out, vectors, held = refs[count:]
    width = query.shape[1]
    each = VECTOR // count
    for offset, piece in zip(offsets, pieces):
        held[lax.rem(where[1] + offset + count, count)] = piece[...].astype(F32)
    for s in range(count):
        rows = pl.ds(s * per, per)
        query[rows, :] = held[s, 0:per, 0:width]
        key[rows, :] = held[s, 0:per, width : width + KVD]
        value[rows, :] = held[s, 0:per, width + KVD : width + 2 * KVD]
        out[rows, :] = held[s, 0:per, width + 2 * KVD :]
        vectors[0:1, pl.ds(s * each, each)] = held[s, per : per + 1, 0:each]


def split_grads(found, where, rows, width):
    offsets = [offset for offset, _ in found]
    count = len(found)
    tall, wide = found[0][1].shape
    shape = lambda columns: jax.ShapeDtypeStruct((rows, columns), F32)
    return pl.pallas_call(
        functools.partial(split_grads_kernel, offsets=offsets, per=rows // count),
        out_shape=(
            shape(width),
            shape(KVD),
            shape(KVD),
            shape(width),
            jax.ShapeDtypeStruct((1, VECTOR), F32),
        ),
        in_specs=[SMEM] + [VMEM] * count,
        out_specs=(VMEM,) * 5,
        scratch_shapes=[pltpu.VMEM((count, tall, wide), F32)],
        compiler_params=LIMIT,
        cost_estimate=cost(0, 6 * rows * wide),
        name="split_grads",
    )(where, *[value for _, value in found])


def stack_rows_kernel(where, *refs, offsets):
    count = len(offsets)
    out = refs[count]
    rows = refs[0].shape[0]
    for offset, piece in zip(offsets, refs[:count]):
        row = pl.multiple_of(lax.rem(where[1] + offset + count, count) * rows, 8)
        out[pl.ds(row, rows), :] = piece[...].astype(F32)


def stack_rows(found, where, place):
    offsets = [offset for offset, _ in found]
    count = len(found)
    rows, width = found[0][1].shape
    if rows % 8:
        return assemble(found, place, F32).reshape(count * rows, width)
    return pl.pallas_call(
        functools.partial(stack_rows_kernel, offsets=offsets),
        out_shape=jax.ShapeDtypeStruct((count * rows, width), F32),
        in_specs=[SMEM] + [VMEM] * count,
        out_specs=VMEM,
        compiler_params=LIMIT,
        cost_estimate=cost(0, 6 * count * rows * width),
        name="stack_rows",
    )(where, *[value for _, value in found])


class Order:
    def __init__(self):
        self.last = None

    def __call__(self, run, *values):
        values = self.hold(*values)
        found = run(*values)
        self.last = tuple(found) if isinstance(found, (tuple, list)) else (found,)
        return found

    def wait(self, *values):
        self.last = (*(self.last or ()), *values)

    def hold(self, *values):
        if self.last is None:
            return values
        return lax.optimization_barrier((*values, *self.last))[: len(values)]


class Ring:
    def __init__(self, count, lead):
        self.count = count
        self.lead = lead
        self.order = [0, 2, 4, 6, 7, 5, 3, 1] if count == 8 else list(range(count))
        self.plus = count // 2
        self.minus = count - 1 - self.plus

    def place(self):
        replica = lax.axis_index("replica")
        if self.count == 8:
            line, side = replica // 2, replica % 2
            return jnp.where(side == 0, line, 7 - line)
        return replica

    def replica(self, place):
        if self.count == 8:
            return jnp.where(place < 4, 2 * place, 15 - 2 * place)
        return place

    def move(self, value, step):
        n = self.count
        pairs = [(self.order[p], self.order[(p + step) % n]) for p in range(n)]
        return lax.ppermute(value, "replica", pairs)

    def both(self):
        return ((self.plus, self.lead), (self.minus, -self.lead))


class RingSum:
    def __init__(self, ring, order, take, *arrays):
        self.ring, self.order, self.take, self.arrays = ring, order, take, arrays
        self.left = [hops for hops, _ in ring.both()]
        self.arrived = []
        self.moving = self._send(None)

    def _send(self, moving):
        ring = self.ring
        active = [i for i in range(2) if self.left[i] > 0]

        def run(*values):
            parts = []
            for n, i in enumerate(active):
                step = ring.both()[i][1]
                part = self.take(step * self.left[i], *values[: len(self.arrays)])
                if moving is not None:
                    got = values[len(self.arrays) + n]
                    part = (part.astype(F32) + got.astype(F32)).astype(BF16)
                parts.append(part)
            return parts

        got = [] if moving is None else [moving[i] for i in active]
        parts = self.order(run, *self.arrays, *got)
        sent = [None, None]
        for part, i in zip(parts, active):
            sent[i] = ring.move(part, ring.both()[i][1])
            self.left[i] -= 1
            if self.left[i] == 0:
                self.arrived.append(sent[i])
        return sent

    def step(self):
        self.moving = self._send(self.moving)

    def total(self):
        while max(self.left) > 0:
            self.step()
        count = len(self.arrays)

        def run(*values):
            own = self.take(0, *values[:count]).astype(F32)
            return sum((v.astype(F32) for v in values[count:]), own).astype(BF16)

        return self.order(run, *self.arrays, *self.arrived)


class RingGather:
    def __init__(self, ring, order, own):
        self.ring, self.order = ring, order
        self.found = [(0, own)]
        self.hop = 0
        self.moving = [own, own]
        self._send()

    def _send(self):
        self.hop += 1
        for i, (hops, step) in enumerate(self.ring.both()):
            if self.hop <= hops:
                self.moving[i] = self.ring.move(self.moving[i], step)
                self.found.append((-step * self.hop, self.moving[i]))

    def step(self):
        if self.hop < self.ring.plus:
            self.moving = list(self.order(lambda *v: v, *self.moving))
            self._send()

    def take(self, first, last):
        found = self.found[first:last]
        values = self.order(lambda *v: v, *[value for _, value in found])
        self.found[first:last] = [(offset, value) for (offset, _), value in zip(found, values)]

    def finish(self):
        while self.hop < self.ring.plus:
            self.step()
        return self.found


class Share:
    def __init__(self, ring, order, own):
        self.ring, self.order = ring, order
        self.found = [(0, (0, 1), own)]
        self.hop = 0
        self.moving = [own, own]
        self._send()

    def _send(self):
        self.hop += 1
        for i, step in enumerate((1, -1)):
            halves = (0, 1)
            if self.hop == self.ring.count // 4:
                halves = (i,)
                self.moving[i] = self.moving[i][:, i : i + 1]
            self.moving[i] = self.ring.move(self.moving[i], step)
            self.found.append((-step * self.hop, halves, self.moving[i]))

    def step(self):
        self.moving = list(self.order(lambda *v: v, *self.moving))
        self._send()


def assemble(found, place, dtype):
    block = found[0][1]
    out = jnp.zeros((len(found),) + block.shape, dtype)
    for offset, value in found:
        start = ((place + offset) % len(found),) + (0,) * block.ndim
        out = lax.dynamic_update_slice(out, value.astype(dtype)[None], start)
    return out


def swap(value, mask):
    return lax.ppermute(value, "group", [(j, j ^ mask) for j in range(4)])


def spread(own):
    one = swap(own, 1)
    two = swap(own, 2)
    return [own, one, two, swap(two, 1)]


class Spread:
    def __init__(self, own):
        self.own, self.two = own, swap(own, 2)

    def step(self, order):
        self.other = swap(order(lambda *v: jnp.stack(v), self.own, self.two), 1)

    def parts(self):
        return self.own, self.other, self.two


class Collect:
    def __init__(self, order, keep, send):
        self.order, self.keep, self.got = order, keep, swap(send, 1)

    def step(self):
        def run(keep, got):
            return (keep[1].astype(F32) + got[1].astype(F32)).astype(BF16)

        self.other = swap(self.order(run, self.keep, self.got), 2)

    def terms(self):
        return self.keep, self.got, self.other


def after(value, *others):
    return lax.optimization_barrier((value,) + others)[0]


FIRST_HEADS = range(0, 8)
OTHER_HEADS = range(8, HEADS)


def make_body(replicas):
    ring_up = Ring(replicas, 1)
    ring_down = Ring(replicas, -1)

    def body(
        hidden_in,
        out_grad,
        positions,
        block_ids,
        gain_one,
        w_query,
        b_query,
        w_key,
        b_key,
        w_value,
        b_value,
        w_out,
        gain_two,
        w_gate,
        w_up,
        w_down,
    ):
        _, part, width = hidden_in.shape
        length = block_ids.shape[1]
        rows = w_gate.shape[0]
        ff = w_down.shape[0]
        half = replicas // 2
        chunk = 2 * rows // replicas
        me = lax.axis_index("group")
        place = ring_up.place()
        where = jnp.stack([me, place])
        order = Order()
        x_value, dy_own = hidden_in[0], out_grad[0]

        packed = order(pack, w_key, w_value, gain_one, b_query, gain_two, b_key, b_value)
        first = Spread(packed)
        wq = Spread(after(w_query, packed))
        offsets = range(-half, half + 1)
        early = [lax.rem(place + (o + replicas), replicas) for o in offsets]
        early += [lax.rem(p, half) for p in early]
        early += [p < half for p in early[: len(offsets)]]
        early += [me ^ k for k in range(4)]
        freqs = THETA ** (-(2.0 * jnp.arange(HEAD_DIM // 2, dtype=F32)) / HEAD_DIM)
        angles = positions[0].astype(F32)[:, None] * jnp.tile(freqs, LANES * 2 // HEAD_DIM)
        sign = jnp.where(jnp.arange(LANES) % HEAD_DIM < HEAD_DIM // 2, -1.0, 1.0)
        ids = block_ids.reshape(4, part)
        own_ids = pick(ids, me).reshape(1, part)
        key_ids = jnp.concatenate([pick(ids, me ^ k) for k in range(4)]).reshape(1, length)
        early += [jnp.cos(angles), jnp.sin(angles) * sign, own_ids, key_ids, where]
        early = lax.optimization_barrier(tuple(early))
        order.wait(*early)
        *early, cosine, sine, own_ids, key_ids, where = early
        count = len(offsets)
        places = dict(zip(offsets, early[:count]))
        rows_at = dict(zip(offsets, early[count : 2 * count]))
        first_half = dict(zip(offsets, early[2 * count : 3 * count]))
        member = early[3 * count :]
        own, near, far_a, far_b = order(
            lambda gate, up: split(where, gate, up, replicas), w_gate, w_up
        )
        first.step(order)
        far_a, far_b = swap(after(far_a, first.two), 2), swap(after(far_b, first.two), 3)
        kv, normed_one, vectors, w_kv = order(
            lambda *v: project_kv(where, *v), x_value, cosine, sine, *first.parts()
        )
        kv = Spread(kv)
        wq.step(order)
        far = order(lambda *v: jnp.stack(v), far_a, far_b)
        pieces = Share(ring_up, order, far)
        kv.step(order)
        wo = Spread(after(w_out, kv.two))
        query, attended, lse, w_q, kv, mask = order(
            lambda *v: attend(FIRST_HEADS, where, *v[:6], v[6:9], v[9:]),
            normed_one,
            vectors,
            cosine,
            sine,
            own_ids,
            key_ids,
            *kv.parts(),
            *wq.parts(),
        )
        pieces.step()
        wo.step(order)
        dy = Spread(after(dy_own, wo.two))
        near = swap(after(near, query), 1)
        attended, lse, residual, normed_two, w_o = order(
            lambda *v: attend_rest(OTHER_HEADS, where, *v[:7], v[7:]),
            x_value,
            vectors,
            mask,
            query,
            kv,
            attended,
            lse,
            *wo.parts(),
        )
        while pieces.hop < replicas // 4:
            pieces.step()
        order.wait(*[value for _, _, value in pieces.found])
        (normed_late,) = order.hold(normed_two)
        one, two = swap(normed_late, 1), swap(normed_late, 2)
        dy.step(order)
        shape = (2, 4, half, chunk, ff)
        moves = []
        for mat in range(2):
            for source in (0, 1):
                moves.append((source, lambda s, m=mat: m, lambda s, m=mat, k=source: (m, s[0] ^ k)))
        for i, (offset, mats, _) in enumerate(pieces.found):
            for slot in range(2):
                for n, mat in enumerate(mats):
                    put = lambda s, d=offset + half, m=mat, k=2 + slot: (m, s[0] ^ k, lax.rem(s[1] + d, half))
                    moves.append((2 + i, lambda s, j=slot, n=n: (j, n), put))
        w_both = order(
            lambda *v: arrange(where, v, shape, moves),
            *[v.reshape(shape[:1] + shape[2:]) for v in (own, near)],
            *[value for _, _, value in pieces.found],
        )
        w_both = w_both.reshape(2, width, ff)

        grad_hidden, dy_a = order(functools.partial(back_units, 0), dy.own, dy.other, w_down)
        tok_a, hid_a, dgate_a, dup_a = order(units, normed_two, one, grad_hidden, w_both)
        three = swap(order.hold(two)[0], 1)
        grad_hidden, dy_b = order(functools.partial(back_units, 1), dy.two, dy.other, w_down)
        tok_b, hid_b, dgate_b, dup_b = order(units, two, three, grad_hidden, w_both)
        grad_gate, grad_up = order(
            lambda *v: weight_grads(v[:2], [v[2:4], v[4:6]]),
            tok_a,
            tok_b,
            dgate_a,
            dgate_b,
            dup_a,
            dup_b,
        )

        def take_units(offset, gate, up):
            row = rows_at[offset]
            return jnp.where(first_half[offset], pick(gate, row, 1), pick(up, row, 1))

        def take_rows(offset, value):
            return pick(value, places[offset])

        shape = (4, half, chunk, ff)
        sum_units = RingSum(
            ring_up, order, take_units, grad_gate.reshape(shape), grad_up.reshape(shape)
        )
        sums = order(
            lambda *v: partial_sums(v[:4], v[4], width, True), dgate_a, dup_a, dgate_b, dup_b, w_both
        )
        to_normed = Collect(order, *sums)
        sum_units.step()
        to_normed.step()
        (grad_down,) = order(lambda *v: weight_grads(v[:2], [v[2:]]), hid_a, hid_b, dy_a, dy_b)
        grad_down = grad_down.reshape(replicas, ff // replicas, width)
        sum_down = RingSum(ring_down, order, take_rows, grad_down)

        dresidual, dbranch, dattended, grad_gain_two = order(
            branch_back, *to_normed.terms(), residual, dy_own, vectors, w_o
        )
        to_w_out = Collect(
            order, *order(lambda *v: out_grads(replicas, where, *v), attended, dbranch)
        )
        sum_down.step()
        args = (mask, query, kv, lse, dattended)
        dq_a, dkv = order(functools.partial(attend_back, FIRST_HEADS), *args)
        sum_units.step()
        to_w_out.step()
        sum_down.step()
        dq_b, dkv = order(functools.partial(attend_back, OTHER_HEADS), *args, dkv)
        dkv = dkv.astype(BF16).reshape(2, 2, part, 2 * KVD)
        to_kv = Collect(order, dkv[:, 0], dkv[:, 1])
        sum_units.step()
        to_kv.step()
        sum_down.step()
        order.wait(to_w_out.other)
        in_grad, *packed = order(
            lambda *v: attention_grads(replicas, where, *v),
            x_value,
            normed_one,
            dresidual,
            dq_a,
            dq_b,
            *to_kv.terms(),
            cosine,
            sine,
            vectors,
            grad_gain_two,
            w_q,
            w_kv,
        )
        to_weights = Collect(order, *packed)
        mine = sum_units.total()
        blocks = [pick(mine, member[0])]
        blocks += [swap(pick(mine, member[k]), k) for k in (1, 2, 3)]
        to_weights.step()
        down = sum_down.total()
        all_units = RingGather(ring_up, order, order(lambda *v: jnp.stack(v), *blocks))
        all_down = RingGather(ring_down, order, down)
        sums_out = order(lambda *v: partial_sums(v[:2], v[2], width, False), hid_a, hid_b, w_down)
        all_down.step()
        def total(*terms):
            one, two = [
                keep[0].astype(F32) + got[0].astype(F32) + other.astype(F32)
                for keep, got, other in (terms[:3], terms[3:])
            ]
            return jnp.concatenate([one, two], axis=2).astype(BF16)

        packed = order(total, *to_weights.terms(), *to_w_out.terms())
        sum_packed = RingSum(ring_down, order, take_rows, packed)
        all_units.step()
        sum_packed.step()
        sum_packed.step()
        all_down.step()
        sum_packed.step()
        all_units.step()
        all_down.step()
        all_packed = RingGather(ring_down, order, sum_packed.total())
        first = all_units.found[:5]
        early = [o for o, _ in first]
        joins = order(lambda *v: join(early, where, rows, replicas, v), *[b for _, b in first])
        all_packed.step()
        all_units.step()
        to_out = Collect(order, *order.hold(*sums_out))
        all_packed.step()
        down = all_down.finish()
        out_down = order(
            lambda *v: stack_rows([(o, b) for (o, _), b in zip(down, v)], where, place),
            *[b for _, b in down],
        )
        to_out.step()
        all_packed.step()
        rest = all_units.finish()[5:]
        late = [o for o, _ in rest]
        joins = order(
            lambda a, b, *v: join(late, where, rows, replicas, v, a, b), *joins, *[b for _, b in rest]
        )
        layer_out = order(
            lambda x, keep, got, other: (
                x + keep[0].astype(F32) + got[0].astype(F32) + other.astype(F32)
            ).astype(BF16),
            residual,
            *to_out.terms(),
        )
        out_gate, out_up = joined(*joins, rows)
        found = all_packed.finish()
        g_w_query, g_w_key, g_w_value, g_w_out, values = order(
            lambda *v: split_grads([(o, b) for (o, _), b in zip(found, v)], where, rows, width),
            *[b for _, b in found],
        )
        values = values.reshape(VECTOR)
        sizes = (rows, rows, rows, KVD // 4, KVD // 4)
        g_one, g_bq, g_two, g_bk, g_bv = [values[s : s + n] for s, n in zip(SPOTS, sizes)]
        return (
            layer_out[None],
            in_grad[None],
            g_one,
            g_w_query,
            g_bq,
            g_w_key,
            g_bk,
            g_w_value,
            g_bv,
            g_w_out,
            g_two,
            out_gate,
            out_up,
            out_down,
        )

    return body


def solution(mesh):
    tokens = P("replica", "group", None)
    matrix = P("group", None)
    vector = P("group")
    weights = (
        vector,
        matrix,
        vector,
        matrix,
        vector,
        matrix,
        vector,
        matrix,
        vector,
        matrix,
        matrix,
        matrix,
    )
    in_specs = (tokens, tokens, P("replica", "group"), P("replica", None)) + weights
    out_specs = (tokens, tokens) + weights
    body = make_body(mesh.shape["replica"])
    return jax.shard_map(body, mesh=mesh, in_specs=in_specs, out_specs=out_specs, check_vma=False)
```

```python
import functools

import jax
import jax.numpy as jnp
import numpy as np
from jax import lax
from jax.experimental import pallas as pl
from jax.experimental.pallas import tpu as pltpu
from jax.sharding import PartitionSpec as P

HEADS = 14
KV_HEADS = 2
HEAD_DIM = 64
GROUPS = HEADS // KV_HEADS
KVD = KV_HEADS * HEAD_DIM
FACTOR = 1.0 / HEAD_DIM**0.5
LANES = 128
HIDDEN_KEY = -1e30
SPOTS = (0, 256, 512, 768, 896)
VECTOR = 1024

EPSILON = 1e-06
THETA = 1000000.0

F32 = jnp.float32
BF16 = jnp.bfloat16

ANY = pl.BlockSpec(memory_space=pl.ANY)
VMEM = pl.BlockSpec(memory_space=pltpu.VMEM)
SMEM = pl.BlockSpec(memory_space=pltpu.SMEM)
LIMIT = pltpu.CompilerParams(vmem_limit_bytes=14 * 1024 * 1024)


def rms_scale(values):
    return lax.rsqrt(jnp.mean(values * values, axis=-1, keepdims=True) + EPSILON)


def mm(left, right):
    return jnp.dot(left, right, preferred_element_type=F32)


def mm_nt(left, right):
    return lax.dot_general(left, right, (((1,), (1,)), ((), ())), preferred_element_type=F32)


def mm_tn(left, right):
    return lax.dot_general(left, right, (((0,), (0,)), ((), ())), preferred_element_type=F32)


def pick(stack, index, axis=0):
    return lax.dynamic_index_in_dim(
        stack, index, axis, keepdims=False, allow_negative_indices=False
    )


def cost(flops, moved, special=0):
    return pl.CostEstimate(flops=int(flops), bytes_accessed=int(moved), transcendentals=int(special))


def turn_back(values, sine):
    wide = values.shape[1]
    lane = lax.broadcasted_iota(jnp.int32, values.shape, 1) % HEAD_DIM
    ahead = pltpu.roll(values, wide - HEAD_DIM // 2, 1)
    behind = pltpu.roll(values, HEAD_DIM // 2, 1)
    return jnp.where(lane < HEAD_DIM // 2, ahead, behind) * sine


def split_kernel(where, gate, up, own, near, far_a, far_b, *, chunk, ff, step):
    me, place = where[0], where[1]
    half = gate.shape[0] // chunk
    for j in range(4):
        columns = pl.ds(j * ff, ff)
        for target, out in ((me, own), (me ^ 1, near)):

            @pl.when(target == j)
            def _(out=out, columns=columns):
                @pl.loop(0, gate.shape[0] // step)
                def _(i):
                    rows = pl.ds(pl.multiple_of(i * step, step), step)
                    out[0, rows, :] = gate[rows, columns]
                    out[1, rows, :] = up[rows, columns]

        for k, far in ((2, far_a), (3, far_b)):

            @pl.when((me ^ k) == j)
            def _(far=far, columns=columns):
                rows = pl.ds(pl.multiple_of(lax.rem(place, half) * chunk, 8), chunk)
                far[0] = gate[rows, columns]
                far[1] = up[rows, columns]


def pack_kernel(key, value, *refs):
    out = refs[-1]
    rows = key.shape[0]
    out[0:rows, 0:KVD] = key[...]
    out[0:rows, KVD:] = value[...]
    out[rows:, :] = jnp.zeros((out.shape[0] - rows, 2 * KVD), BF16)
    for i, ref in enumerate(refs[:-1]):
        size = ref.shape[0]
        out[rows + 8 * i : rows + 8 * i + 1, 0:size] = ref[...].reshape(1, size)


def pack(key, value, *vectors):
    rows = key.shape[0]
    return pl.pallas_call(
        pack_kernel,
        out_shape=jax.ShapeDtypeStruct((rows + 8 * len(vectors), 2 * KVD), BF16),
        in_specs=[VMEM] * (2 + len(vectors)),
        out_specs=VMEM,
        cost_estimate=cost(0, 8 * rows * KVD),
        name="pack",
    )(key, value, *vectors)


def split(where, gate, up, replicas):
    rows = gate.shape[0]
    ff = gate.shape[1] // 4
    chunk = 2 * rows // replicas
    if chunk % 8:
        me, place = where[0], where[1]
        both = jnp.stack([gate, up]).reshape(2, rows, 4, ff).transpose(2, 0, 1, 3)
        far = [pick(both, me ^ k).reshape(2, replicas // 2, chunk, ff) for k in (2, 3)]
        spot = place % (replicas // 2)
        return pick(both, me), pick(both, me ^ 1), pick(far[0], spot, 1), pick(far[1], spot, 1)
    shape = jax.ShapeDtypeStruct((2, rows, ff), BF16)
    piece = jax.ShapeDtypeStruct((2, chunk, ff), BF16)
    return pl.pallas_call(
        functools.partial(split_kernel, chunk=chunk, ff=ff, step=32),
        out_shape=(shape, shape, piece, piece),
        in_specs=[SMEM, VMEM, VMEM],
        out_specs=(VMEM,) * 4,
        compiler_params=LIMIT,
        cost_estimate=cost(0, 16 * rows * ff),
        name="split",
    )(where, gate, up)


def arrange_kernel(where, *refs, moves):
    out, sems = refs[-2], refs[-1]
    copies = []
    for i, (source, take, put) in enumerate(moves):
        copy = pltpu.make_async_copy(refs[source].at[take(where)], out.at[put(where)], sems.at[i])
        copy.start()
        copies.append(copy)
    for copy in copies:
        copy.wait()


def arrange(where, sources, shape, moves):
    size = 1
    for extent in shape:
        size *= extent
    return pl.pallas_call(
        functools.partial(arrange_kernel, moves=moves),
        out_shape=jax.ShapeDtypeStruct(shape, BF16),
        in_specs=[SMEM] + [ANY] * len(sources),
        out_specs=VMEM,
        scratch_shapes=[pltpu.SemaphoreType.DMA((len(moves),))],
        compiler_params=LIMIT,
        cost_estimate=cost(0, 4 * size),
        name="arrange",
    )(where, *sources)


def join_kernel(where, *refs, offsets, half, ff):
    count = len(offsets)
    pieces = refs[:count]
    gate, up, slab, sems = refs[-4:]
    me = where[0]
    chunk = pieces[0].shape[1]

    def spot(i):
        return lax.rem(where[1] + offsets[i] + 2 * half, 2 * half)

    def copy(i, out):
        row = pl.multiple_of(lax.rem(spot(i), half) * chunk, 8)
        return pltpu.make_async_copy(slab.at[i % 2], out.at[pl.ds(row, chunk), :], sems.at[i])

    for i in range(count):
        if i >= 2:
            copy(i - 2, gate).wait()
        for j in range(4):
            slab[i % 2, :, pl.ds(j * ff, ff)] = pieces[i][me ^ j].astype(F32)

        @pl.when(spot(i) < half)
        def _(i=i):
            copy(i, gate).start()

        @pl.when(spot(i) >= half)
        def _(i=i):
            copy(i, up).start()

    for i in range(count - 2, count):
        copy(i, gate).wait()


def join(offsets, where, rows, replicas, values, *before):
    count = len(offsets)
    _, chunk, ff = values[0].shape
    half = replicas // 2
    if chunk % 8:
        got = before[0] if before else jnp.zeros((replicas, chunk, 4, ff), F32)
        for offset, value in zip(offsets, values):
            value = jnp.stack([pick(value, where[0] ^ j) for j in range(4)], axis=1)
            spot = (where[1] + offset) % replicas
            got = lax.dynamic_update_slice(got, value.astype(F32)[None], (spot, 0, 0, 0))
        return got, got
    shape = jax.ShapeDtypeStruct((rows, 4 * ff), F32)
    return pl.pallas_call(
        functools.partial(join_kernel, offsets=offsets, half=half, ff=ff),
        out_shape=(shape, shape),
        in_specs=[SMEM] + [VMEM] * count + [ANY] * len(before),
        out_specs=(ANY, ANY),
        scratch_shapes=[pltpu.VMEM((2, chunk, 4 * ff), F32), pltpu.SemaphoreType.DMA((count,))],
        input_output_aliases={1 + count: 0, 2 + count: 1} if before else {},
        compiler_params=LIMIT,
        cost_estimate=cost(0, 48 * rows * ff * count // replicas),
        name="join",
    )(where, *values, *before)


def joined(gate, up, rows):
    if gate.ndim == 2:
        return gate, up
    gate = gate.reshape(2, rows, -1)
    return gate[0], gate[1]


def load_rows(where, blocks, out, sems, first):
    rows = blocks[0].shape[0]
    copies = []
    for k, block in enumerate(blocks):
        row = pl.multiple_of((where[0] ^ k) * rows, 8)
        copies.append(pltpu.make_async_copy(block, out.at[pl.ds(row, rows), :], sems.at[first + k]))
        copies[-1].start()
    return copies


def order_vec(me, blocks, row, size, out, to):
    parts = [b[row : row + 1, 0:size].astype(F32) for b in blocks]
    odd = jnp.full(parts[0].shape, me % 2, jnp.int32) == 1
    far = jnp.full(parts[0].shape, me // 2, jnp.int32) == 1
    for j in range(4):
        same = jnp.where(odd, parts[j ^ 1], parts[j])
        other = jnp.where(odd, parts[j ^ 3], parts[j ^ 2])
        out[pl.ds(to, 1), pl.ds(j * size, size)] = jnp.where(far, other, same)


def four(own, other, two):
    return (own, other.at[0], two, other.at[1])


def kv_kernel(where, hidden, cosine, sine, own, other, two, kv, normed_out, vectors, weights):
    blocks = four(own, other, two)
    width = hidden.shape[1]
    rows = width // 4
    vectors[...] = jnp.zeros_like(vectors)
    for i, size in enumerate((rows, rows, rows, KVD // 4, KVD // 4)):
        order_vec(where[0], blocks, rows + 8 * i, size, vectors, i)
    for k, block in enumerate(blocks):
        row = pl.multiple_of((where[0] ^ k) * rows, 8)
        weights[pl.ds(row, rows), :] = block[0:rows, :]
    x = hidden[...].astype(F32)
    normed = (x * rms_scale(x) * vectors[0:1, 0:width]).astype(BF16)
    normed_out[...] = normed
    both = mm(normed, weights[...])
    key = both[:, :KVD] + vectors[3:4, 0:KVD]
    key = key * cosine[...] + turn_back(key, sine[...])
    kv[:, 0:KVD] = key.astype(BF16)
    kv[:, KVD : 2 * KVD] = (both[:, KVD:] + vectors[4:5, 0:KVD]).astype(BF16)


def project_kv(where, hidden, cosine, sine, *blocks):
    part, width = hidden.shape
    return pl.pallas_call(
        kv_kernel,
        out_shape=(
            jax.ShapeDtypeStruct((part, 2 * KVD), BF16),
            jax.ShapeDtypeStruct((part, width), BF16),
            jax.ShapeDtypeStruct((8, width), F32),
            jax.ShapeDtypeStruct((width, 2 * KVD), BF16),
        ),
        in_specs=[SMEM] + [VMEM] * 6,
        out_specs=(VMEM,) * 4,
        compiler_params=LIMIT,
        cost_estimate=cost(4 * part * width * KVD, 4 * part * width),
        name="kv",
    )(where, hidden, cosine, sine, *blocks)


def heads_forward(heads, query, kv, mask, attended, logs, first):
    lane = lax.broadcasted_iota(jnp.int32, logs.shape, 1)
    for h in heads:
        g = h // GROUPS
        keys = kv[:, pl.ds(g * HEAD_DIM, HEAD_DIM)]
        values = kv[:, pl.ds(KVD + g * HEAD_DIM, HEAD_DIM)]
        lanes = pl.ds(h * HEAD_DIM, HEAD_DIM)
        scores = mm_nt(query[:, lanes], keys) + mask[...]
        top = jnp.max(scores, axis=-1, keepdims=True)
        raised = jnp.exp(scores - top)
        total = jnp.sum(raised, axis=-1, keepdims=True)
        logs = jnp.where(lane == h, top + jnp.log(total), logs)
        probs = (raised * (1.0 / total)).astype(BF16)
        attended[:, pl.ds(h * HEAD_DIM - first, HEAD_DIM)] = mm(probs, values).astype(BF16)
    return logs


def attend_kernel(where, normed_one, vectors, cosine, sine, own_ids, key_ids, *refs, heads):
    blocks, wq = four(*refs[0:3]), four(*refs[3:6])
    query, attended, lse, w_q, kv, mask, sems = refs[6:]
    part, width = normed_one.shape
    copies = load_rows(where, wq, w_q, sems, 0)
    for k, block in enumerate(blocks):
        kv[pl.ds(k * part, part), :] = block[...]
    square = (part, part)
    diagonal = lax.broadcasted_iota(jnp.int32, square, 0) == lax.broadcasted_iota(jnp.int32, square, 1)
    own = jnp.where(diagonal, own_ids[...].astype(F32), 0.0)
    own = jnp.sum(own, axis=1, keepdims=True)
    mask[...] = jnp.where(key_ids[...].astype(F32) <= own, 0.0, HIDDEN_KEY)
    cos, sin = cosine[...], sine[...]
    for copy in copies:
        copy.wait()
    for first in range(0, width, LANES):
        lanes = pl.ds(first, LANES)
        value = mm(normed_one[...], w_q[:, lanes]) + vectors[1:2, lanes]
        value = value * cos + turn_back(value, sin)
        query[:, lanes] = (value.astype(BF16).astype(F32) * FACTOR).astype(BF16)
    logs = jnp.zeros((part, LANES), F32)
    lse[...] = heads_forward(heads, query, kv, mask, attended, logs, 0)


def attend(heads, where, normed_one, vectors, cosine, sine, own_ids, key_ids, kv, wq):
    part, width = normed_one.shape
    length = key_ids.shape[1]
    work = part * length * len(heads)
    return pl.pallas_call(
        functools.partial(attend_kernel, heads=heads),
        out_shape=(
            jax.ShapeDtypeStruct((part, width), BF16),
            jax.ShapeDtypeStruct((part, len(heads) * HEAD_DIM), BF16),
            jax.ShapeDtypeStruct((part, LANES), F32),
            jax.ShapeDtypeStruct((width, width), BF16),
            jax.ShapeDtypeStruct((length, 2 * KVD), BF16),
            jax.ShapeDtypeStruct((part, length), F32),
        ),
        in_specs=[SMEM] + [VMEM] * 9 + [ANY] * 3,
        out_specs=(VMEM,) * 6,
        scratch_shapes=[pltpu.SemaphoreType.DMA((4,))],
        compiler_params=LIMIT,
        cost_estimate=cost(4 * work * HEAD_DIM + 2 * part * width * width, 8 * part * width, work),
        name="attend",
    )(where, normed_one, vectors, cosine, sine, own_ids, key_ids, *kv, *wq)


def residual_kernel(where, hidden, vectors, mask, query, kv, before, lse_before, *refs, heads):
    wo = four(*refs[0:3])
    attended, lse, residual, normed, w_o, sems = refs[3:]
    first = before.shape[1]
    late = load_rows(where, wo, w_o, sems, 0)
    attended[:, 0:first] = before[...]
    lse[...] = heads_forward(heads, query, kv, mask, attended, lse_before[...], 0)
    for copy in late:
        copy.wait()
    value = hidden[...].astype(F32) + mm(attended[...], w_o[...])
    residual[...] = value
    normed[...] = (value * rms_scale(value) * vectors[2:3, :]).astype(BF16)


def attend_rest(heads, where, hidden, vectors, mask, query, kv, before, lse, wo):
    part, width = hidden.shape
    work = part * kv.shape[0] * len(heads)
    tokens = jax.ShapeDtypeStruct((part, width), BF16)
    return pl.pallas_call(
        functools.partial(residual_kernel, heads=heads),
        out_shape=(
            tokens,
            jax.ShapeDtypeStruct((part, LANES), F32),
            jax.ShapeDtypeStruct((part, width), F32),
            tokens,
            jax.ShapeDtypeStruct((width, width), BF16),
        ),
        in_specs=[SMEM] + [VMEM] * 7 + [ANY] * 3,
        out_specs=(VMEM,) * 5,
        scratch_shapes=[pltpu.SemaphoreType.DMA((4,))],
        compiler_params=LIMIT,
        cost_estimate=cost(4 * work * HEAD_DIM + 2 * part * width * width, 8 * part * width, work),
        name="attend_rest",
    )(where, hidden, vectors, mask, query, kv, before, lse, *wo)


def units_kernel(one, two, grad_hidden, weights, tokens, hidden, dgate, dup):
    part = one.shape[0]
    tokens[0:part, :] = one[...]
    tokens[part:, :] = two[...]
    value = tokens[...]
    gate = mm(value, weights[0])
    up = mm(value, weights[1])
    back = grad_hidden[...]
    sigma = jax.nn.sigmoid(gate)
    active = gate * sigma
    hidden[...] = (active * up).astype(BF16)
    dup[...] = (back * active).astype(BF16)
    dgate[...] = (back * up * sigma * (1.0 + gate * (1.0 - sigma))).astype(BF16)


def back_units_kernel(dy_one, dy_two, w_down, out, dy, *, slot):
    part = dy_one.shape[0]
    dy[0:part, :] = dy_one[...]
    dy[part:, :] = dy_two[slot]
    out[...] = mm_nt(dy[...], w_down[...])


def back_units(slot, dy_one, dy_two, w_down):
    part, width = dy_one.shape
    ff = w_down.shape[0]
    return pl.pallas_call(
        functools.partial(back_units_kernel, slot=slot),
        out_shape=(
            jax.ShapeDtypeStruct((2 * part, ff), F32),
            jax.ShapeDtypeStruct((2 * part, width), BF16),
        ),
        in_specs=[VMEM] * 3,
        out_specs=(VMEM, VMEM),
        compiler_params=LIMIT,
        cost_estimate=cost(4 * part * width * ff, 2 * width * ff + 8 * part * ff),
        name="back_units",
    )(dy_one, dy_two, w_down)


def units(one, two, grad_hidden, weights):
    part, width = one.shape
    ff = weights.shape[2]
    shape = jax.ShapeDtypeStruct((2 * part, ff), BF16)
    return pl.pallas_call(
        units_kernel,
        out_shape=(jax.ShapeDtypeStruct((2 * part, width), BF16), shape, shape, shape),
        in_specs=[VMEM] * 4,
        out_specs=(VMEM,) * 4,
        compiler_params=LIMIT,
        cost_estimate=cost(8 * part * width * ff, 6 * width * ff, 2 * part * ff),
        name="units",
    )(one, two, grad_hidden, weights)


def weight_kernel(*refs, count):
    left_a, left_b = refs[0:2]
    rights = refs[2 : 2 + 2 * count]
    outs = refs[2 + 2 * count :]
    for i, out in enumerate(outs):
        total = mm_tn(left_a[...], rights[2 * i][...]) + mm_tn(left_b[...], rights[2 * i + 1][...])
        out[...] = total.astype(BF16)


def weight_grads(left, rights):
    tall = left[0].shape[1]
    wide = rights[0][0].shape[1]
    count = len(rights)
    shape = jax.ShapeDtypeStruct((tall, wide), BF16)
    return pl.pallas_call(
        functools.partial(weight_kernel, count=count),
        out_shape=(shape,) * count,
        in_specs=[VMEM] * (2 + 2 * count),
        out_specs=(VMEM,) * count,
        compiler_params=LIMIT,
        cost_estimate=cost(4 * count * left[0].shape[0] * tall * wide, 6 * count * tall * wide),
        name="weight_grads",
    )(*left, *[r for pair in rights for r in pair])


def partial_kernel(*refs, mats, transposed):
    lefts = refs[: 2 * mats]
    weights, keep, send = refs[2 * mats :]
    part = keep.shape[1]
    for chip in range(2):
        if transposed:
            total = mm_nt(lefts[2 * chip][...], weights[0])
            total += mm_nt(lefts[2 * chip + 1][...], weights[1])
        else:
            total = mm(lefts[chip][...], weights[...])
        keep[chip] = total[:part].astype(BF16)
        send[chip] = total[part:].astype(BF16)


def partial_sums(lefts, weights, width, transposed):
    rows = lefts[0].shape[0]
    mats = len(lefts) // 2
    shape = jax.ShapeDtypeStruct((2, rows // 2, width), BF16)
    return pl.pallas_call(
        functools.partial(partial_kernel, mats=mats, transposed=transposed),
        out_shape=(shape, shape),
        in_specs=[VMEM] * (2 * mats + 1),
        out_specs=(VMEM, VMEM),
        compiler_params=LIMIT,
        cost_estimate=cost(4 * mats * rows * lefts[0].shape[1] * width, 8 * mats * rows * width),
        name="partial_sums",
    )(*lefts, weights)


def branch_kernel(own, near, far, residual, dy, vectors, w_o, dresidual, dbranch, dattended, gain):
    value = residual[...]
    scale = rms_scale(value)
    unit = value * scale
    grad = own[0].astype(F32) + near[0].astype(F32) + far[...].astype(F32)
    gain[...] = jnp.sum(grad * unit, axis=0, keepdims=True)
    inner = grad * vectors[2:3, :]
    total = scale * (inner - unit * jnp.mean(inner * unit, axis=-1, keepdims=True))
    total = dy[...].astype(F32) + total
    dresidual[...] = total
    low = total.astype(BF16)
    dbranch[...] = low
    dattended[...] = mm_nt(low, w_o[...]).astype(BF16)


def branch_back(own, near, far, residual, dy, vectors, w_o):
    part, width = residual.shape
    tokens = jax.ShapeDtypeStruct((part, width), BF16)
    return pl.pallas_call(
        branch_kernel,
        out_shape=(
            jax.ShapeDtypeStruct((part, width), F32),
            tokens,
            tokens,
            jax.ShapeDtypeStruct((1, width), F32),
        ),
        in_specs=[VMEM] * 7,
        out_specs=(VMEM,) * 4,
        compiler_params=LIMIT,
        cost_estimate=cost(2 * part * width * width, 20 * part * width),
        name="branch_back",
    )(own, near, far, residual, dy, vectors, w_o)


def back_kernel(mask, query, kv, lse, dattended, *refs, heads, first):
    dquery, dkv = refs[-2:]
    logs = lse[...]
    lane = lax.broadcasted_iota(jnp.int32, logs.shape, 1)
    if len(refs) > 2:
        dkv[...] = refs[0][...]
    else:
        dkv[...] = jnp.zeros_like(dkv)
    for h in heads:
        g = h // GROUPS
        k_lanes = pl.ds(g * HEAD_DIM, HEAD_DIM)
        v_lanes = pl.ds(KVD + g * HEAD_DIM, HEAD_DIM)
        lanes = pl.ds(h * HEAD_DIM, HEAD_DIM)
        q, do = query[:, lanes], dattended[:, lanes]
        keys, values = kv[:, k_lanes], kv[:, v_lanes]
        log = jnp.sum(jnp.where(lane == h, logs, 0.0), axis=-1, keepdims=True)
        probs = jnp.exp(mm_nt(q, keys) + mask[...] - log)
        dprobs = mm_nt(do, values)
        total = jnp.sum(probs * dprobs, axis=-1, keepdims=True)
        dscores = (probs * (dprobs - total)).astype(BF16)
        dquery[:, pl.ds(h * HEAD_DIM - first, HEAD_DIM)] = mm(dscores, keys) * FACTOR
        dkv[:, k_lanes] += mm_tn(dscores, q)
        dkv[:, v_lanes] += mm_tn(probs.astype(BF16), do)


def attend_back(heads, mask, query, kv, lse, dattended, *before):
    part = query.shape[0]
    length = kv.shape[0]
    first = heads[0] * HEAD_DIM
    work = part * length * len(heads)
    return pl.pallas_call(
        functools.partial(back_kernel, heads=heads, first=first),
        out_shape=(
            jax.ShapeDtypeStruct((part, len(heads) * HEAD_DIM), F32),
            jax.ShapeDtypeStruct((length, 2 * KVD), F32),
        ),
        in_specs=[VMEM] * (5 + len(before)),
        out_specs=(VMEM, VMEM),
        compiler_params=LIMIT,
        cost_estimate=cost(10 * work * HEAD_DIM, 8 * length * KVD, work),
        name="attend_back",
    )(mask, query, kv, lse, dattended, *before)


def deal(me, weights, per, keep, send):
    count = keep.shape[1]
    for k in range(4):
        out = (keep, send)[k % 2]
        for r in range(count):
            out[k // 2, r, 0:per, :] = weights[me ^ k, pl.ds(r * per, per), :].astype(BF16)


def out_grads_kernel(where, attended, dbranch, keep, send, weights):
    rows, width = weights.shape[1:]
    per = rows // keep.shape[1]
    weights[...] = mm_tn(attended[...], dbranch[...]).reshape(4, rows, width)
    if per < keep.shape[2]:
        keep[...] = jnp.zeros(keep.shape, BF16)
        send[...] = jnp.zeros(send.shape, BF16)
    deal(where[0], weights, per, keep, send)


def out_grads(replicas, where, attended, dbranch):
    part, width = attended.shape
    rows = width // 4
    tall = padded(rows, replicas)
    shape = jax.ShapeDtypeStruct((2, replicas, tall, width), BF16)
    return pl.pallas_call(
        out_grads_kernel,
        out_shape=(shape, shape),
        in_specs=[SMEM] + [VMEM] * 2,
        out_specs=(VMEM, VMEM),
        scratch_shapes=[pltpu.VMEM((4, rows, width), F32)],
        compiler_params=LIMIT,
        cost_estimate=cost(2 * part * width * width, 8 * width * width),
        name="out_grads",
    )(where, attended, dbranch)


def padded(rows, replicas):
    return -(-(rows // replicas + 1) // 8) * 8


def grads_kernel(where, hidden, normed, dresidual, dq_a, dq_b, own, near, far, cosine, sine, vectors, gain_two, w_q, w_kv, in_grad, keep, send, dpre, weights, values):
    me = where[0]
    part, width = hidden.shape
    rows = width // 4
    total_wide = width + 2 * KVD
    cos, sin = cosine[...], sine[...]
    split_at = dq_a.shape[1]
    grad = own[0].astype(F32) + near[0].astype(F32) + far[...].astype(F32)
    for first in range(0, width + KVD, LANES):
        if first < split_at:
            value = dq_a[:, pl.ds(first, LANES)]
        elif first < width:
            value = dq_b[:, pl.ds(first - split_at, LANES)]
        else:
            value = grad[:, :KVD]
        dpre[:, pl.ds(first, LANES)] = (value * cos - turn_back(value, sin)).astype(BF16)
    dpre[:, pl.ds(width + KVD, KVD)] = grad[:, KVD:].astype(BF16)
    bias = jnp.sum(dpre[...].astype(F32), axis=0, keepdims=True)

    x = hidden[...].astype(F32)
    scale = rms_scale(x)
    unit = x * scale
    back = mm_nt(dpre[:, 0:width], w_q[...]) + mm_nt(dpre[:, pl.ds(width, 2 * KVD)], w_kv[...])
    gain_one = jnp.sum(back * unit, axis=0, keepdims=True)
    inner = back * vectors[0:1, :]
    total = scale * (inner - unit * jnp.mean(inner * unit, axis=-1, keepdims=True))
    in_grad[...] = (dresidual[...] + total).astype(BF16)

    cut = width + KVD
    weights[...] = mm_tn(normed[...], dpre[...]).reshape(4, rows, total_wide)
    sizes = (rows, rows, rows, KVD // 4, KVD // 4)
    sources = (gain_one, bias[:, :width], gain_two[...], bias[:, width:cut], bias[:, cut:])
    values[...] = jnp.zeros_like(values)
    for j in range(4):
        for spot, size, source in zip(SPOTS, sizes, sources):
            values[j, 0:1, pl.ds(spot, size)] = source[:, j * size : (j + 1) * size]
    count = keep.shape[1]
    per = rows // count
    each = VECTOR // count
    keep[...] = jnp.zeros(keep.shape, BF16)
    send[...] = jnp.zeros(send.shape, BF16)
    deal(me, weights, per, keep, send)
    for k in range(4):
        out = (keep, send)[k % 2]
        for r in range(count):
            line = values[me ^ k, 0:1, pl.ds(r * each, each)]
            out[k // 2, r, per : per + 1, 0:each] = line.astype(BF16)


def attention_grads(replicas, where, hidden, *args):
    part, width = hidden.shape
    rows = width // 4
    wide = width + 2 * KVD
    shape = jax.ShapeDtypeStruct((2, replicas, padded(rows, replicas), wide), BF16)
    return pl.pallas_call(
        grads_kernel,
        out_shape=(jax.ShapeDtypeStruct((part, width), BF16), shape, shape),
        in_specs=[SMEM] + [VMEM] * 14,
        out_specs=(VMEM,) * 3,
        scratch_shapes=[
            pltpu.VMEM((part, wide), BF16),
            pltpu.VMEM((4, rows, wide), F32),
            pltpu.VMEM((4, 8, VECTOR), F32),
        ],
        compiler_params=LIMIT,
        cost_estimate=cost(8 * part * width * width, 20 * width * width),
        name="attention_grads",
    )(where, hidden, *args)


def split_grads_kernel(where, *refs, offsets, per):
    count = len(offsets)
    pieces = refs[:count]
    query, key, value, out, vectors, held = refs[count:]
    width = query.shape[1]
    each = VECTOR // count
    for offset, piece in zip(offsets, pieces):
        held[lax.rem(where[1] + offset + count, count)] = piece[...].astype(F32)
    for s in range(count):
        rows = pl.ds(s * per, per)
        query[rows, :] = held[s, 0:per, 0:width]
        key[rows, :] = held[s, 0:per, width : width + KVD]
        value[rows, :] = held[s, 0:per, width + KVD : width + 2 * KVD]
        out[rows, :] = held[s, 0:per, width + 2 * KVD :]
        vectors[0:1, pl.ds(s * each, each)] = held[s, per : per + 1, 0:each]


def split_grads(found, where, rows, width):
    offsets = [offset for offset, _ in found]
    count = len(found)
    tall, wide = found[0][1].shape
    shape = lambda columns: jax.ShapeDtypeStruct((rows, columns), F32)
    return pl.pallas_call(
        functools.partial(split_grads_kernel, offsets=offsets, per=rows // count),
        out_shape=(
            shape(width),
            shape(KVD),
            shape(KVD),
            shape(width),
            jax.ShapeDtypeStruct((1, VECTOR), F32),
        ),
        in_specs=[SMEM] + [VMEM] * count,
        out_specs=(VMEM,) * 5,
        scratch_shapes=[pltpu.VMEM((count, tall, wide), F32)],
        compiler_params=LIMIT,
        cost_estimate=cost(0, 6 * rows * wide),
        name="split_grads",
    )(where, *[value for _, value in found])


def stack_rows_kernel(where, *refs, offsets):
    count = len(offsets)
    out = refs[count]
    rows = refs[0].shape[0]
    for offset, piece in zip(offsets, refs[:count]):
        row = pl.multiple_of(lax.rem(where[1] + offset + count, count) * rows, 8)
        out[pl.ds(row, rows), :] = piece[...].astype(F32)


def stack_rows(found, where, place):
    offsets = [offset for offset, _ in found]
    count = len(found)
    rows, width = found[0][1].shape
    if rows % 8:
        return assemble(found, place, F32).reshape(count * rows, width)
    return pl.pallas_call(
        functools.partial(stack_rows_kernel, offsets=offsets),
        out_shape=jax.ShapeDtypeStruct((count * rows, width), F32),
        in_specs=[SMEM] + [VMEM] * count,
        out_specs=VMEM,
        compiler_params=LIMIT,
        cost_estimate=cost(0, 6 * count * rows * width),
        name="stack_rows",
    )(where, *[value for _, value in found])


class Order:
    def __init__(self):
        self.last = None

    def __call__(self, run, *values):
        values = self.hold(*values)
        found = run(*values)
        self.last = tuple(found) if isinstance(found, (tuple, list)) else (found,)
        return found

    def wait(self, *values):
        self.last = (*(self.last or ()), *values)

    def hold(self, *values):
        if self.last is None:
            return values
        return lax.optimization_barrier((*values, *self.last))[: len(values)]


class Ring:
    def __init__(self, count, lead):
        self.count = count
        self.lead = lead
        self.order = [0, 2, 4, 6, 7, 5, 3, 1] if count == 8 else list(range(count))
        self.plus = count // 2
        self.minus = count - 1 - self.plus

    def place(self):
        replica = lax.axis_index("replica")
        if self.count == 8:
            line, side = replica // 2, replica % 2
            return jnp.where(side == 0, line, 7 - line)
        return replica

    def replica(self, place):
        if self.count == 8:
            return jnp.where(place < 4, 2 * place, 15 - 2 * place)
        return place

    def move(self, value, step):
        n = self.count
        pairs = [(self.order[p], self.order[(p + step) % n]) for p in range(n)]
        return lax.ppermute(value, "replica", pairs)

    def both(self):
        return ((self.plus, self.lead), (self.minus, -self.lead))


class RingSum:
    def __init__(self, ring, order, take, *arrays):
        self.ring, self.order, self.take, self.arrays = ring, order, take, arrays
        self.left = [hops for hops, _ in ring.both()]
        self.arrived = []
        self.moving = self._send(None)

    def _send(self, moving):
        ring = self.ring
        active = [i for i in range(2) if self.left[i] > 0]

        def run(*values):
            parts = []
            for n, i in enumerate(active):
                step = ring.both()[i][1]
                part = self.take(step * self.left[i], *values[: len(self.arrays)])
                if moving is not None:
                    got = values[len(self.arrays) + n]
                    part = (part.astype(F32) + got.astype(F32)).astype(BF16)
                parts.append(part)
            return parts

        got = [] if moving is None else [moving[i] for i in active]
        parts = self.order(run, *self.arrays, *got)
        sent = [None, None]
        for part, i in zip(parts, active):
            sent[i] = ring.move(part, ring.both()[i][1])
            self.left[i] -= 1
            if self.left[i] == 0:
                self.arrived.append(sent[i])
        return sent

    def step(self):
        self.moving = self._send(self.moving)

    def total(self):
        while max(self.left) > 0:
            self.step()
        count = len(self.arrays)

        def run(*values):
            own = self.take(0, *values[:count]).astype(F32)
            return sum((v.astype(F32) for v in values[count:]), own).astype(BF16)

        return self.order(run, *self.arrays, *self.arrived)


class RingGather:
    def __init__(self, ring, order, own):
        self.ring, self.order = ring, order
        self.found = [(0, own)]
        self.hop = 0
        self.moving = [own, own]
        self._send()

    def _send(self):
        self.hop += 1
        for i, (hops, step) in enumerate(self.ring.both()):
            if self.hop <= hops:
                self.moving[i] = self.ring.move(self.moving[i], step)
                self.found.append((-step * self.hop, self.moving[i]))

    def step(self):
        if self.hop < self.ring.plus:
            self.moving = list(self.order(lambda *v: v, *self.moving))
            self._send()

    def take(self, first, last):
        found = self.found[first:last]
        values = self.order(lambda *v: v, *[value for _, value in found])
        self.found[first:last] = [(offset, value) for (offset, _), value in zip(found, values)]

    def finish(self):
        while self.hop < self.ring.plus:
            self.step()
        return self.found


class Share:
    def __init__(self, ring, order, own):
        self.ring, self.order = ring, order
        self.found = [(0, (0, 1), own)]
        self.hop = 0
        self.moving = [own, own]
        self._send()

    def _send(self):
        self.hop += 1
        for i, step in enumerate((1, -1)):
            halves = (0, 1)
            if self.hop == self.ring.count // 4:
                halves = (i,)
                self.moving[i] = self.moving[i][:, i : i + 1]
            self.moving[i] = self.ring.move(self.moving[i], step)
            self.found.append((-step * self.hop, halves, self.moving[i]))

    def step(self):
        self.moving = list(self.order(lambda *v: v, *self.moving))
        self._send()


def assemble(found, place, dtype):
    block = found[0][1]
    out = jnp.zeros((len(found),) + block.shape, dtype)
    for offset, value in found:
        start = ((place + offset) % len(found),) + (0,) * block.ndim
        out = lax.dynamic_update_slice(out, value.astype(dtype)[None], start)
    return out


def swap(value, mask):
    return lax.ppermute(value, "group", [(j, j ^ mask) for j in range(4)])


def spread(own):
    one = swap(own, 1)
    two = swap(own, 2)
    return [own, one, two, swap(two, 1)]


class Spread:
    def __init__(self, own):
        self.own, self.two = own, swap(own, 2)

    def step(self, order):
        self.other = swap(order(lambda *v: jnp.stack(v), self.own, self.two), 1)

    def parts(self):
        return self.own, self.other, self.two


class Collect:
    def __init__(self, order, keep, send):
        self.order, self.keep, self.got = order, keep, swap(send, 1)

    def step(self):
        def run(keep, got):
            return (keep[1].astype(F32) + got[1].astype(F32)).astype(BF16)

        self.other = swap(self.order(run, self.keep, self.got), 2)

    def terms(self):
        return self.keep, self.got, self.other


def after(value, *others):
    return lax.optimization_barrier((value,) + others)[0]


FIRST_HEADS = range(0, 8)
OTHER_HEADS = range(8, HEADS)


def make_body(replicas):
    ring_up = Ring(replicas, 1)
    ring_down = Ring(replicas, -1)

    def body(
        hidden_in,
        out_grad,
        positions,
        block_ids,
        gain_one,
        w_query,
        b_query,
        w_key,
        b_key,
        w_value,
        b_value,
        w_out,
        gain_two,
        w_gate,
        w_up,
        w_down,
    ):
        _, part, width = hidden_in.shape
        length = block_ids.shape[1]
        rows = w_gate.shape[0]
        ff = w_down.shape[0]
        half = replicas // 2
        chunk = 2 * rows // replicas
        me = lax.axis_index("group")
        place = ring_up.place()
        where = jnp.stack([me, place])
        order = Order()
        x_value, dy_own = hidden_in[0], out_grad[0]

        packed = order(pack, w_key, w_value, gain_one, b_query, gain_two, b_key, b_value)
        first = Spread(packed)
        wq = Spread(after(w_query, packed))
        offsets = range(-half, half + 1)
        early = [lax.rem(place + (o + replicas), replicas) for o in offsets]
        early += [lax.rem(p, half) for p in early]
        early += [p < half for p in early[: len(offsets)]]
        early += [me ^ k for k in range(4)]
        freqs = THETA ** (-(2.0 * np.arange(HEAD_DIM // 2)) / HEAD_DIM)
        freqs = np.tile(freqs, LANES * 2 // HEAD_DIM).astype(np.float32)
        angles = positions[0].astype(F32)[:, None] * freqs
        sign = np.where(np.arange(LANES) % HEAD_DIM < HEAD_DIM // 2, -1.0, 1.0).astype(np.float32)
        ids = block_ids.reshape(4, part)
        own_ids = pick(ids, me).reshape(1, part)
        key_ids = jnp.concatenate([pick(ids, me ^ k) for k in range(4)]).reshape(1, length)
        early += [jnp.cos(angles), jnp.sin(angles) * sign, own_ids, key_ids, where]
        early = lax.optimization_barrier(tuple(early))
        order.wait(*early)
        *early, cosine, sine, own_ids, key_ids, where = early
        count = len(offsets)
        places = dict(zip(offsets, early[:count]))
        rows_at = dict(zip(offsets, early[count : 2 * count]))
        first_half = dict(zip(offsets, early[2 * count : 3 * count]))
        member = early[3 * count :]
        own, near, far_a, far_b = order(
            lambda gate, up: split(where, gate, up, replicas), w_gate, w_up
        )
        first.step(order)
        far_a, far_b = swap(after(far_a, first.two), 2), swap(after(far_b, first.two), 3)
        kv, normed_one, vectors, w_kv = order(
            lambda *v: project_kv(where, *v), x_value, cosine, sine, *first.parts()
        )
        kv = Spread(kv)
        wq.step(order)
        far = order(lambda *v: jnp.stack(v), far_a, far_b)
        pieces = Share(ring_up, order, far)
        kv.step(order)
        wo = Spread(after(w_out, kv.two))
        query, attended, lse, w_q, kv, mask = order(
            lambda *v: attend(FIRST_HEADS, where, *v[:6], v[6:9], v[9:]),
            normed_one,
            vectors,
            cosine,
            sine,
            own_ids,
            key_ids,
            *kv.parts(),
            *wq.parts(),
        )
        pieces.step()
        wo.step(order)
        dy = Spread(after(dy_own, wo.two))
        near = swap(after(near, query), 1)
        attended, lse, residual, normed_two, w_o = order(
            lambda *v: attend_rest(OTHER_HEADS, where, *v[:7], v[7:]),
            x_value,
            vectors,
            mask,
            query,
            kv,
            attended,
            lse,
            *wo.parts(),
        )
        while pieces.hop < replicas // 4:
            pieces.step()
        order.wait(*[value for _, _, value in pieces.found])
        (normed_late,) = order.hold(normed_two)
        one, two = swap(normed_late, 1), swap(normed_late, 2)
        dy.step(order)
        shape = (2, 4, half, chunk, ff)
        moves = []
        for mat in range(2):
            for source in (0, 1):
                moves.append((source, lambda s, m=mat: m, lambda s, m=mat, k=source: (m, s[0] ^ k)))
        for i, (offset, mats, _) in enumerate(pieces.found):
            for slot in range(2):
                for n, mat in enumerate(mats):
                    put = lambda s, d=offset + half, m=mat, k=2 + slot: (m, s[0] ^ k, lax.rem(s[1] + d, half))
                    moves.append((2 + i, lambda s, j=slot, n=n: (j, n), put))
        w_both = order(
            lambda *v: arrange(where, v, shape, moves),
            *[v.reshape(shape[:1] + shape[2:]) for v in (own, near)],
            *[value for _, _, value in pieces.found],
        )
        w_both = w_both.reshape(2, width, ff)

        grad_hidden, dy_a = order(functools.partial(back_units, 0), dy.own, dy.other, w_down)
        tok_a, hid_a, dgate_a, dup_a = order(units, normed_two, one, grad_hidden, w_both)
        three = swap(order.hold(two)[0], 1)
        grad_hidden, dy_b = order(functools.partial(back_units, 1), dy.two, dy.other, w_down)
        tok_b, hid_b, dgate_b, dup_b = order(units, two, three, grad_hidden, w_both)
        grad_gate, grad_up = order(
            lambda *v: weight_grads(v[:2], [v[2:4], v[4:6]]),
            tok_a,
            tok_b,
            dgate_a,
            dgate_b,
            dup_a,
            dup_b,
        )

        def take_units(offset, gate, up):
            row = rows_at[offset]
            return jnp.where(first_half[offset], pick(gate, row, 1), pick(up, row, 1))

        def take_rows(offset, value):
            return pick(value, places[offset])

        shape = (4, half, chunk, ff)
        sum_units = RingSum(
            ring_up, order, take_units, grad_gate.reshape(shape), grad_up.reshape(shape)
        )
        sums = order(
            lambda *v: partial_sums(v[:4], v[4], width, True), dgate_a, dup_a, dgate_b, dup_b, w_both
        )
        to_normed = Collect(order, *sums)
        sum_units.step()
        to_normed.step()
        (grad_down,) = order(lambda *v: weight_grads(v[:2], [v[2:]]), hid_a, hid_b, dy_a, dy_b)
        grad_down = grad_down.reshape(replicas, ff // replicas, width)
        sum_down = RingSum(ring_down, order, take_rows, grad_down)

        dresidual, dbranch, dattended, grad_gain_two = order(
            branch_back, *to_normed.terms(), residual, dy_own, vectors, w_o
        )
        to_w_out = Collect(
            order, *order(lambda *v: out_grads(replicas, where, *v), attended, dbranch)
        )
        sum_down.step()
        args = (mask, query, kv, lse, dattended)
        dq_a, dkv = order(functools.partial(attend_back, FIRST_HEADS), *args)
        sum_units.step()
        to_w_out.step()
        sum_down.step()
        dq_b, dkv = order(functools.partial(attend_back, OTHER_HEADS), *args, dkv)
        dkv = dkv.astype(BF16).reshape(2, 2, part, 2 * KVD)
        to_kv = Collect(order, dkv[:, 0], dkv[:, 1])
        sum_units.step()
        to_kv.step()
        sum_down.step()
        order.wait(to_w_out.other)
        in_grad, *packed = order(
            lambda *v: attention_grads(replicas, where, *v),
            x_value,
            normed_one,
            dresidual,
            dq_a,
            dq_b,
            *to_kv.terms(),
            cosine,
            sine,
            vectors,
            grad_gain_two,
            w_q,
            w_kv,
        )
        to_weights = Collect(order, *packed)
        mine = sum_units.total()
        blocks = [pick(mine, member[0])]
        blocks += [swap(pick(mine, member[k]), k) for k in (1, 2, 3)]
        to_weights.step()
        down = sum_down.total()
        all_units = RingGather(ring_up, order, order(lambda *v: jnp.stack(v), *blocks))
        all_down = RingGather(ring_down, order, down)
        sums_out = order(lambda *v: partial_sums(v[:2], v[2], width, False), hid_a, hid_b, w_down)
        all_down.step()
        def total(*terms):
            one, two = [
                keep[0].astype(F32) + got[0].astype(F32) + other.astype(F32)
                for keep, got, other in (terms[:3], terms[3:])
            ]
            return jnp.concatenate([one, two], axis=2).astype(BF16)

        packed = order(total, *to_weights.terms(), *to_w_out.terms())
        sum_packed = RingSum(ring_down, order, take_rows, packed)
        all_units.step()
        sum_packed.step()
        sum_packed.step()
        all_down.step()
        sum_packed.step()
        all_units.step()
        all_down.step()
        all_packed = RingGather(ring_down, order, sum_packed.total())
        first = all_units.found[:5]
        early = [o for o, _ in first]
        joins = order(lambda *v: join(early, where, rows, replicas, v), *[b for _, b in first])
        all_packed.step()
        all_units.step()
        to_out = Collect(order, *order.hold(*sums_out))
        all_packed.step()
        down = all_down.finish()
        out_down = order(
            lambda *v: stack_rows([(o, b) for (o, _), b in zip(down, v)], where, place),
            *[b for _, b in down],
        )
        to_out.step()
        all_packed.step()
        rest = all_units.finish()[5:]
        late = [o for o, _ in rest]
        joins = order(
            lambda a, b, *v: join(late, where, rows, replicas, v, a, b), *joins, *[b for _, b in rest]
        )
        layer_out = order(
            lambda x, keep, got, other: (
                x + keep[0].astype(F32) + got[0].astype(F32) + other.astype(F32)
            ).astype(BF16),
            residual,
            *to_out.terms(),
        )
        out_gate, out_up = joined(*joins, rows)
        found = all_packed.finish()
        g_w_query, g_w_key, g_w_value, g_w_out, values = order(
            lambda *v: split_grads([(o, b) for (o, _), b in zip(found, v)], where, rows, width),
            *[b for _, b in found],
        )
        values = values.reshape(VECTOR)
        sizes = (rows, rows, rows, KVD // 4, KVD // 4)
        g_one, g_bq, g_two, g_bk, g_bv = [values[s : s + n] for s, n in zip(SPOTS, sizes)]
        return (
            layer_out[None],
            in_grad[None],
            g_one,
            g_w_query,
            g_bq,
            g_w_key,
            g_bk,
            g_w_value,
            g_bv,
            g_w_out,
            g_two,
            out_gate,
            out_up,
            out_down,
        )

    return body


def solution(mesh):
    tokens = P("replica", "group", None)
    matrix = P("group", None)
    vector = P("group")
    weights = (
        vector,
        matrix,
        vector,
        matrix,
        vector,
        matrix,
        vector,
        matrix,
        vector,
        matrix,
        matrix,
        matrix,
    )
    in_specs = (tokens, tokens, P("replica", "group"), P("replica", None)) + weights
    out_specs = (tokens, tokens) + weights
    body = make_body(mesh.shape["replica"])
    return jax.shard_map(body, mesh=mesh, in_specs=in_specs, out_specs=out_specs, check_vma=False)
```
